512 devices in a mesh: ctx: 32 (over x, z), ch: 16 (over y, core).
Axes of the slice: x: 4, y: 8, z: 8, core: 2. Of those that a mesh axis runs over, the one named last changes fastest.
Arguments:
- tokens: bfloat16 [4096, 4096], P('ctx'), may hold values from -6 to 6
- projections: bfloat16 [3, 4096, 4096], P(None, 'ctx', 'ch'), may hold values from -0.09375 to 0.09375
- decay_rates: float32 [4096, 16], P('ch'), may hold values from 0.00012207031 to 0.03
- residues: float32 [4096, 16], P('ch'), may hold values from -1.5 to 1.5
- short_filter: bfloat16 [4096, 128], P('ch'), may hold values from -0.5 to 0.5
Outputs:
- mixed: bfloat16 [4096, 4096], P('ctx', 'ch')
The draws below stay inside these ranges and needn't reach their ends.
All inputs are finite; a program needn't handle non-finite values.
Results may differ from the reference program's by a relative error of at most 0.0068.
Values may be sent and summed in bfloat16 or wider, within the bound.
No kernel may reach another device: no remote copies, remote signals or barrier semaphores. Data moves between devices by JAX's collectives and lax.ppermute only.
A program may use at most 64 MiB of HBM per device.

```python
import math
import jax
import jax.numpy as jnp
from jax import lax

D = 4096
MODES = 16
MR = 128
TOKENS = 4096


def level_of(stream_key, dims, split, least, top_value):
    factor_of = 1.0
    for axis_at, shards_of in split:
        steps = jax.random.uniform(jax.random.fold_in(jax.random.fold_in(stream_key, 6), axis_at), (shards_of,), jnp.float32, least / len(split), top_value / len(split))
        factor_of = factor_of * jnp.repeat(jnp.exp(steps), dims[axis_at] // shards_of).reshape((-1,) + (1,) * (len(dims) - 1 - axis_at))
    return factor_of


def centred(key, extent, deviation, most, cuts=(), held_as=jnp.bfloat16):
    result = jax.random.normal(key, extent, jnp.float32) * deviation
    if len(cuts) > 0:
        result = level_of(key, extent, cuts, -0.22, 0.18) * result
    return jnp.clip(result, min=-most, max=most).astype(held_as)


def setup_inputs(seed: int = 0) -> dict:
    key_list = jax.random.split(jax.random.key(seed), 6)
    tokens = centred(key_list[0], (TOKENS, D), 1.0, 6.0, ((0, 32),))
    projections = centred(key_list[1], (3, D, D), D ** -0.5, 0.09375, ((1, 32), (2, 16)))
    decay_rates = jnp.clip(jnp.exp(math.log(0.03) - 5.5043554 * jax.random.uniform(key_list[2], (D, MODES), jnp.float32) ** level_of(key_list[2], (D, MODES), ((0, 16),), -0.2, 0.2)), 0.00012207031, 0.03)
    residues = centred(key_list[3], (D, MODES), 0.25, 1.5, ((0, 16),), jnp.float32)
    short_filter = centred(key_list[4], (D, MR), MR ** -0.5, 0.5, ((0, 16),))
    return dict(tokens=tokens, projections=projections, decay_rates=decay_rates, residues=residues, short_filter=short_filter)


def impulse_rows(rate_rows, residue_rows):
    positions = jnp.arange(TOKENS, dtype=jnp.float32)[None, :]

    def add_mode(mode_index, running):
        mode_rate = lax.dynamic_slice_in_dim(rate_rows, mode_index, 1, 1)
        weight = lax.dynamic_slice_in_dim(residue_rows, mode_index, 1, 1)
        return running + weight * jnp.sqrt(2.0 * mode_rate) * jnp.exp(-mode_rate * positions)
    start_value = jnp.zeros((rate_rows.shape[0], TOKENS), jnp.float32)
    return lax.fori_loop(0, MODES, add_mode, start_value)

def long_convolution(operands):
    signal, rate_rows, residue_rows = operands
    impulse = impulse_rows(rate_rows, residue_rows)
    spectrum = jnp.fft.rfft(signal, n=2 * TOKENS, axis=1) * jnp.fft.rfft(impulse, n=2 * TOKENS, axis=1)
    return jnp.fft.irfft(spectrum, n=2 * TOKENS, axis=1)[:, :TOKENS]

def reference(tokens, projections, decay_rates, residues, short_filter):
    gate_in = jnp.dot(tokens, projections[0], preferred_element_type=jnp.float32).astype(jnp.bfloat16)
    values = jnp.dot(tokens, projections[1], preferred_element_type=jnp.float32).astype(jnp.bfloat16)
    gate_out = jnp.dot(tokens, projections[2], preferred_element_type=jnp.float32).astype(jnp.bfloat16)
    signal = (gate_in.astype(jnp.float32) * values.astype(jnp.float32)).T
    block_width = min(D, 256)
    groups = D // block_width
    convolved = lax.map(long_convolution, (signal.reshape(groups, block_width, TOKENS), decay_rates.reshape(groups, block_width, MODES), residues.reshape(groups, block_width, MODES)))
    convolved = convolved.reshape(D, TOKENS).T
    gated_rows = (gate_out.astype(jnp.float32) * convolved).astype(jnp.bfloat16)
    padded = jnp.pad(gated_rows.astype(jnp.float32), ((MR - 1, 0), (0, 0)))
    tap_table = short_filter.astype(jnp.float32)

    def add_tap(tap_index, running):
        offset = MR - 1 - tap_index
        shifted = lax.dynamic_slice_in_dim(padded, offset, TOKENS, 0)
        weight = lax.dynamic_slice_in_dim(tap_table, tap_index, 1, 1)[:, 0]
        return running + shifted * weight[None, :]
    filtered = lax.fori_loop(0, MR, add_tap, jnp.zeros((TOKENS, D), jnp.float32))
    return filtered.astype(jnp.bfloat16)
```

```python
import math

import jax
import jax.numpy as jnp
import numpy as np
from jax import lax
from jax.experimental import pallas as pl
from jax.experimental.pallas import tpu as pltpu
from jax.sharding import PartitionSpec as P

f32, bf16 = jnp.float32, jnp.bfloat16
highest = lax.Precision.HIGHEST

NX, NZ, NC = 4, 8, 2
ROWS = 128
LANES = 128
HALF = 64
SPAN = 2 * ROWS
MODES = 16
SHIFTS = (1, 3, 2)

x_groups = [[x * NZ + z for x in range(NX)] for z in range(NZ)]
z_groups = [[x * NZ + z for z in range(NZ)] for x in range(NX)]


def real_transform():
    bins, places = np.arange(ROWS)[:, None], np.arange(SPAN)[None, :]
    angles = 2 * math.pi * (bins * places % SPAN) / SPAN
    real, imag = np.cos(angles), -np.sin(angles)
    imag[0] = np.where(np.arange(SPAN) % 2 == 0, 1.0, -1.0)
    return np.concatenate([real, imag]).astype(np.float32)


def inverse_transform():
    places, bins = np.arange(SPAN)[:, None], np.arange(ROWS)[None, :]
    angles = 2 * math.pi * (bins * places % SPAN) / SPAN
    real, imag = 2 * np.cos(angles), -2 * np.sin(angles)
    real[:, 0] = 1.0
    imag[:, 0] = np.where(np.arange(SPAN) % 2 == 0, 1.0, -1.0)
    return (np.concatenate([real, imag], axis=1) / SPAN).astype(np.float32)


def dot32(a, b):
    return jnp.dot(a, b, precision=highest, preferred_element_type=f32)


def multiply_spectra(u, h):
    first = lax.broadcasted_iota(jnp.int32, (ROWS, u.shape[1]), 0) == 0
    ur, ui, hr, hi = u[:ROWS], u[ROWS:], h[:ROWS], h[ROWS:]
    both = ui * hi
    real = ur * hr - jnp.where(first, 0.0, both)
    imag = jnp.where(first, both, ur * hi + ui * hr)
    return jnp.concatenate([real, imag], axis=0)


def lower_lanes(shape):
    return lax.broadcasted_iota(jnp.int32, shape, len(shape) - 1) < HALF


def swap_halves(v):
    return pltpu.roll(v, HALF, v.ndim - 1)


def call(body, outs, name, *args, scratch=(), flops=10**9):
    return pl.pallas_call(
        body,
        out_shape=outs,
        in_specs=[pl.BlockSpec(memory_space=pltpu.VMEM)] * len(args),
        out_specs=jax.tree.map(lambda _: pl.BlockSpec(memory_space=pltpu.VMEM), outs),
        scratch_shapes=scratch,
        compiler_params=pltpu.CompilerParams(vmem_limit_bytes=8 << 20),
        cost_estimate=pl.CostEstimate(flops=flops, bytes_accessed=flops // 200, transcendentals=0),
        name=name,
    )(*args)


def spread_weights(w_ref, out_ref):
    low = lower_lanes((ROWS, LANES))
    low_half = lower_lanes((HALF, LANES))
    for x in range(NX):
        at = pl.ds(LANES * (x // 2), LANES)
        a, v, o = (w_ref[k, :, at].astype(f32) for k in range(3))
        if x % 2 == 0:
            both = jnp.where(low, a, swap_halves(v))
            packed = jnp.where(low_half, o[:HALF], swap_halves(o[HALF:]))
        else:
            both = jnp.where(low, swap_halves(a), v)
            packed = jnp.where(low_half, swap_halves(o[:HALF]), o[HALF:])
        both, packed = both.astype(bf16), packed.astype(bf16)
        for z in range(NZ):
            out_ref[x * NZ + z, :ROWS] = both
            out_ref[x * NZ + z, ROWS:] = packed


def build_tables(a_ref, w_ref, taps_ref, fwd_ref, into_ref, out_ref, long_ref, short_ref):
    t = lax.broadcasted_iota(jnp.int32, (ROWS, LANES), 0).astype(f32)
    impulse = jnp.zeros((ROWS, LANES), f32)
    for m in range(MODES):
        rate, weight = a_ref[m : m + 1, :], w_ref[m : m + 1, :]
        into_ref[m] = jnp.exp(-rate * (ROWS - 1.0 - t))
        out_ref[m] = weight * jnp.exp(-rate * (t + 1.0))
        impulse = impulse + weight * jnp.exp(-rate * t)
    transform = fwd_ref[:, :ROWS]
    long_ref[...] = dot32(transform, impulse)
    short_ref[...] = dot32(transform, taps_ref[...])


def positions():
    ctx, ch = lax.axis_index("ctx"), lax.axis_index("ch")
    return lax.div(ctx, NZ), lax.rem(ctx, NZ), lax.rem(ch, NC)


def fill_products(tokens_ref, near_refs, far_refs, weight_ref, product_ref):
    x, _, core = positions()
    width = near_refs[0].shape[1]
    near = pl.ds(pl.multiple_of(core * width, width), width)
    far = pl.ds(pl.multiple_of((1 - core) * width, width), width)
    product_ref[x] = jnp.dot(tokens_ref[...], weight_ref[...], preferred_element_type=f32)
    for shift, near_ref, far_ref in zip(SHIFTS, near_refs, far_refs):
        product_ref[lax.rem(x + (NX - shift), NX)] = jnp.dot(
            near_ref[...], weight_ref[near, :], preferred_element_type=f32
        ) + jnp.dot(far_ref[...], weight_ref[far, :], preferred_element_type=f32)


def make_signal(tokens_ref, n0, n1, n2, f0, f1, f2, blocks_ref, into_ref, signal_ref, state_ref, weight_ref, product_ref):
    for block in range(NX * NZ):
        weight_ref[ROWS * block : ROWS * (block + 1), :] = blocks_ref[block, :ROWS]
    fill_products(tokens_ref, (n0, n1, n2), (f0, f1, f2), weight_ref, product_ref)
    low = lower_lanes((ROWS, LANES))
    for pair in range(NX // 2):
        parts = []
        for chunk in (2 * pair, 2 * pair + 1):
            both = product_ref[chunk].astype(bf16).astype(f32)
            parts.append(both * swap_halves(both))
        signal = jnp.where(low, parts[0], parts[1])
        signal_ref[:, LANES * pair : LANES * (pair + 1)] = signal
        for m in range(MODES):
            state = jnp.sum(signal * into_ref[m], axis=0, keepdims=True)
            for z in range(NZ):
                state_ref[z, pair * MODES + m : pair * MODES + m + 1, :] = state


def make_gates(tokens_ref, n0, n1, n2, f0, f1, f2, blocks_ref, signal_ref, fwd_ref, inv_ref, long_ref, both_ref, weight_ref, product_ref):
    low_half = lower_lanes((HALF, LANES))
    for block in range(NX * NZ):
        packed = blocks_ref[block, ROWS:].astype(f32)
        turned = swap_halves(packed)
        weight_ref[ROWS * block : ROWS * block + HALF, :] = jnp.where(low_half, packed, turned).astype(bf16)
        weight_ref[ROWS * block + HALF : ROWS * (block + 1), :] = jnp.where(low_half, turned, packed).astype(bf16)
    fill_products(tokens_ref, (n0, n1, n2), (f0, f1, f2), weight_ref, product_ref)
    spectrum = dot32(fwd_ref[:, :ROWS], signal_ref[...])
    response = jnp.concatenate([long_ref[...]] * 2, axis=1)
    both_ref[:, : 2 * LANES] = dot32(inv_ref[:ROWS, :], multiply_spectra(spectrum, response))
    low = lower_lanes((ROWS, LANES))
    for pair in range(NX // 2):
        gate = jnp.where(low, product_ref[2 * pair], product_ref[2 * pair + 1])
        both_ref[:, LANES * (2 + pair) : LANES * (3 + pair)] = gate.astype(bf16).astype(f32)


def carry_in(states_ref, a_ref, z):
    low = lower_lanes((MODES, LANES))
    rate = a_ref[...] * float(ROWS)
    decay = jnp.exp(-rate)
    decay_row = jnp.exp(-rate * float(NZ))
    decay_here = jnp.exp(-rate * z.astype(f32))
    before, whole = [], []
    for pair in range(NX // 2):
        upto = jnp.zeros((MODES, LANES), f32)
        total = jnp.zeros((MODES, LANES), f32)
        for k in range(NZ):
            step = states_ref[k, pair * MODES : (pair + 1) * MODES, :]
            upto = jnp.where(k < z, upto * decay + step, upto)
            total = total * decay + step
        before.append(upto)
        whole.append(total)
    swapped = [swap_halves(v) for v in whole]
    first = jnp.where(low, 0.0, swapped[0])
    second = jnp.where(
        low,
        swapped[0] + decay_row * whole[0],
        swapped[1] + decay_row * (whole[0] + decay_row * swapped[0]),
    )
    return [before[0] + decay_here * first, before[1] + decay_here * second]


def gate_rows(both_ref, carries, out_ref):
    parts = []
    for pair in range(NX // 2):
        value = both_ref[:, LANES * pair : LANES * (pair + 1)]
        for m in range(MODES):
            value = value + out_ref[m] * carries[pair][m : m + 1, :]
        gate = both_ref[:, LANES * (2 + pair) : LANES * (3 + pair)]
        parts.append((gate * value).astype(bf16).astype(f32))
    return parts


def finish(both_ref, arrived_ref, states_ref, a_ref, out_ref, fwd_ref, inv_ref, short_ref, packed_ref):
    _, z, _ = positions()
    low = lower_lanes((ROWS, LANES))
    own = gate_rows(both_ref, carry_in(states_ref, a_ref, z), out_ref)
    arrived = gate_rows(arrived_ref, carry_in(states_ref, a_ref, lax.rem(z + NZ - 1, NZ)), out_ref)
    turned = [swap_halves(v) for v in arrived]
    shifted = [jnp.where(low, 0.0, turned[0]), jnp.where(low, turned[0], turned[1])]
    previous = jnp.concatenate([jnp.where(z == 0, s, a) for s, a in zip(shifted, arrived)], axis=1)
    window = jnp.concatenate([previous, jnp.concatenate(own, axis=1)], axis=0)
    response = jnp.concatenate([short_ref[...]] * 2, axis=1)
    mixed = dot32(inv_ref[ROWS:, :], multiply_spectra(dot32(fwd_ref[...], window), response))
    low_half = lower_lanes((HALF, LANES))
    for pair in range(2):
        top = mixed[:HALF, LANES * pair : LANES * (pair + 1)]
        bottom = mixed[HALF:, LANES * pair : LANES * (pair + 1)]
        packed_ref[2 * pair] = jnp.where(low_half, top, swap_halves(bottom)).astype(bf16)
        packed_ref[2 * pair + 1] = jnp.where(low_half, swap_halves(top), bottom).astype(bf16)


def unpack_rows(packed_ref, out_ref):
    low = lower_lanes((HALF, LANES))
    for pair in range(2):
        a, b = (packed_ref[2 * pair + h].astype(f32) for h in range(2))
        lanes = slice(LANES * pair, LANES * (pair + 1))
        out_ref[:HALF, lanes] = jnp.where(low, a, swap_halves(b)).astype(bf16)
        out_ref[HALF:, lanes] = jnp.where(low, swap_halves(a), b).astype(bf16)


def per_device(tokens, projections, decay_rates, residues, short_filter):
    sds = jax.ShapeDtypeStruct
    x = lax.axis_index("ctx") // NZ
    core = lax.axis_index("ch") % NC
    width = tokens.shape[1] // NC
    count = NX * NZ
    depth = count * ROWS
    blocks = call(spread_weights, sds((count, ROWS + HALF, LANES), bf16), "spread_weights", projections)
    blocks = lax.all_to_all(blocks, "ctx", 0, 0, tiled=True)
    half = lax.dynamic_slice_in_dim(tokens, core * width, width, 1)
    swap = [(k, k ^ 1) for k in range(lax.axis_size("ch"))]
    near, far = [], []
    for shift in SHIFTS:
        moves = [(a * NZ + b, (a + shift) % NX * NZ + b) for a in range(NX) for b in range(NZ)]
        near.append(lax.ppermute(half, "ctx", moves))
        far.append(lax.ppermute(near[-1], "ch", swap))

    rates = lax.dynamic_slice_in_dim(decay_rates, x * HALF, HALF, 0).T
    weights = lax.dynamic_slice_in_dim(residues, x * HALF, HALF, 0).T * jnp.sqrt(2.0 * rates)
    taps = lax.dynamic_slice_in_dim(short_filter, x * HALF, HALF, 0).T.astype(f32)
    rates, weights, taps = (jnp.concatenate([v, v], axis=1) for v in (rates, weights, taps))
    forward, inverse = jnp.asarray(real_transform()), jnp.asarray(inverse_transform())
    table = sds((MODES, ROWS, LANES), f32)
    spectrum = sds((SPAN, LANES), f32)
    into, out, long_spectrum, short_spectrum = call(
        build_tables, (table, table, spectrum, spectrum), "build_tables", rates, weights, taps, forward
    )
    scratch = [pltpu.VMEM((depth, LANES), bf16), pltpu.VMEM((NX, ROWS, LANES), f32)]
    operands = (tokens, *near, *far, blocks)
    signal, states = call(
        make_signal,
        (sds((ROWS, 2 * LANES), f32), sds((NZ, 2 * MODES, LANES), f32)),
        "make_signal",
        *operands,
        into,
        scratch=scratch,
    )
    states = lax.all_to_all(states, "ctx", 0, 0, tiled=True, axis_index_groups=z_groups)
    both = call(
        make_gates,
        sds((ROWS, 4 * LANES), f32),
        "make_gates",
        *operands,
        signal,
        forward,
        inverse,
        long_spectrum,
        scratch=scratch,
        flops=5 * 10**9,
    )
    onward = [(a * NZ + b, a * NZ + (b + 1) % NZ) for a in range(NX) for b in range(NZ)]
    arrived = lax.ppermute(both, "ctx", onward)
    packed = call(
        finish,
        sds((NX, HALF, LANES), bf16),
        "finish",
        both,
        arrived,
        states,
        rates,
        out,
        forward,
        inverse,
        short_spectrum,
    )
    packed = lax.all_to_all(packed, "ctx", 0, 0, tiled=True, axis_index_groups=x_groups)
    return call(unpack_rows, sds((ROWS, 2 * LANES), bf16), "unpack_rows", packed)


def solution(mesh):
    in_specs = (P("ctx", None), P(None, "ctx", "ch"), P("ch", None), P("ch", None), P("ch", None))
    return jax.shard_map(per_device, mesh=mesh, in_specs=in_specs, out_specs=P("ctx", "ch"), check_vma=False)
```

```python
import math

import jax
import jax.numpy as jnp
import numpy as np
from jax import lax
from jax.experimental import pallas as pl
from jax.experimental.pallas import tpu as pltpu
from jax.sharding import PartitionSpec as P

f32, bf16 = jnp.float32, jnp.bfloat16
highest = lax.Precision.HIGHEST

NX, NZ, NC = 4, 8, 2
ROWS = 128
LANES = 128
HALF = 64
SPAN = 2 * ROWS
MODES = 16

x_groups = [[x * NZ + z for x in range(NX)] for z in range(NZ)]
z_groups = [[x * NZ + z for z in range(NZ)] for x in range(NX)]


def real_transform():
    bins, places = np.arange(ROWS)[:, None], np.arange(SPAN)[None, :]
    angles = 2 * math.pi * (bins * places % SPAN) / SPAN
    real, imag = np.cos(angles), -np.sin(angles)
    imag[0] = np.where(np.arange(SPAN) % 2 == 0, 1.0, -1.0)
    return np.concatenate([real, imag]).astype(np.float32)


def inverse_transform():
    places, bins = np.arange(SPAN)[:, None], np.arange(ROWS)[None, :]
    angles = 2 * math.pi * (bins * places % SPAN) / SPAN
    real, imag = 2 * np.cos(angles), -2 * np.sin(angles)
    real[:, 0] = 1.0
    imag[:, 0] = np.where(np.arange(SPAN) % 2 == 0, 1.0, -1.0)
    return (np.concatenate([real, imag], axis=1) / SPAN).astype(np.float32)


def dot32(a, b):
    return jnp.dot(a, b, precision=highest, preferred_element_type=f32)


def multiply_spectra(u, h):
    first = lax.broadcasted_iota(jnp.int32, (ROWS, u.shape[1]), 0) == 0
    ur, ui, hr, hi = u[:ROWS], u[ROWS:], h[:ROWS], h[ROWS:]
    both = ui * hi
    real = ur * hr - jnp.where(first, 0.0, both)
    imag = jnp.where(first, both, ur * hi + ui * hr)
    return jnp.concatenate([real, imag], axis=0)


def lower_lanes(shape):
    return lax.broadcasted_iota(jnp.int32, shape, len(shape) - 1) < HALF


def swap_halves(v):
    return pltpu.roll(v, HALF, v.ndim - 1)


VMEM, ANY = pl.BlockSpec(memory_space=pltpu.VMEM), pl.BlockSpec(memory_space=pl.ANY)


def call(body, outs, *args, scratch=(), flops=10**8, far=0, out_specs=None):
    return pl.pallas_call(
        body,
        out_shape=outs,
        in_specs=[ANY] * far + [VMEM] * (len(args) - far),
        out_specs=jax.tree.map(lambda _: VMEM, outs) if out_specs is None else out_specs,
        scratch_shapes=scratch,
        compiler_params=pltpu.CompilerParams(vmem_limit_bytes=(60 if far else 16) << 20),
        cost_estimate=pl.CostEstimate(flops=flops, bytes_accessed=flops // 200, transcendentals=0),
    )(*args)


def spread_weights(w_ref, out_ref, block_ref, sems):
    low = lower_lanes((ROWS, LANES))
    low_half = lower_lanes((HALF, LANES))
    for x in range(NX):
        at = pl.ds(LANES * (x // 2), LANES)
        a, v, o = (w_ref[k, :, at].astype(f32) for k in range(3))
        if x % 2 == 0:
            both = jnp.where(low, a, swap_halves(v))
            packed = jnp.where(low_half, o[:HALF], swap_halves(o[HALF:]))
        else:
            both = jnp.where(low, swap_halves(a), v)
            packed = jnp.where(low_half, swap_halves(o[:HALF]), o[HALF:])
        both, packed = both.astype(bf16), packed.astype(bf16)
        block_ref[x, :ROWS] = both
        block_ref[x, ROWS:] = packed
        for z in range(NZ):
            pltpu.make_async_copy(block_ref.at[x], out_ref.at[x * NZ + z], sems.at[x * NZ + z]).start()
    for x in range(NX):
        for z in range(NZ):
            pltpu.make_async_copy(block_ref.at[x], out_ref.at[x * NZ + z], sems.at[x * NZ + z]).wait()


def build_tables(a_ref, w_ref, taps_ref, fwd_ref, out_ref, long_ref, short_ref):
    t = lax.broadcasted_iota(jnp.int32, (ROWS, LANES), 0).astype(f32)
    impulse = jnp.zeros((ROWS, LANES), f32)
    for m in range(MODES):
        rate, weight = a_ref[m : m + 1, :], w_ref[m : m + 1, :]
        out_ref[m] = weight * jnp.exp(-rate * (t + 1.0))
        impulse = impulse + weight * jnp.exp(-rate * t)
    transform = fwd_ref[:, :ROWS]
    long_ref[...] = dot32(transform, impulse)
    short_ref[...] = dot32(transform, taps_ref[...])


def positions():
    ctx, ch = lax.axis_index("ctx"), lax.axis_index("ch")
    return lax.div(ctx, NZ), lax.rem(ctx, NZ), lax.rem(ch, NC)


def token_copies(refs, bufs, sems):
    return [pltpu.make_async_copy(r, b, sems.at[k]) for k, (r, b) in enumerate(zip(refs, bufs))]


def fill_products(copies, bufs, weights_of, product_ref):
    x, _, core = positions()
    near = lax.rem(x + NX - 1 + 2 * core, NX)
    far = lax.rem(x + NX + 1 - 2 * core, NX)
    whole = weights_of(0, NX * NZ)
    for k, place in ((0, x), (1, near), (2, far)):
        copies[k].wait()
        product_ref[place] = jnp.dot(bufs[k][...], whole, preferred_element_type=f32)
    count = NX * NZ // NC
    copies[3].wait()
    total = jnp.dot(bufs[3][...], weights_of(core * count, count), preferred_element_type=f32)
    copies[4].wait()
    total = total + jnp.dot(bufs[4][...], weights_of((1 - core) * count, count), preferred_element_type=f32)
    product_ref[lax.rem(x + 2, NX)] = total


def make_signal(t0, t1, t2, t3, t4, blocks_ref, a_ref, signal_ref, state_ref, b0, b1, b2, b3, b4, into_ref, product_ref, sems):
    bufs = (b0, b1, b2, b3, b4)
    copies = token_copies((t0, t1, t2, t3, t4), bufs, sems)
    for copy in copies:
        copy.start()
    back = ROWS - 1.0 - lax.broadcasted_iota(jnp.int32, (ROWS, LANES), 0).astype(f32)
    for m in range(MODES):
        into_ref[m] = jnp.exp(-a_ref[m : m + 1, :] * back)

    def weights_of(first, count):
        return blocks_ref[pl.ds(first, count), :ROWS, :].reshape(count * ROWS, LANES)

    fill_products(copies, bufs, weights_of, product_ref)
    low = lower_lanes((ROWS, LANES))
    for pair in range(NX // 2):
        parts = []
        for chunk in (2 * pair, 2 * pair + 1):
            both = product_ref[chunk].astype(bf16).astype(f32)
            parts.append(both * swap_halves(both))
        signal = jnp.where(low, parts[0], parts[1])
        signal_ref[:, LANES * pair : LANES * (pair + 1)] = signal
        for m in range(MODES):
            state = jnp.sum(signal * into_ref[m], axis=0, keepdims=True)
            for z in range(NZ):
                state_ref[z, pair * MODES + m : pair * MODES + m + 1, :] = state


def make_gates(t0, t1, t2, t3, t4, blocks_ref, signal_ref, fwd_ref, inv_ref, long_ref, both_ref, b0, b1, b2, b3, b4, weight_ref, product_ref, sems):
    bufs = (b0, b1, b2, b3, b4)
    copies = token_copies((t0, t1, t2, t3, t4), bufs, sems)
    for copy in copies:
        copy.start()
    low_half = lower_lanes((HALF, LANES))
    for block in range(NX * NZ):
        packed = blocks_ref[block, ROWS:].astype(f32)
        turned = swap_halves(packed)
        weight_ref[block, :HALF, :] = jnp.where(low_half, packed, turned).astype(bf16)
        weight_ref[block, HALF:, :] = jnp.where(low_half, turned, packed).astype(bf16)

    def weights_of(first, count):
        return weight_ref[pl.ds(first, count)].reshape(count * ROWS, LANES)

    fill_products(copies, bufs, weights_of, product_ref)
    spectrum = dot32(fwd_ref[:, :ROWS], signal_ref[...])
    response = jnp.concatenate([long_ref[...]] * 2, axis=1)
    both_ref[:, : 2 * LANES] = dot32(inv_ref[:ROWS, :], multiply_spectra(spectrum, response))
    low = lower_lanes((ROWS, LANES))
    for pair in range(NX // 2):
        gate = jnp.where(low, product_ref[2 * pair], product_ref[2 * pair + 1])
        both_ref[:, LANES * (2 + pair) : LANES * (3 + pair)] = gate.astype(bf16).astype(f32)


def carry_in(states_ref, a_ref, z):
    low = lower_lanes((MODES, LANES))
    rate = a_ref[...] * float(ROWS)
    decay = jnp.exp(-rate)
    decay_row = jnp.exp(-rate * float(NZ))
    decay_here = jnp.exp(-rate * z.astype(f32))
    before, whole = [], []
    for pair in range(NX // 2):
        upto = jnp.zeros((MODES, LANES), f32)
        total = jnp.zeros((MODES, LANES), f32)
        for k in range(NZ):
            step = states_ref[k, pair * MODES : (pair + 1) * MODES, :]
            upto = jnp.where(k < z, upto * decay + step, upto)
            total = total * decay + step
        before.append(upto)
        whole.append(total)
    swapped = [swap_halves(v) for v in whole]
    first = jnp.where(low, 0.0, swapped[0])
    second = jnp.where(
        low,
        swapped[0] + decay_row * whole[0],
        swapped[1] + decay_row * (whole[0] + decay_row * swapped[0]),
    )
    return [before[0] + decay_here * first, before[1] + decay_here * second]


def gate_rows(both_ref, carries, out_ref):
    parts = []
    for pair in range(NX // 2):
        value = both_ref[:, LANES * pair : LANES * (pair + 1)]
        for m in range(MODES):
            value = value + out_ref[m] * carries[pair][m : m + 1, :]
        gate = both_ref[:, LANES * (2 + pair) : LANES * (3 + pair)]
        parts.append((gate * value).astype(bf16).astype(f32))
    return parts


def finish(both_ref, arrived_ref, states_ref, a_ref, out_ref, fwd_ref, inv_ref, short_ref, packed_ref):
    _, z, _ = positions()
    low = lower_lanes((ROWS, LANES))
    own = gate_rows(both_ref, carry_in(states_ref, a_ref, z), out_ref)
    arrived = gate_rows(arrived_ref, carry_in(states_ref, a_ref, lax.rem(z + NZ - 1, NZ)), out_ref)
    turned = [swap_halves(v) for v in arrived]
    shifted = [jnp.where(low, 0.0, turned[0]), jnp.where(low, turned[0], turned[1])]
    previous = jnp.concatenate([jnp.where(z == 0, s, a) for s, a in zip(shifted, arrived)], axis=1)
    window = jnp.concatenate([previous, jnp.concatenate(own, axis=1)], axis=0)
    response = jnp.concatenate([short_ref[...]] * 2, axis=1)
    mixed = dot32(inv_ref[ROWS:, :], multiply_spectra(dot32(fwd_ref[...], window), response))
    low_half = lower_lanes((HALF, LANES))
    for pair in range(2):
        top = mixed[:HALF, LANES * pair : LANES * (pair + 1)]
        bottom = mixed[HALF:, LANES * pair : LANES * (pair + 1)]
        packed_ref[2 * pair] = jnp.where(low_half, top, swap_halves(bottom)).astype(bf16)
        packed_ref[2 * pair + 1] = jnp.where(low_half, swap_halves(top), bottom).astype(bf16)


def unpack_rows(packed_ref, out_ref):
    low = lower_lanes((HALF, LANES))
    for pair in range(2):
        a, b = (packed_ref[2 * pair + h].astype(f32) for h in range(2))
        lanes = slice(LANES * pair, LANES * (pair + 1))
        out_ref[:HALF, lanes] = jnp.where(low, a, swap_halves(b)).astype(bf16)
        out_ref[HALF:, lanes] = jnp.where(low, swap_halves(a), b).astype(bf16)


def per_device(tokens, projections, decay_rates, residues, short_filter):
    sds = jax.ShapeDtypeStruct
    x = lax.axis_index("ctx") // NZ
    core = lax.axis_index("ch") % NC
    rows, features = tokens.shape
    width = features // NC
    count = NX * NZ
    wide = lax.axis_size("ch")

    def place(a, b, k):
        return (a % NX * NZ + b) * wide + k

    outward = [
        (place(a, b, k), place(a + 1 - 2 * (k % NC), b, k)) for a in range(NX) for b in range(NZ) for k in range(wide)
    ]
    swap = [(k, k ^ 1) for k in range(wide)]
    near = lax.ppermute(tokens, ("ctx", "ch"), outward)
    blocks = call(
        spread_weights,
        sds((count, ROWS + HALF, LANES), bf16),
        projections,
        scratch=[pltpu.VMEM((NX, ROWS + HALF, LANES), bf16), pltpu.SemaphoreType.DMA((count,))],
        out_specs=ANY,
    )
    blocks = lax.all_to_all(blocks, "ctx", 0, 0, tiled=True)
    far = lax.ppermute(near, "ch", swap)
    half = lax.ppermute(lax.dynamic_slice_in_dim(near, core * width, width, 1), ("ctx", "ch"), outward)
    other = lax.ppermute(half, "ch", swap)

    rates = lax.dynamic_slice_in_dim(decay_rates, x * HALF, HALF, 0).T
    weights = lax.dynamic_slice_in_dim(residues, x * HALF, HALF, 0).T * jnp.sqrt(2.0 * rates)
    taps = lax.dynamic_slice_in_dim(short_filter, x * HALF, HALF, 0).T.astype(f32)
    rates, weights, taps = (jnp.concatenate([v, v], axis=1) for v in (rates, weights, taps))
    forward, inverse = jnp.asarray(real_transform()), jnp.asarray(inverse_transform())
    table = sds((MODES, ROWS, LANES), f32)
    spectrum = sds((SPAN, LANES), f32)
    out, long_spectrum, short_spectrum = call(build_tables, (table, spectrum, spectrum), rates, weights, taps, forward)
    buffers = [pltpu.VMEM((rows, features), bf16)] * 3 + [pltpu.VMEM((rows, width), bf16)] * 2
    products = pltpu.VMEM((NX, ROWS, LANES), f32)
    arrivals = pltpu.SemaphoreType.DMA((5,))
    operands = (tokens, near, far, half, other, blocks)
    signal, states = call(
        make_signal,
        (sds((ROWS, 2 * LANES), f32), sds((NZ, 2 * MODES, LANES), f32)),
        *operands,
        rates,
        scratch=[*buffers, pltpu.VMEM((MODES, ROWS, LANES), f32), products, arrivals],
        far=5,
    )
    states = lax.all_to_all(states, "ctx", 0, 0, tiled=True, axis_index_groups=z_groups)
    both = call(
        make_gates,
        sds((ROWS, 4 * LANES), f32),
        *operands,
        signal,
        forward,
        inverse,
        long_spectrum,
        scratch=[*buffers, pltpu.VMEM((count, ROWS, LANES), bf16), products, arrivals],
        far=5,
    )
    onward = [(a * NZ + b, a * NZ + (b + 1) % NZ) for a in range(NX) for b in range(NZ)]
    arrived = lax.ppermute(both, "ctx", onward)
    packed = call(
        finish, sds((NX, HALF, LANES), bf16), both, arrived, states, rates, out, forward, inverse, short_spectrum
    )
    packed = lax.all_to_all(packed, "ctx", 0, 0, tiled=True, axis_index_groups=x_groups)
    return call(unpack_rows, sds((ROWS, 2 * LANES), bf16), packed)


def solution(mesh):
    in_specs = (P("ctx", None), P(None, "ctx", "ch"), P("ch", None), P("ch", None), P("ch", None))
    return jax.shard_map(per_device, mesh=mesh, in_specs=in_specs, out_specs=P("ctx", "ch"), check_vma=False)
```

```python
import math

import jax
import jax.numpy as jnp
import numpy as np
from jax import lax
from jax.experimental import pallas as pl
from jax.experimental.pallas import tpu as pltpu
from jax.sharding import PartitionSpec as P

f32, bf16 = jnp.float32, jnp.bfloat16
highest = lax.Precision.HIGHEST

NX, NZ, NC = 4, 8, 2
ROWS = 128
LANES = 128
HALF = 64
SPAN = 2 * ROWS
MODES = 16

x_groups = [[x * NZ + z for x in range(NX)] for z in range(NZ)]
z_groups = [[x * NZ + z for z in range(NZ)] for x in range(NX)]


def real_transform():
    bins, places = np.arange(ROWS)[:, None], np.arange(SPAN)[None, :]
    angles = 2 * math.pi * (bins * places % SPAN) / SPAN
    real, imag = np.cos(angles), -np.sin(angles)
    imag[0] = np.where(np.arange(SPAN) % 2 == 0, 1.0, -1.0)
    return np.concatenate([real, imag]).astype(np.float32)


def inverse_transform():
    places, bins = np.arange(SPAN)[:, None], np.arange(ROWS)[None, :]
    angles = 2 * math.pi * (bins * places % SPAN) / SPAN
    real, imag = 2 * np.cos(angles), -2 * np.sin(angles)
    real[:, 0] = 1.0
    imag[:, 0] = np.where(np.arange(SPAN) % 2 == 0, 1.0, -1.0)
    return (np.concatenate([real, imag], axis=1) / SPAN).astype(np.float32)


def dot32(a, b):
    return jnp.dot(a, b, precision=highest, preferred_element_type=f32)


def multiply_spectra(u, h):
    first = lax.broadcasted_iota(jnp.int32, (ROWS, u.shape[1]), 0) == 0
    ur, ui, hr, hi = u[:ROWS], u[ROWS:], h[:ROWS], h[ROWS:]
    both = ui * hi
    real = ur * hr - jnp.where(first, 0.0, both)
    imag = jnp.where(first, both, ur * hi + ui * hr)
    return jnp.concatenate([real, imag], axis=0)


def lower_lanes(shape):
    return lax.broadcasted_iota(jnp.int32, shape, len(shape) - 1) < HALF


def swap_halves(v):
    return pltpu.roll(v, HALF, v.ndim - 1)


VMEM, ANY = pl.BlockSpec(memory_space=pltpu.VMEM), pl.BlockSpec(memory_space=pl.ANY)


def call(body, outs, *args, scratch=(), flops=10**8, far=0, out_specs=None):
    return pl.pallas_call(
        body,
        out_shape=outs,
        in_specs=[ANY] * far + [VMEM] * (len(args) - far),
        out_specs=jax.tree.map(lambda _: VMEM, outs) if out_specs is None else out_specs,
        scratch_shapes=scratch,
        compiler_params=pltpu.CompilerParams(vmem_limit_bytes=(60 if far else 16) << 20),
        cost_estimate=pl.CostEstimate(flops=flops, bytes_accessed=flops // 200, transcendentals=0),
    )(*args)


def spread_weights(w_ref, out_ref, block_ref, sems):
    low = lower_lanes((ROWS, LANES))
    low_half = lower_lanes((HALF, LANES))
    for x in range(NX):
        at = pl.ds(LANES * (x // 2), LANES)
        a, v, o = (w_ref[k, :, at].astype(f32) for k in range(3))
        if x % 2 == 0:
            both = jnp.where(low, a, swap_halves(v))
            packed = jnp.where(low_half, o[:HALF], swap_halves(o[HALF:]))
        else:
            both = jnp.where(low, swap_halves(a), v)
            packed = jnp.where(low_half, swap_halves(o[:HALF]), o[HALF:])
        both, packed = both.astype(bf16), packed.astype(bf16)
        block_ref[x, :ROWS] = both
        block_ref[x, ROWS:] = packed
        for z in range(NZ):
            pltpu.make_async_copy(block_ref.at[x], out_ref.at[x * NZ + z], sems.at[x * NZ + z]).start()
    for x in range(NX):
        for z in range(NZ):
            pltpu.make_async_copy(block_ref.at[x], out_ref.at[x * NZ + z], sems.at[x * NZ + z]).wait()


def build_tables(a_ref, w_ref, taps_ref, fwd_ref, out_ref, long_ref, short_ref):
    t = lax.broadcasted_iota(jnp.int32, (ROWS, LANES), 0).astype(f32)
    impulse = jnp.zeros((ROWS, LANES), f32)
    for m in range(MODES):
        rate, weight = a_ref[m : m + 1, :], w_ref[m : m + 1, :]
        out_ref[m] = weight * jnp.exp(-rate * (t + 1.0))
        impulse = impulse + weight * jnp.exp(-rate * t)
    transform = fwd_ref[:, :ROWS]
    long_ref[...] = dot32(transform, impulse)
    short_ref[...] = dot32(transform, taps_ref[...])


def positions():
    ctx, ch = lax.axis_index("ctx"), lax.axis_index("ch")
    return lax.div(ctx, NZ), lax.rem(ctx, NZ), lax.rem(ch, NC)


PARTS = 4


def project(t0, t1, t2, t3, t4, blocks_ref, a_ref, streams_ref, state_ref, tokens_ref, arrived_ref, wide_ref, into_ref, product_ref, sems, block_sems):
    x, _, core = positions()
    near = lax.rem(x + NX - 1 + 2 * core, NX)
    far = lax.rem(x + NX + 1 - 2 * core, NX)
    across = lax.rem(x + 2, NX)
    part = t0.shape[1] // PARTS
    share = NX * NZ // PARTS

    def rows_of(k):
        return pl.ds(pl.multiple_of(k * ROWS, ROWS), ROWS)

    def block_copy(j):
        at = pl.ds(j * share, share)
        return pltpu.make_async_copy(blocks_ref.at[at], arrived_ref.at[at], block_sems.at[j])

    def token_copies(j):
        at = pl.ds(j * part, part)
        found = [
            pltpu.make_async_copy(ref.at[:, at], tokens_ref.at[rows_of(k), at], sems.at[i, j])
            for i, (ref, k) in enumerate(((t0, x), (t1, near), (t2, far)))
        ]
        half = PARTS // NC
        inner = pl.ds((j % half) * part, part)
        mine = (j // half) == core
        return found, mine, [
            pltpu.make_async_copy(ref.at[:, inner], tokens_ref.at[rows_of(across), at], sems.at[3, j]) for ref in (t3, t4)
        ]

    plans = [token_copies(j) for j in range(PARTS)]
    for j in range(PARTS):
        block_copy(j).start()
        found, mine, (first, second) = plans[j]
        for copy in found:
            copy.start()
        pl.when(mine)(first.start)
        pl.when(jnp.logical_not(mine))(second.start)
    back = ROWS - 1.0 - lax.broadcasted_iota(jnp.int32, (ROWS, LANES), 0).astype(f32)
    for m in range(MODES):
        into_ref[m] = jnp.exp(-a_ref[m : m + 1, :] * back)
    low_half = lower_lanes((HALF, LANES))
    for j in range(PARTS):
        block_copy(j).wait()
        for block in range(j * share, (j + 1) * share):
            top, bottom = pl.ds(ROWS * block, HALF), pl.ds(ROWS * block + HALF, HALF)
            wide_ref[pl.ds(ROWS * block, ROWS), :LANES] = arrived_ref[block, :ROWS]
            packed = arrived_ref[block, ROWS:].astype(f32)
            turned = swap_halves(packed)
            wide_ref[top, LANES:] = jnp.where(low_half, packed, turned).astype(bf16)
            wide_ref[bottom, LANES:] = jnp.where(low_half, turned, packed).astype(bf16)
        found, _, (first, _) = plans[j]
        for copy in found:
            copy.wait()
        first.wait()
        at = slice(j * part, (j + 1) * part)
        term = jnp.dot(tokens_ref[:, at], wide_ref[at, :], preferred_element_type=f32)
        product_ref[...] = term if j == 0 else product_ref[...] + term
    low = lower_lanes((ROWS, LANES))
    for pair in range(NX // 2):
        lanes = slice(LANES * pair, LANES * (pair + 1))
        chunks = [slice(ROWS * k, ROWS * (k + 1)) for k in (2 * pair, 2 * pair + 1)]
        a, b = (product_ref[k, :LANES].astype(bf16).astype(f32) for k in chunks)
        turned_a, turned_b = swap_halves(a), swap_halves(b)
        gate_in, values = jnp.where(low, a, turned_b), jnp.where(low, turned_a, b)
        gate_out = jnp.where(low, product_ref[chunks[0], LANES:], product_ref[chunks[1], LANES:])
        signal = gate_in * values
        for k, value in enumerate((gate_in, values, gate_out)):
            streams_ref[k, :, lanes] = value.astype(bf16)
        for m in range(MODES):
            state = jnp.sum(signal * into_ref[m], axis=0, keepdims=True)
            for z in range(NZ):
                state_ref[z, pair * MODES + m : pair * MODES + m + 1, :] = state


def filter_inside(streams_ref, fwd_ref, inv_ref, long_ref):
    signal = streams_ref[0].astype(f32) * streams_ref[1].astype(f32)
    spectrum = dot32(fwd_ref[:, :ROWS], signal)
    response = jnp.concatenate([long_ref[...]] * 2, axis=1)
    return dot32(inv_ref[:ROWS, :], multiply_spectra(spectrum, response))


def filter_chunks(streams_ref, fwd_ref, inv_ref, long_ref, local_ref):
    local_ref[...] = filter_inside(streams_ref, fwd_ref, inv_ref, long_ref)


def carry_in(states_ref, a_ref, z):
    low = lower_lanes((MODES, LANES))
    rate = a_ref[...] * float(ROWS)
    decay = jnp.exp(-rate)
    decay_row = jnp.exp(-rate * float(NZ))
    decay_here = jnp.exp(-rate * z.astype(f32))
    before, whole = [], []
    for pair in range(NX // 2):
        upto = jnp.zeros((MODES, LANES), f32)
        total = jnp.zeros((MODES, LANES), f32)
        for k in range(NZ):
            step = states_ref[k, pair * MODES : (pair + 1) * MODES, :]
            upto = jnp.where(k < z, upto * decay + step, upto)
            total = total * decay + step
        before.append(upto)
        whole.append(total)
    swapped = [swap_halves(v) for v in whole]
    first = jnp.where(low, 0.0, swapped[0])
    second = jnp.where(
        low,
        swapped[0] + decay_row * whole[0],
        swapped[1] + decay_row * (whole[0] + decay_row * swapped[0]),
    )
    return [before[0] + decay_here * first, before[1] + decay_here * second]


def gate_rows(streams_ref, local, carries, out_ref):
    parts = []
    for pair in range(NX // 2):
        lanes = slice(LANES * pair, LANES * (pair + 1))
        value = local[:, lanes]
        for m in range(MODES):
            value = value + out_ref[m] * carries[pair][m : m + 1, :]
        parts.append((streams_ref[2, :, lanes].astype(f32) * value).astype(bf16).astype(f32))
    return parts


def finish(streams_ref, local_ref, arrived_ref, states_ref, a_ref, out_ref, fwd_ref, inv_ref, long_ref, short_ref, packed_ref):
    _, z, _ = positions()
    low = lower_lanes((ROWS, LANES))
    before = filter_inside(arrived_ref, fwd_ref, inv_ref, long_ref)
    own = gate_rows(streams_ref, local_ref[...], carry_in(states_ref, a_ref, z), out_ref)
    arrived = gate_rows(arrived_ref, before, carry_in(states_ref, a_ref, lax.rem(z + NZ - 1, NZ)), out_ref)
    turned = [swap_halves(v) for v in arrived]
    shifted = [jnp.where(low, 0.0, turned[0]), jnp.where(low, turned[0], turned[1])]
    previous = jnp.concatenate([jnp.where(z == 0, s, a) for s, a in zip(shifted, arrived)], axis=1)
    window = jnp.concatenate([previous, jnp.concatenate(own, axis=1)], axis=0)
    response = jnp.concatenate([short_ref[...]] * 2, axis=1)
    mixed = dot32(inv_ref[ROWS:, :], multiply_spectra(dot32(fwd_ref[...], window), response))
    low_half = lower_lanes((HALF, LANES))
    for pair in range(2):
        top = mixed[:HALF, LANES * pair : LANES * (pair + 1)]
        bottom = mixed[HALF:, LANES * pair : LANES * (pair + 1)]
        packed_ref[2 * pair] = jnp.where(low_half, top, swap_halves(bottom)).astype(bf16)
        packed_ref[2 * pair + 1] = jnp.where(low_half, swap_halves(top), bottom).astype(bf16)


def unpack_rows(packed_ref, out_ref):
    low = lower_lanes((HALF, LANES))
    for pair in range(2):
        a, b = (packed_ref[2 * pair + h].astype(f32) for h in range(2))
        lanes = slice(LANES * pair, LANES * (pair + 1))
        out_ref[:HALF, lanes] = jnp.where(low, a, swap_halves(b)).astype(bf16)
        out_ref[HALF:, lanes] = jnp.where(low, swap_halves(a), b).astype(bf16)


def per_device(tokens, projections, decay_rates, residues, short_filter):
    sds = jax.ShapeDtypeStruct
    x = lax.axis_index("ctx") // NZ
    core = lax.axis_index("ch") % NC
    rows, features = tokens.shape
    width = features // NC
    count = NX * NZ
    wide = lax.axis_size("ch")

    def place(a, b, k):
        return (a % NX * NZ + b) * wide + k

    outward = [
        (place(a, b, k), place(a + 1 - 2 * (k % NC), b, k)) for a in range(NX) for b in range(NZ) for k in range(wide)
    ]
    swap = [(k, k ^ 1) for k in range(wide)]
    near = lax.ppermute(tokens, ("ctx", "ch"), outward)
    blocks = call(
        spread_weights,
        sds((count, ROWS + HALF, LANES), bf16),
        projections,
        scratch=[pltpu.VMEM((NX, ROWS + HALF, LANES), bf16), pltpu.SemaphoreType.DMA((count,))],
        out_specs=ANY,
    )
    blocks = lax.all_to_all(blocks, "ctx", 0, 0, tiled=True)
    far = lax.ppermute(near, "ch", swap)
    half = lax.ppermute(lax.dynamic_slice_in_dim(near, core * width, width, 1), ("ctx", "ch"), outward)
    other = lax.ppermute(half, "ch", swap)

    rates = lax.dynamic_slice_in_dim(decay_rates, x * HALF, HALF, 0).T
    weights = lax.dynamic_slice_in_dim(residues, x * HALF, HALF, 0).T * jnp.sqrt(2.0 * rates)
    taps = lax.dynamic_slice_in_dim(short_filter, x * HALF, HALF, 0).T.astype(f32)
    rates, weights, taps = (jnp.concatenate([v, v], axis=1) for v in (rates, weights, taps))
    forward, inverse = jnp.asarray(real_transform()), jnp.asarray(inverse_transform())
    table = sds((MODES, ROWS, LANES), f32)
    spectrum = sds((SPAN, LANES), f32)
    out, long_spectrum, short_spectrum = call(build_tables, (table, spectrum, spectrum), rates, weights, taps, forward)
    streams, states = call(
        project,
        (sds((3, ROWS, 2 * LANES), bf16), sds((NZ, 2 * MODES, LANES), f32)),
        tokens,
        near,
        far,
        half,
        other,
        blocks,
        rates,
        scratch=[
            pltpu.VMEM((NX * rows, features), bf16),
            pltpu.VMEM((count, ROWS + HALF, LANES), bf16),
            pltpu.VMEM((features, 2 * LANES), bf16),
            pltpu.VMEM((MODES, ROWS, LANES), f32),
            pltpu.VMEM((NX * rows, 2 * LANES), f32),
            pltpu.SemaphoreType.DMA((4, PARTS)),
            pltpu.SemaphoreType.DMA((PARTS,)),
        ],
        far=6,
    )
    states = lax.all_to_all(states, "ctx", 0, 0, tiled=True, axis_index_groups=z_groups)
    onward = [(a * NZ + b, a * NZ + (b + 1) % NZ) for a in range(NX) for b in range(NZ)]
    arrived = lax.ppermute(streams, "ctx", onward)
    local = call(filter_chunks, sds((ROWS, 2 * LANES), f32), streams, forward, inverse, long_spectrum)
    packed = call(
        finish,
        sds((NX, HALF, LANES), bf16),
        streams,
        local,
        arrived,
        states,
        rates,
        out,
        forward,
        inverse,
        long_spectrum,
        short_spectrum,
    )
    packed = lax.all_to_all(packed, "ctx", 0, 0, tiled=True, axis_index_groups=x_groups)
    return call(unpack_rows, sds((ROWS, 2 * LANES), bf16), packed)


def solution(mesh):
    in_specs = (P("ctx", None), P(None, "ctx", "ch"), P("ch", None), P("ch", None), P("ch", None))
    return jax.shard_map(per_device, mesh=mesh, in_specs=in_specs, out_specs=P("ctx", "ch"), check_vma=False)
```

```python
import math

import jax
import jax.numpy as jnp
import numpy as np
from jax import lax
from jax.experimental import pallas as pl
from jax.experimental.pallas import tpu as pltpu
from jax.sharding import PartitionSpec as P

f32, bf16 = jnp.float32, jnp.bfloat16
highest = lax.Precision.HIGHEST

NX, NZ, NC = 4, 8, 2
ROWS = 128
LANES = 128
HALF = 64
SPAN = 2 * ROWS
MODES = 16

parity_groups = [[x * NZ + z for x in range(NX) for z in range(p, NZ, 2)] for p in range(2)]
x_groups = [[x * NZ + z for x in range(NX)] for z in range(NZ)]
z_groups = [[x * NZ + z for z in range(NZ)] for x in range(NX)]


def real_transform():
    bins, places = np.arange(ROWS)[:, None], np.arange(SPAN)[None, :]
    angles = 2 * math.pi * (bins * places % SPAN) / SPAN
    real, imag = np.cos(angles), -np.sin(angles)
    imag[0] = np.where(np.arange(SPAN) % 2 == 0, 1.0, -1.0)
    return np.concatenate([real, imag]).astype(np.float32)


def inverse_transform():
    places, bins = np.arange(SPAN)[:, None], np.arange(ROWS)[None, :]
    angles = 2 * math.pi * (bins * places % SPAN) / SPAN
    real, imag = 2 * np.cos(angles), -2 * np.sin(angles)
    real[:, 0] = 1.0
    imag[:, 0] = np.where(np.arange(SPAN) % 2 == 0, 1.0, -1.0)
    return (np.concatenate([real, imag], axis=1) / SPAN).astype(np.float32)


def dot32(a, b):
    return jnp.dot(a, b, precision=highest, preferred_element_type=f32)


def multiply_spectra(u, h):
    first = lax.broadcasted_iota(jnp.int32, (ROWS, u.shape[1]), 0) == 0
    ur, ui, hr, hi = u[:ROWS], u[ROWS:], h[:ROWS], h[ROWS:]
    both = ui * hi
    real = ur * hr - jnp.where(first, 0.0, both)
    imag = jnp.where(first, both, ur * hi + ui * hr)
    return jnp.concatenate([real, imag], axis=0)


def lower_lanes(shape):
    return lax.broadcasted_iota(jnp.int32, shape, len(shape) - 1) < HALF


def swap_halves(v):
    return pltpu.roll(v, HALF, v.ndim - 1)


VMEM, ANY = pl.BlockSpec(memory_space=pltpu.VMEM), pl.BlockSpec(memory_space=pltpu.HBM)


def call(body, outs, *args, scratch=(), flops=10**8, far=0, out_specs=None):
    return pl.pallas_call(
        body,
        out_shape=outs,
        in_specs=[ANY] * far + [VMEM] * (len(args) - far),
        out_specs=jax.tree.map(lambda _: VMEM, outs) if out_specs is None else out_specs,
        scratch_shapes=scratch,
        compiler_params=pltpu.CompilerParams(vmem_limit_bytes=16 << 20),
        cost_estimate=pl.CostEstimate(flops=flops, bytes_accessed=flops // 200, transcendentals=0),
    )(*args)


def spread_weights(w_ref, out_ref, block_ref, sems):
    low = lower_lanes((ROWS, LANES))
    low_half = lower_lanes((HALF, LANES))
    for x in range(NX):
        at = pl.ds(LANES * (x // 2), LANES)
        a, v, o = (w_ref[k, :, at].astype(f32) for k in range(3))
        if x % 2 == 0:
            both = jnp.where(low, a, swap_halves(v))
            packed = jnp.where(low_half, o[:HALF], swap_halves(o[HALF:]))
        else:
            both = jnp.where(low, swap_halves(a), v)
            packed = jnp.where(low_half, swap_halves(o[:HALF]), o[HALF:])
        both, packed = both.astype(bf16), packed.astype(bf16)
        block_ref[x, :ROWS] = both
        block_ref[x, ROWS:] = packed
        for z in range(NZ // 2):
            at = x * (NZ // 2) + z
            pltpu.make_async_copy(block_ref.at[x], out_ref.at[at], sems.at[at]).start()
    for x in range(NX):
        for z in range(NZ // 2):
            at = x * (NZ // 2) + z
            pltpu.make_async_copy(block_ref.at[x], out_ref.at[at], sems.at[at]).wait()


def build_tables(a_ref, w_ref, taps_ref, fwd_ref, out_ref, long_ref, short_ref):
    t = lax.broadcasted_iota(jnp.int32, (ROWS, LANES), 0).astype(f32)
    impulse = jnp.zeros((ROWS, LANES), f32)
    for m in range(MODES):
        rate, weight = a_ref[m : m + 1, :], w_ref[m : m + 1, :]
        out_ref[m] = weight * jnp.exp(-rate * (t + 1.0))
        impulse = impulse + weight * jnp.exp(-rate * t)
    transform = fwd_ref[:, :ROWS]
    long_ref[...] = dot32(transform, impulse)
    short_ref[...] = dot32(transform, taps_ref[...])


def positions():
    ctx, ch = lax.axis_index("ctx"), lax.axis_index("ch")
    return lax.div(ctx, NZ), lax.rem(ctx, NZ), lax.rem(ch, NC)


BLOCKS = NX * NZ // 2


def widen(blocks_ref, wide_ref):
    low_half = lower_lanes((HALF, LANES))
    for block in range(BLOCKS):
        top, bottom = slice(ROWS * block, ROWS * block + HALF), slice(ROWS * block + HALF, ROWS * (block + 1))
        wide_ref[ROWS * block : ROWS * (block + 1), :LANES] = blocks_ref[block, :ROWS]
        packed = blocks_ref[block, ROWS:].astype(f32)
        turned = swap_halves(packed)
        wide_ref[top, LANES:] = jnp.where(low_half, packed, turned).astype(bf16)
        wide_ref[bottom, LANES:] = jnp.where(low_half, turned, packed).astype(bf16)


def project_first(t0, t1, t2, t3, t4, blocks_ref, product_ref, rest_ref, tokens_ref, wide_ref, sems):
    x, z, core = positions()
    near = lax.rem(x + NX - 1 + 2 * core, NX)
    far = lax.rem(x + NX + 1 - 2 * core, NX)
    across = lax.rem(x + 2, NX)
    half = BLOCKS // NC

    def rows_of(k):
        return pl.ds(pl.multiple_of(k * ROWS, ROWS), ROWS)

    for side, target in ((0, tokens_ref), (1, rest_ref)):
        parity = lax.rem(z + side, 2)
        for i in range(BLOCKS):
            to = pl.ds(LANES * i, LANES)
            at = pl.ds(pl.multiple_of((2 * i + parity) * LANES, LANES), LANES)
            for k, (ref, place) in enumerate(((t0, x), (t1, near), (t2, far))):
                pltpu.make_async_copy(ref.at[:, at], target.at[rows_of(place), to], sems.at[k, side]).start()
            inner = pl.ds(pl.multiple_of((2 * (i % half) + parity) * LANES, LANES), LANES)
            mine = (i // half) == core
            first = pltpu.make_async_copy(t3.at[:, inner], target.at[rows_of(across), to], sems.at[3, side])
            second = pltpu.make_async_copy(t4.at[:, inner], target.at[rows_of(across), to], sems.at[3, side])
            pl.when(mine)(first.start)
            pl.when(jnp.logical_not(mine))(second.start)
    widen(blocks_ref, wide_ref)

    def wait(target, side):
        for k in range(4):
            rows = target.at[slice(ROWS * k, ROWS * (k + 1))]
            pltpu.make_async_copy(rows, rows, sems.at[k, side]).wait()

    wait(tokens_ref, 0)
    product_ref[...] = jnp.dot(tokens_ref[...], wide_ref[...], preferred_element_type=f32)
    wait(rest_ref, 1)


def project_rest(rest_ref, product_ref, blocks_ref, a_ref, streams_ref, state_ref, wide_ref, into_ref, total_ref):
    widen(blocks_ref, wide_ref)
    total_ref[...] = product_ref[...] + jnp.dot(rest_ref[...], wide_ref[...], preferred_element_type=f32)
    back = ROWS - 1.0 - lax.broadcasted_iota(jnp.int32, (ROWS, LANES), 0).astype(f32)
    for m in range(MODES):
        into_ref[m] = jnp.exp(-a_ref[m : m + 1, :] * back)
    low = lower_lanes((ROWS, LANES))
    for pair in range(NX // 2):
        lanes = slice(LANES * pair, LANES * (pair + 1))
        chunks = [slice(ROWS * k, ROWS * (k + 1)) for k in (2 * pair, 2 * pair + 1)]
        a, b = (total_ref[k, :LANES].astype(bf16).astype(f32) for k in chunks)
        turned_a, turned_b = swap_halves(a), swap_halves(b)
        gate_in, values = jnp.where(low, a, turned_b), jnp.where(low, turned_a, b)
        gate_out = jnp.where(low, total_ref[chunks[0], LANES:], total_ref[chunks[1], LANES:])
        signal = gate_in * values
        for k, value in enumerate((gate_in, values, gate_out)):
            streams_ref[k, :, lanes] = value.astype(bf16)
        for m in range(MODES):
            state = jnp.sum(signal * into_ref[m], axis=0, keepdims=True)
            for z in range(NZ):
                state_ref[z, pair * MODES + m : pair * MODES + m + 1, :] = state


def filter_inside(streams_ref, fwd_ref, inv_ref, long_ref):
    signal = streams_ref[0].astype(f32) * streams_ref[1].astype(f32)
    spectrum = dot32(fwd_ref[:, :ROWS], signal)
    response = jnp.concatenate([long_ref[...]] * 2, axis=1)
    return dot32(inv_ref[:ROWS, :], multiply_spectra(spectrum, response))


def filter_chunks(streams_ref, fwd_ref, inv_ref, long_ref, local_ref):
    local_ref[...] = filter_inside(streams_ref, fwd_ref, inv_ref, long_ref)


def carry_in(states_ref, a_ref, z):
    low = lower_lanes((MODES, LANES))
    rate = a_ref[...] * float(ROWS)
    decay = jnp.exp(-rate)
    decay_row = jnp.exp(-rate * float(NZ))
    decay_here = jnp.exp(-rate * z.astype(f32))
    before, whole = [], []
    for pair in range(NX // 2):
        upto = jnp.zeros((MODES, LANES), f32)
        total = jnp.zeros((MODES, LANES), f32)
        for k in range(NZ):
            step = states_ref[k, pair * MODES : (pair + 1) * MODES, :]
            upto = jnp.where(k < z, upto * decay + step, upto)
            total = total * decay + step
        before.append(upto)
        whole.append(total)
    swapped = [swap_halves(v) for v in whole]
    first = jnp.where(low, 0.0, swapped[0])
    second = jnp.where(
        low,
        swapped[0] + decay_row * whole[0],
        swapped[1] + decay_row * (whole[0] + decay_row * swapped[0]),
    )
    return [before[0] + decay_here * first, before[1] + decay_here * second]


def gate_rows(streams_ref, local, carries, out_ref):
    parts = []
    for pair in range(NX // 2):
        lanes = slice(LANES * pair, LANES * (pair + 1))
        value = local[:, lanes]
        for m in range(MODES):
            value = value + out_ref[m] * carries[pair][m : m + 1, :]
        parts.append((streams_ref[2, :, lanes].astype(f32) * value).astype(bf16).astype(f32))
    return parts


def finish(streams_ref, local_ref, arrived_ref, states_ref, a_ref, out_ref, fwd_ref, inv_ref, long_ref, short_ref, packed_ref):
    _, z, _ = positions()
    low = lower_lanes((ROWS, LANES))
    before = filter_inside(arrived_ref, fwd_ref, inv_ref, long_ref)
    own = gate_rows(streams_ref, local_ref[...], carry_in(states_ref, a_ref, z), out_ref)
    arrived = gate_rows(arrived_ref, before, carry_in(states_ref, a_ref, lax.rem(z + NZ - 1, NZ)), out_ref)
    turned = [swap_halves(v) for v in arrived]
    shifted = [jnp.where(low, 0.0, turned[0]), jnp.where(low, turned[0], turned[1])]
    previous = jnp.concatenate([jnp.where(z == 0, s, a) for s, a in zip(shifted, arrived)], axis=1)
    window = jnp.concatenate([previous, jnp.concatenate(own, axis=1)], axis=0)
    response = jnp.concatenate([short_ref[...]] * 2, axis=1)
    mixed = dot32(inv_ref[ROWS:, :], multiply_spectra(dot32(fwd_ref[...], window), response))
    low_half = lower_lanes((HALF, LANES))
    for pair in range(2):
        top = mixed[:HALF, LANES * pair : LANES * (pair + 1)]
        bottom = mixed[HALF:, LANES * pair : LANES * (pair + 1)]
        packed_ref[2 * pair] = jnp.where(low_half, top, swap_halves(bottom)).astype(bf16)
        packed_ref[2 * pair + 1] = jnp.where(low_half, swap_halves(top), bottom).astype(bf16)


def unpack_rows(packed_ref, out_ref):
    low = lower_lanes((HALF, LANES))
    for pair in range(2):
        a, b = (packed_ref[2 * pair + h].astype(f32) for h in range(2))
        lanes = slice(LANES * pair, LANES * (pair + 1))
        out_ref[:HALF, lanes] = jnp.where(low, a, swap_halves(b)).astype(bf16)
        out_ref[HALF:, lanes] = jnp.where(low, swap_halves(a), b).astype(bf16)


def per_device(tokens, projections, decay_rates, residues, short_filter):
    sds = jax.ShapeDtypeStruct
    x = lax.axis_index("ctx") // NZ
    core = lax.axis_index("ch") % NC
    rows, features = tokens.shape
    width = features // NC
    wide = lax.axis_size("ch")

    def place(a, b, k):
        return (a % NX * NZ + b) * wide + k

    outward = [
        (place(a, b, k), place(a + 1 - 2 * (k % NC), b, k)) for a in range(NX) for b in range(NZ) for k in range(wide)
    ]
    swap = [(k, k ^ 1) for k in range(wide)]
    near = lax.ppermute(tokens, ("ctx", "ch"), outward)
    blocks = call(
        spread_weights,
        sds((BLOCKS, ROWS + HALF, LANES), bf16),
        projections,
        scratch=[pltpu.VMEM((NX, ROWS + HALF, LANES), bf16), pltpu.SemaphoreType.DMA((BLOCKS,))],
        out_specs=ANY,
    )
    blocks = lax.all_to_all(blocks, "ctx", 0, 0, tiled=True, axis_index_groups=parity_groups)
    across = [
        (place(a, b, k), place(a, (b + 1 - 2 * (k % NC)) % NZ, k)) for a in range(NX) for b in range(NZ) for k in range(wide)
    ]
    rest_blocks = lax.ppermute(blocks, ("ctx", "ch"), across)
    far = lax.ppermute(near, "ch", swap)
    half = lax.ppermute(lax.dynamic_slice_in_dim(near, core * width, width, 1), ("ctx", "ch"), outward)
    other = lax.ppermute(half, "ch", swap)

    rates = lax.dynamic_slice_in_dim(decay_rates, x * HALF, HALF, 0).T
    weights = lax.dynamic_slice_in_dim(residues, x * HALF, HALF, 0).T * jnp.sqrt(2.0 * rates)
    taps = lax.dynamic_slice_in_dim(short_filter, x * HALF, HALF, 0).T.astype(f32)
    rates, weights, taps = (jnp.concatenate([v, v], axis=1) for v in (rates, weights, taps))
    forward, inverse = jnp.asarray(real_transform()), jnp.asarray(inverse_transform())
    table = sds((MODES, ROWS, LANES), f32)
    spectrum = sds((SPAN, LANES), f32)
    out, long_spectrum, short_spectrum = call(build_tables, (table, spectrum, spectrum), rates, weights, taps, forward)
    half_depth = BLOCKS * ROWS
    product, rest = call(
        project_first,
        (sds((NX * rows, 2 * LANES), f32), sds((NX * rows, half_depth), bf16)),
        tokens,
        near,
        far,
        half,
        other,
        blocks,
        scratch=[
            pltpu.VMEM((NX * rows, half_depth), bf16),
            pltpu.VMEM((half_depth, 2 * LANES), bf16),
            pltpu.SemaphoreType.DMA((4, 2)),
        ],
        far=5,
    )
    streams, states = call(
        project_rest,
        (sds((3, ROWS, 2 * LANES), bf16), sds((NZ, 2 * MODES, LANES), f32)),
        rest,
        product,
        rest_blocks,
        rates,
        scratch=[
            pltpu.VMEM((half_depth, 2 * LANES), bf16),
            pltpu.VMEM((MODES, ROWS, LANES), f32),
            pltpu.VMEM((NX * rows, 2 * LANES), f32),
        ],
    )
    states = lax.all_to_all(states, "ctx", 0, 0, tiled=True, axis_index_groups=z_groups)
    onward = [(a * NZ + b, a * NZ + (b + 1) % NZ) for a in range(NX) for b in range(NZ)]
    arrived = lax.ppermute(streams, "ctx", onward)
    local = call(filter_chunks, sds((ROWS, 2 * LANES), f32), streams, forward, inverse, long_spectrum)
    packed = call(
        finish,
        sds((NX, HALF, LANES), bf16),
        streams,
        local,
        arrived,
        states,
        rates,
        out,
        forward,
        inverse,
        long_spectrum,
        short_spectrum,
    )
    packed = lax.all_to_all(packed, "ctx", 0, 0, tiled=True, axis_index_groups=x_groups)
    return call(unpack_rows, sds((ROWS, 2 * LANES), bf16), packed)


def solution(mesh):
    in_specs = (P("ctx", None), P(None, "ctx", "ch"), P("ch", None), P("ch", None), P("ch", None))
    return jax.shard_map(per_device, mesh=mesh, in_specs=in_specs, out_specs=P("ctx", "ch"), check_vma=False)
```

```python
import math

import jax
import jax.numpy as jnp
import numpy as np
from jax import lax
from jax.experimental import pallas as pl
from jax.experimental.pallas import tpu as pltpu
from jax.sharding import PartitionSpec as P

f32, bf16 = jnp.float32, jnp.bfloat16

NX, NZ, NC = 4, 8, 2
ROWS = 128
LANES = 128
HALF = 64
SPAN = 2 * ROWS
MODES = 16

parity_groups = [[x * NZ + z for x in range(NX) for z in range(p, NZ, 2)] for p in range(2)]
x_groups = [[x * NZ + z for x in range(NX)] for z in range(NZ)]
z_groups = [[x * NZ + z for z in range(NZ)] for x in range(NX)]


def real_transform():
    bins, places = np.arange(ROWS)[:, None], np.arange(SPAN)[None, :]
    angles = 2 * math.pi * (bins * places % SPAN) / SPAN
    real, imag = np.cos(angles), -np.sin(angles)
    imag[0] = np.where(np.arange(SPAN) % 2 == 0, 1.0, -1.0)
    return np.concatenate([real, imag]).astype(np.float32)


def inverse_transform():
    places, bins = np.arange(SPAN)[:, None], np.arange(ROWS)[None, :]
    angles = 2 * math.pi * (bins * places % SPAN) / SPAN
    real, imag = 2 * np.cos(angles), -2 * np.sin(angles)
    real[:, 0] = 1.0
    imag[:, 0] = np.where(np.arange(SPAN) % 2 == 0, 1.0, -1.0)
    return (np.concatenate([real, imag], axis=1) / SPAN).astype(np.float32)


def halves(v):
    high = v.astype(bf16)
    return high, (v - high.astype(f32)).astype(bf16)


def dot_pair(a, b):
    high, low = halves(a)
    if b.dtype == bf16:
        return dot(high, b) + dot(low, b)
    b_high, b_low = halves(b)
    return dot(high, b_high) + (dot(high, b_low) + dot(low, b_high))


def dot(a, b):
    return jnp.dot(a, b, preferred_element_type=f32)


def multiply_spectra(u, h):
    first = lax.broadcasted_iota(jnp.int32, (ROWS, u.shape[1]), 0) == 0
    ur, ui, hr, hi = u[:ROWS], u[ROWS:], h[:ROWS], h[ROWS:]
    both = ui * hi
    real = ur * hr - jnp.where(first, 0.0, both)
    imag = jnp.where(first, both, ur * hi + ui * hr)
    return jnp.concatenate([real, imag], axis=0)


def lower_lanes(shape):
    return lax.broadcasted_iota(jnp.int32, shape, len(shape) - 1) < HALF


def swap_halves(v):
    return pltpu.roll(v, HALF, v.ndim - 1)


VMEM, ANY = pl.BlockSpec(memory_space=pltpu.VMEM), pl.BlockSpec(memory_space=pltpu.HBM)


def call(body, outs, *args, scratch=(), flops=10**8, far=0, out_specs=None):
    return pl.pallas_call(
        body,
        out_shape=outs,
        in_specs=[ANY] * far + [VMEM] * (len(args) - far),
        out_specs=jax.tree.map(lambda _: VMEM, outs) if out_specs is None else out_specs,
        scratch_shapes=scratch,
        compiler_params=pltpu.CompilerParams(vmem_limit_bytes=16 << 20),
        cost_estimate=pl.CostEstimate(flops=flops, bytes_accessed=flops // 200, transcendentals=0),
    )(*args)


def spread_weights(w_ref, out_ref, block_ref, sems):
    low = lower_lanes((ROWS, LANES))
    low_half = lower_lanes((HALF, LANES))
    for x in range(NX):
        at = pl.ds(LANES * (x // 2), LANES)
        a, v, o = (w_ref[k, :, at].astype(f32) for k in range(3))
        if x % 2 == 0:
            both = jnp.where(low, a, swap_halves(v))
            packed = jnp.where(low_half, o[:HALF], swap_halves(o[HALF:]))
        else:
            both = jnp.where(low, swap_halves(a), v)
            packed = jnp.where(low_half, swap_halves(o[:HALF]), o[HALF:])
        both, packed = both.astype(bf16), packed.astype(bf16)
        block_ref[x, :ROWS] = both
        block_ref[x, ROWS:] = packed
        for z in range(NZ // 2):
            at = x * (NZ // 2) + z
            pltpu.make_async_copy(block_ref.at[x], out_ref.at[at], sems.at[at]).start()
    for x in range(NX):
        for z in range(NZ // 2):
            at = x * (NZ // 2) + z
            pltpu.make_async_copy(block_ref.at[x], out_ref.at[at], sems.at[at]).wait()


def build_tables(a_ref, w_ref, taps_ref, fwd_ref, out_ref, long_ref, short_ref):
    t = lax.broadcasted_iota(jnp.int32, (ROWS, LANES), 0).astype(f32)
    impulse = jnp.zeros((ROWS, LANES), f32)
    for m in range(MODES):
        rate, weight = a_ref[m : m + 1, :], w_ref[m : m + 1, :]
        out_ref[m] = weight * jnp.exp(-rate * (t + 1.0))
        impulse = impulse + weight * jnp.exp(-rate * t)
    transform = fwd_ref[:, :ROWS]
    long_ref[...] = dot_pair(transform, impulse)
    short_ref[...] = dot_pair(transform, taps_ref[...])


def positions():
    ctx, ch = lax.axis_index("ctx"), lax.axis_index("ch")
    return lax.div(ctx, NZ), lax.rem(ctx, NZ), lax.rem(ch, NC)


BLOCKS = NX * NZ // 2


def widen(blocks_ref, wide_ref):
    low_half = lower_lanes((HALF, LANES))
    for block in range(BLOCKS):
        top, bottom = slice(ROWS * block, ROWS * block + HALF), slice(ROWS * block + HALF, ROWS * (block + 1))
        wide_ref[ROWS * block : ROWS * (block + 1), :LANES] = blocks_ref[block, :ROWS]
        packed = blocks_ref[block, ROWS:].astype(f32)
        turned = swap_halves(packed)
        wide_ref[top, LANES:] = jnp.where(low_half, packed, turned).astype(bf16)
        wide_ref[bottom, LANES:] = jnp.where(low_half, turned, packed).astype(bf16)


def project_first(t0, t1, t2, t3, t4, blocks_ref, a_ref, product_ref, rest_ref, into_ref, tokens_ref, wide_ref, sems):
    x, z, core = positions()
    near = lax.rem(x + NX - 1 + 2 * core, NX)
    far = lax.rem(x + NX + 1 - 2 * core, NX)
    across = lax.rem(x + 2, NX)
    half = BLOCKS // NC

    def rows_of(k):
        return pl.ds(pl.multiple_of(k * ROWS, ROWS), ROWS)

    for side, target in ((0, tokens_ref), (1, rest_ref)):
        parity = lax.rem(z + side, 2)
        for i in range(BLOCKS):
            to = pl.ds(LANES * i, LANES)
            at = pl.ds(pl.multiple_of((2 * i + parity) * LANES, LANES), LANES)
            for k, (ref, place) in enumerate(((t0, x), (t1, near), (t2, far))):
                pltpu.make_async_copy(ref.at[:, at], target.at[rows_of(place), to], sems.at[k, side]).start()
            inner = pl.ds(pl.multiple_of((2 * (i % half) + parity) * LANES, LANES), LANES)
            mine = (i // half) == core
            first = pltpu.make_async_copy(t3.at[:, inner], target.at[rows_of(across), to], sems.at[3, side])
            second = pltpu.make_async_copy(t4.at[:, inner], target.at[rows_of(across), to], sems.at[3, side])
            pl.when(mine)(first.start)
            pl.when(jnp.logical_not(mine))(second.start)
    widen(blocks_ref, wide_ref)
    back = ROWS - 1.0 - lax.broadcasted_iota(jnp.int32, (ROWS, LANES), 0).astype(f32)
    for m in range(MODES):
        into_ref[m] = jnp.exp(-a_ref[m : m + 1, :] * back)

    def wait(target, side):
        for k in range(4):
            rows = target.at[slice(ROWS * k, ROWS * (k + 1))]
            pltpu.make_async_copy(rows, rows, sems.at[k, side]).wait()

    wait(tokens_ref, 0)
    product_ref[...] = jnp.dot(tokens_ref[...], wide_ref[...], preferred_element_type=f32)
    wait(rest_ref, 1)


def project_rest(rest_ref, product_ref, blocks_ref, into_ref, streams_ref, state_ref, wide_ref, total_ref):
    widen(blocks_ref, wide_ref)
    total_ref[...] = product_ref[...] + jnp.dot(rest_ref[...], wide_ref[...], preferred_element_type=f32)
    low = lower_lanes((ROWS, LANES))
    for pair in range(NX // 2):
        lanes = slice(LANES * pair, LANES * (pair + 1))
        chunks = [slice(ROWS * k, ROWS * (k + 1)) for k in (2 * pair, 2 * pair + 1)]
        a, b = (total_ref[k, :LANES].astype(bf16).astype(f32) for k in chunks)
        turned_a, turned_b = swap_halves(a), swap_halves(b)
        gate_in, values = jnp.where(low, a, turned_b), jnp.where(low, turned_a, b)
        gate_out = jnp.where(low, total_ref[chunks[0], LANES:], total_ref[chunks[1], LANES:])
        signal = gate_in * values
        for k, value in enumerate((gate_in, values, gate_out)):
            streams_ref[k, :, lanes] = value.astype(bf16)
        for m in range(MODES):
            state = jnp.sum(signal * into_ref[m], axis=0, keepdims=True)
            for z in range(NZ):
                state_ref[z, pair * MODES + m : pair * MODES + m + 1, :] = state


def filter_inside(streams_ref, fwd_ref, inv_ref, long_ref):
    signal = streams_ref[0].astype(f32) * streams_ref[1].astype(f32)
    spectrum = dot_pair(fwd_ref[:, :ROWS], signal)
    response = jnp.concatenate([long_ref[...]] * 2, axis=1)
    return dot_pair(inv_ref[:ROWS, :], multiply_spectra(spectrum, response))


def filter_chunks(streams_ref, fwd_ref, inv_ref, long_ref, local_ref):
    local_ref[...] = filter_inside(streams_ref, fwd_ref, inv_ref, long_ref)


def carry_in(states_ref, a_ref, z):
    low = lower_lanes((MODES, LANES))
    rate = a_ref[...] * float(ROWS)
    decay = jnp.exp(-rate)
    decay_row = jnp.exp(-rate * float(NZ))
    decay_here = jnp.exp(-rate * z.astype(f32))
    before, whole = [], []
    for pair in range(NX // 2):
        upto = jnp.zeros((MODES, LANES), f32)
        total = jnp.zeros((MODES, LANES), f32)
        for k in range(NZ):
            step = states_ref[k, pair * MODES : (pair + 1) * MODES, :]
            upto = jnp.where(k < z, upto * decay + step, upto)
            total = total * decay + step
        before.append(upto)
        whole.append(total)
    swapped = [swap_halves(v) for v in whole]
    first = jnp.where(low, 0.0, swapped[0])
    second = jnp.where(
        low,
        swapped[0] + decay_row * whole[0],
        swapped[1] + decay_row * (whole[0] + decay_row * swapped[0]),
    )
    return [before[0] + decay_here * first, before[1] + decay_here * second]


def gate_rows(streams_ref, local, carries, out_ref):
    parts = []
    for pair in range(NX // 2):
        lanes = slice(LANES * pair, LANES * (pair + 1))
        value = local[:, lanes]
        for m in range(MODES):
            value = value + out_ref[m] * carries[pair][m : m + 1, :]
        parts.append((streams_ref[2, :, lanes].astype(f32) * value).astype(bf16).astype(f32))
    return parts


def finish(streams_ref, local_ref, arrived_ref, states_ref, a_ref, out_ref, fwd_ref, inv_ref, long_ref, short_ref, packed_ref):
    _, z, _ = positions()
    low = lower_lanes((ROWS, LANES))
    before = filter_inside(arrived_ref, fwd_ref, inv_ref, long_ref)
    own = gate_rows(streams_ref, local_ref[...], carry_in(states_ref, a_ref, z), out_ref)
    arrived = gate_rows(arrived_ref, before, carry_in(states_ref, a_ref, lax.rem(z + NZ - 1, NZ)), out_ref)
    turned = [swap_halves(v) for v in arrived]
    shifted = [jnp.where(low, 0.0, turned[0]), jnp.where(low, turned[0], turned[1])]
    previous = jnp.concatenate([jnp.where(z == 0, s, a) for s, a in zip(shifted, arrived)], axis=1)
    window = jnp.concatenate([previous, jnp.concatenate(own, axis=1)], axis=0).astype(bf16)
    response = jnp.concatenate([short_ref[...]] * 2, axis=1)
    mixed = dot_pair(inv_ref[ROWS:, :], multiply_spectra(dot_pair(fwd_ref[...], window), response))
    low_half = lower_lanes((HALF, LANES))
    for pair in range(2):
        top = mixed[:HALF, LANES * pair : LANES * (pair + 1)]
        bottom = mixed[HALF:, LANES * pair : LANES * (pair + 1)]
        packed_ref[2 * pair] = jnp.where(low_half, top, swap_halves(bottom)).astype(bf16)
        packed_ref[2 * pair + 1] = jnp.where(low_half, swap_halves(top), bottom).astype(bf16)


def unpack_rows(packed_ref, out_ref):
    low = lower_lanes((HALF, LANES))
    for pair in range(2):
        a, b = (packed_ref[2 * pair + h].astype(f32) for h in range(2))
        lanes = slice(LANES * pair, LANES * (pair + 1))
        out_ref[:HALF, lanes] = jnp.where(low, a, swap_halves(b)).astype(bf16)
        out_ref[HALF:, lanes] = jnp.where(low, swap_halves(a), b).astype(bf16)


def per_device(tokens, projections, decay_rates, residues, short_filter):
    sds = jax.ShapeDtypeStruct
    x = lax.axis_index("ctx") // NZ
    core = lax.axis_index("ch") % NC
    rows, features = tokens.shape
    width = features // NC
    wide = lax.axis_size("ch")

    def place(a, b, k):
        return (a % NX * NZ + b) * wide + k

    outward = [
        (place(a, b, k), place(a + 1 - 2 * (k % NC), b, k)) for a in range(NX) for b in range(NZ) for k in range(wide)
    ]
    swap = [(k, k ^ 1) for k in range(wide)]
    near = lax.ppermute(tokens, ("ctx", "ch"), outward)
    blocks = call(
        spread_weights,
        sds((BLOCKS, ROWS + HALF, LANES), bf16),
        projections,
        scratch=[pltpu.VMEM((NX, ROWS + HALF, LANES), bf16), pltpu.SemaphoreType.DMA((BLOCKS,))],
        out_specs=ANY,
    )
    blocks = lax.all_to_all(blocks, "ctx", 0, 0, tiled=True, axis_index_groups=parity_groups)
    across = [
        (place(a, b, k), place(a, (b + 1 - 2 * (k % NC)) % NZ, k)) for a in range(NX) for b in range(NZ) for k in range(wide)
    ]
    rest_blocks = lax.ppermute(blocks, ("ctx", "ch"), across)
    far = lax.ppermute(near, "ch", swap)
    half = lax.ppermute(lax.dynamic_slice_in_dim(near, core * width, width, 1), ("ctx", "ch"), outward)
    other = lax.ppermute(half, "ch", swap)

    rates = lax.dynamic_slice_in_dim(decay_rates, x * HALF, HALF, 0).T
    weights = lax.dynamic_slice_in_dim(residues, x * HALF, HALF, 0).T * jnp.sqrt(2.0 * rates)
    taps = lax.dynamic_slice_in_dim(short_filter, x * HALF, HALF, 0).T.astype(f32)
    rates, weights, taps = (jnp.concatenate([v, v], axis=1) for v in (rates, weights, taps))
    forward, inverse = jnp.asarray(real_transform()), jnp.asarray(inverse_transform())
    table = sds((MODES, ROWS, LANES), f32)
    spectrum = sds((SPAN, LANES), f32)
    out, long_spectrum, short_spectrum = call(build_tables, (table, spectrum, spectrum), rates, weights, taps, forward)
    half_depth = BLOCKS * ROWS
    product, rest, into = call(
        project_first,
        (sds((NX * rows, 2 * LANES), f32), sds((NX * rows, half_depth), bf16), table),
        tokens,
        near,
        far,
        half,
        other,
        blocks,
        rates,
        scratch=[
            pltpu.VMEM((NX * rows, half_depth), bf16),
            pltpu.VMEM((half_depth, 2 * LANES), bf16),
            pltpu.SemaphoreType.DMA((4, 2)),
        ],
        far=5,
    )
    streams, states = call(
        project_rest,
        (sds((3, ROWS, 2 * LANES), bf16), sds((NZ, 2 * MODES, LANES), f32)),
        rest,
        product,
        rest_blocks,
        into,
        scratch=[
            pltpu.VMEM((half_depth, 2 * LANES), bf16),
            pltpu.VMEM((NX * rows, 2 * LANES), f32),
        ],
    )
    states = lax.all_to_all(states, "ctx", 0, 0, tiled=True, axis_index_groups=z_groups)
    onward = [(a * NZ + b, a * NZ + (b + 1) % NZ) for a in range(NX) for b in range(NZ)]
    arrived = lax.ppermute(streams, "ctx", onward)
    local = call(filter_chunks, sds((ROWS, 2 * LANES), f32), streams, forward, inverse, long_spectrum)
    packed = call(
        finish,
        sds((NX, HALF, LANES), bf16),
        streams,
        local,
        arrived,
        states,
        rates,
        out,
        forward,
        inverse,
        long_spectrum,
        short_spectrum,
    )
    packed = lax.all_to_all(packed, "ctx", 0, 0, tiled=True, axis_index_groups=x_groups)
    return call(unpack_rows, sds((ROWS, 2 * LANES), bf16), packed)


def solution(mesh):
    in_specs = (P("ctx", None), P(None, "ctx", "ch"), P("ch", None), P("ch", None), P("ch", None))
    return jax.shard_map(per_device, mesh=mesh, in_specs=in_specs, out_specs=P("ctx", "ch"), check_vma=False)
```

```python
import math

import jax
import jax.numpy as jnp
import numpy as np
from jax import lax
from jax.experimental import pallas as pl
from jax.experimental.pallas import tpu as pltpu
from jax.sharding import PartitionSpec as P

f32, bf16 = jnp.float32, jnp.bfloat16

NX, NZ, NC = 4, 8, 2
ROWS = 128
LANES = 128
HALF = 64
SPAN = 2 * ROWS
MODES = 16
STEP = 8

parity_groups = [[x * NZ + z for x in range(NX) for z in range(p, NZ, 2)] for p in range(2)]


def real_transform():
    bins, places = np.arange(ROWS)[:, None], np.arange(SPAN)[None, :]
    angles = 2 * math.pi * (bins * places % SPAN) / SPAN
    real, imag = np.cos(angles), -np.sin(angles)
    imag[0] = np.where(np.arange(SPAN) % 2 == 0, 1.0, -1.0)
    return np.concatenate([real, imag]).astype(np.float32)


def inverse_transform():
    places, bins = np.arange(SPAN)[:, None], np.arange(ROWS)[None, :]
    angles = 2 * math.pi * (bins * places % SPAN) / SPAN
    real, imag = 2 * np.cos(angles), -2 * np.sin(angles)
    real[:, 0] = 1.0
    imag[:, 0] = np.where(np.arange(SPAN) % 2 == 0, 1.0, -1.0)
    return (np.concatenate([real, imag], axis=1) / SPAN).astype(np.float32)


def halves(v):
    high = v.astype(bf16)
    return high, (v - high.astype(f32)).astype(bf16)


def dot_pair(a, b):
    high, low = halves(a)
    if b.dtype == bf16:
        return dot(high, b) + dot(low, b)
    b_high, b_low = halves(b)
    return dot(high, b_high) + (dot(high, b_low) + dot(low, b_high))


def dot(a, b):
    return jnp.dot(a, b, preferred_element_type=f32)


def multiply_spectra(u, h):
    first = lax.broadcasted_iota(jnp.int32, (ROWS, u.shape[1]), 0) == 0
    ur, ui, hr, hi = u[:ROWS], u[ROWS:], h[:ROWS], h[ROWS:]
    both = ui * hi
    real = ur * hr - jnp.where(first, 0.0, both)
    imag = jnp.where(first, both, ur * hi + ui * hr)
    return jnp.concatenate([real, imag], axis=0)


def lower_lanes(shape):
    return lax.broadcasted_iota(jnp.int32, shape, len(shape) - 1) < HALF


def swap_halves(v):
    return pltpu.roll(v, HALF, v.ndim - 1)


VMEM, ANY = pl.BlockSpec(memory_space=pltpu.VMEM), pl.BlockSpec(memory_space=pltpu.HBM)


def call(body, outs, *args, scratch=(), flops=10**8, far=0, out_specs=None):
    return pl.pallas_call(
        body,
        out_shape=outs,
        in_specs=[ANY] * far + [VMEM] * (len(args) - far),
        out_specs=jax.tree.map(lambda _: VMEM, outs) if out_specs is None else out_specs,
        scratch_shapes=scratch,
        compiler_params=pltpu.CompilerParams(vmem_limit_bytes=16 << 20),
        cost_estimate=pl.CostEstimate(flops=flops, bytes_accessed=flops // 200, transcendentals=0),
    )(*args)


def spread_weights(w_ref, out_ref, block_ref, sems):
    low = lower_lanes((ROWS, LANES))
    low_half = lower_lanes((HALF, LANES))
    for x in range(NX):
        at = pl.ds(LANES * (x // 2), LANES)
        a, v, o = (w_ref[k, :, at].astype(f32) for k in range(3))
        if x % 2 == 0:
            both = jnp.where(low, a, swap_halves(v))
            packed = jnp.where(low_half, o[:HALF], swap_halves(o[HALF:]))
        else:
            both = jnp.where(low, swap_halves(a), v)
            packed = jnp.where(low_half, swap_halves(o[:HALF]), o[HALF:])
        both, packed = both.astype(bf16), packed.astype(bf16)
        block_ref[x, :ROWS] = both
        block_ref[x, ROWS:] = packed
        for z in range(NZ // 2):
            at = x * (NZ // 2) + z
            pltpu.make_async_copy(block_ref.at[x], out_ref.at[at], sems.at[at]).start()
    for x in range(NX):
        for z in range(NZ // 2):
            at = x * (NZ // 2) + z
            pltpu.make_async_copy(block_ref.at[x], out_ref.at[at], sems.at[at]).wait()


def build_tables(a_ref, w_ref, taps_ref, fwd_ref, near_ref, far_ref, long_ref, short_ref):
    channels = a_ref.shape[1]
    t = lax.broadcasted_iota(jnp.int32, (ROWS, channels), 0).astype(f32)
    step = lax.broadcasted_iota(jnp.int32, (STEP, channels), 0).astype(f32)
    block = lax.broadcasted_iota(jnp.int32, (ROWS // STEP, channels), 0).astype(f32) * float(STEP)
    impulse = jnp.zeros((ROWS, channels), f32)
    for m in range(MODES):
        rate, weight = a_ref[m : m + 1, :], w_ref[m : m + 1, :]
        near_ref[m] = weight * jnp.exp(-rate * (step + 1.0))
        far_ref[m] = jnp.exp(-rate * block)
        impulse = impulse + weight * jnp.exp(-rate * t)
    transform = fwd_ref[:, :ROWS]
    long_ref[...] = dot_pair(transform, impulse)
    short_ref[...] = dot_pair(transform, taps_ref[...])


def positions():
    ctx, ch = lax.axis_index("ctx"), lax.axis_index("ch")
    return lax.div(ctx, NZ), lax.rem(ctx, NZ), lax.rem(ch, NC)


BLOCKS = NX * NZ // 2


def widen(blocks_ref, wide_ref):
    low_half = lower_lanes((HALF, LANES))
    for block in range(BLOCKS):
        top, bottom = slice(ROWS * block, ROWS * block + HALF), slice(ROWS * block + HALF, ROWS * (block + 1))
        wide_ref[ROWS * block : ROWS * (block + 1), :LANES] = blocks_ref[block, :ROWS]
        packed = blocks_ref[block, ROWS:].astype(f32)
        turned = swap_halves(packed)
        wide_ref[top, LANES:] = jnp.where(low_half, packed, turned).astype(bf16)
        wide_ref[bottom, LANES:] = jnp.where(low_half, turned, packed).astype(bf16)


def project_first(t0, t1, t2, t3, t4, blocks_ref, a_ref, product_ref, rest_ref, into_ref, tokens_ref, wide_ref, sems):
    x, z, core = positions()
    near = lax.rem(x + NX - 1 + 2 * core, NX)
    far = lax.rem(x + NX + 1 - 2 * core, NX)
    across = lax.rem(x + 2, NX)
    half = BLOCKS // NC

    def rows_of(k):
        return pl.ds(pl.multiple_of(k * ROWS, ROWS), ROWS)

    for side, target in ((0, tokens_ref), (1, rest_ref)):
        parity = lax.rem(z + side, 2)
        for i in range(BLOCKS):
            to = pl.ds(LANES * i, LANES)
            at = pl.ds(pl.multiple_of((2 * i + parity) * LANES, LANES), LANES)
            for k, (ref, place) in enumerate(((t0, x), (t1, near), (t2, far))):
                pltpu.make_async_copy(ref.at[:, at], target.at[rows_of(place), to], sems.at[k, side]).start()
            inner = pl.ds(pl.multiple_of((2 * (i % half) + parity) * LANES, LANES), LANES)
            mine = (i // half) == core
            first = pltpu.make_async_copy(t3.at[:, inner], target.at[rows_of(across), to], sems.at[3, side])
            second = pltpu.make_async_copy(t4.at[:, inner], target.at[rows_of(across), to], sems.at[3, side])
            pl.when(mine)(first.start)
            pl.when(jnp.logical_not(mine))(second.start)
    widen(blocks_ref, wide_ref)
    back = ROWS - 1.0 - lax.broadcasted_iota(jnp.int32, (ROWS, LANES), 0).astype(f32)
    for m in range(MODES):
        into_ref[m] = jnp.exp(-a_ref[m : m + 1, :] * back)

    def wait(target, side):
        for k in range(4):
            rows = target.at[slice(ROWS * k, ROWS * (k + 1))]
            pltpu.make_async_copy(rows, rows, sems.at[k, side]).wait()

    wait(tokens_ref, 0)
    product_ref[...] = jnp.dot(tokens_ref[...], wide_ref[...], preferred_element_type=f32)
    wait(rest_ref, 1)


def project_rest(rest_ref, product_ref, blocks_ref, into_ref, a_ref, streams_ref, carry_ref, wide_ref, total_ref, state_ref):
    widen(blocks_ref, wide_ref)
    total_ref[...] = product_ref[...] + jnp.dot(rest_ref[...], wide_ref[...], preferred_element_type=f32)
    low = lower_lanes((ROWS, LANES))
    for pair in range(NX // 2):
        lanes = slice(LANES * pair, LANES * (pair + 1))
        chunks = [slice(ROWS * k, ROWS * (k + 1)) for k in (2 * pair, 2 * pair + 1)]
        a, b = (total_ref[k, :LANES].astype(bf16).astype(f32) for k in chunks)
        turned_a, turned_b = swap_halves(a), swap_halves(b)
        gate_in, values = jnp.where(low, a, turned_b), jnp.where(low, turned_a, b)
        gate_out = jnp.where(low, total_ref[chunks[0], LANES:], total_ref[chunks[1], LANES:])
        signal = gate_in * values
        for k, value in enumerate((gate_in, values, gate_out)):
            streams_ref[k, :, lanes] = value.astype(bf16)
        for m in range(MODES):
            state_ref[pair, m : m + 1, :] = jnp.sum(signal * into_ref[m], axis=0, keepdims=True)
    share_states(state_ref, a_ref, carry_ref)


def share_states(state_ref, a_ref, carry_ref):
    _, here, _ = positions()
    here = here.astype(f32)
    rate = a_ref[...] * float(ROWS)
    low = lower_lanes((MODES, LANES))
    nothing = jnp.zeros((MODES, LANES), f32)
    row = jnp.exp(-rate * float(NZ))
    states, earlier = [], [nothing]
    for x in range(NX):
        state = state_ref[x // 2]
        turned = swap_halves(state)
        states.append(jnp.where(low, state, turned) if x % 2 == 0 else jnp.where(low, turned, state))
        earlier.append(states[-1] + row * earlier[-1])
    same, across = [], []
    for z in range(NZ):
        after = z - 1.0 - here
        same.append(jnp.where(after >= 0.0, jnp.exp(-rate * jnp.maximum(after, 0.0)), 0.0))
        across.append(jnp.exp(-rate * (z + NZ - 1.0 - here)))
    last = nothing
    for x in range(NX):
        for z in range(NZ):
            now = same[z] * states[x] + across[z] * earlier[x]
            carry_ref[x * NZ + z] = jnp.where(low, now, last)
            last = now


def pack(streams_ref, arrived_ref, p0, p1, p2, p3, chunk_ref):
    x, z, _ = positions()
    low = lower_lanes((HALF, LANES))
    chunk_ref[NX] = jnp.zeros(chunk_ref.shape[1:], bf16)
    for first, ref in ((0, streams_ref), (NX + 1, arrived_ref)):
        for k in range(3):
            for pair in range(NX // 2):
                lanes = slice(LANES * pair, LANES * (pair + 1))
                top, bottom = ref[k, :HALF, lanes].astype(f32), ref[k, HALF:, lanes].astype(f32)
                chunk_ref[first + 2 * pair, k] = jnp.where(low, top, swap_halves(bottom)).astype(bf16)
                chunk_ref[first + 2 * pair + 1, k] = jnp.where(low, swap_halves(top), bottom).astype(bf16)
    back = jnp.where(z == 0, 1, 0)
    for k, ref in enumerate((p0, p1, p2, p3)):
        chunk = lax.rem(x + k, NX)
        ref[0] = chunk_ref[chunk]
        ref[1] = chunk_ref[NX + 1 + chunk - back]


def finish(p0, p1, p2, p3, carry_ref, near_ref, far_ref, fwd_ref, inv_ref, long_ref, short_ref, out_ref, part_ref):
    x, _, _ = positions()
    for k, ref in enumerate((p0, p1, p2, p3)):
        part_ref[lax.rem(x + NX - k, NX)] = ref[...]
    low, low_modes = lower_lanes((HALF, LANES)), lower_lanes((MODES, LANES))

    def whole(side, k):
        columns = []
        for pair in range(NX // 2):
            a, b = (part_ref[2 * pair + h, side, k].astype(f32) for h in range(2))
            top, bottom = jnp.where(low, a, swap_halves(b)), jnp.where(low, swap_halves(a), b)
            columns.append(jnp.concatenate([top, bottom], axis=0))
        return jnp.concatenate(columns, axis=1)

    signal = jnp.concatenate([whole(side, 0) * whole(side, 1) for side in range(2)], axis=1)
    response = jnp.concatenate([long_ref[...]] * 2, axis=1)
    local = dot_pair(inv_ref[:ROWS, :], multiply_spectra(dot_pair(fwd_ref[:, :ROWS], signal), response))
    carries = []
    for group in range(NX):
        total = carry_ref[group * NZ]
        for z in range(1, NZ):
            total = total + carry_ref[group * NZ + z]
        carries.append(total)
    gated = []
    for side in range(2):
        columns = []
        for pair in range(NX // 2):
            a, b = carries[2 * pair], carries[2 * pair + 1]
            if side == 0:
                carry = jnp.where(low_modes, a, swap_halves(b))
            else:
                carry = jnp.where(low_modes, swap_halves(a), b)
            lanes = slice(LANES * pair, LANES * (pair + 1))
            heads = [near_ref[m, :, lanes] * carry[m : m + 1, :] for m in range(MODES)]
            blocks = []
            for i in range(ROWS // STEP):
                value = local[STEP * i : STEP * (i + 1), 2 * LANES * side + LANES * pair : 2 * LANES * side + LANES * (pair + 1)]
                for m in range(MODES):
                    value = value + heads[m] * far_ref[m, i : i + 1, lanes]
                blocks.append(value)
            columns.append(jnp.concatenate(blocks, axis=0))
        gated.append((whole(side, 2) * jnp.concatenate(columns, axis=1)).astype(bf16))
    window = jnp.concatenate([gated[1], gated[0]], axis=0)
    mixed = dot_pair(inv_ref[ROWS:, :], multiply_spectra(dot_pair(fwd_ref[...], window), short_ref[...]))
    out_ref[...] = mixed.astype(bf16)


def per_device(tokens, projections, decay_rates, residues, short_filter):
    sds = jax.ShapeDtypeStruct
    x = lax.axis_index("ctx") // NZ
    core = lax.axis_index("ch") % NC
    rows, features = tokens.shape
    width = features // NC
    count = NX * NZ
    wide = lax.axis_size("ch")

    def place(a, b, k):
        return (a % NX * NZ + b) * wide + k

    outward = [
        (place(a, b, k), place(a + 1 - 2 * (k % NC), b, k)) for a in range(NX) for b in range(NZ) for k in range(wide)
    ]
    swap = [(k, k ^ 1) for k in range(wide)]
    near = lax.ppermute(tokens, ("ctx", "ch"), outward)
    blocks = call(
        spread_weights,
        sds((BLOCKS, ROWS + HALF, LANES), bf16),
        projections,
        scratch=[pltpu.VMEM((NX, ROWS + HALF, LANES), bf16), pltpu.SemaphoreType.DMA((BLOCKS,))],
        out_specs=ANY,
    )
    blocks = lax.all_to_all(blocks, "ctx", 0, 0, tiled=True, axis_index_groups=parity_groups)
    across = [
        (place(a, b, k), place(a, (b + 1 - 2 * (k % NC)) % NZ, k)) for a in range(NX) for b in range(NZ) for k in range(wide)
    ]
    rest_blocks = lax.ppermute(blocks, ("ctx", "ch"), across)
    far = lax.ppermute(near, "ch", swap)
    half = lax.ppermute(lax.dynamic_slice_in_dim(near, core * width, width, 1), ("ctx", "ch"), outward)
    other = lax.ppermute(half, "ch", swap)

    rates = lax.dynamic_slice_in_dim(decay_rates, x * HALF, HALF, 0).T
    rates = jnp.concatenate([rates, rates], axis=1)
    all_rates = decay_rates.T
    all_weights = residues.T * jnp.sqrt(2.0 * all_rates)
    taps = short_filter.T.astype(f32)
    channels = all_rates.shape[1]
    forward, inverse = jnp.asarray(real_transform()), jnp.asarray(inverse_transform())
    table = sds((MODES, ROWS, LANES), f32)
    spectrum = sds((SPAN, channels), f32)
    steps, jumps, long_spectrum, short_spectrum = call(
        build_tables,
        (sds((MODES, STEP, channels), f32), sds((MODES, ROWS // STEP, channels), f32), spectrum, spectrum),
        all_rates,
        all_weights,
        taps,
        forward,
    )
    half_depth = BLOCKS * ROWS
    product, rest, into = call(
        project_first,
        (sds((NX * rows, 2 * LANES), f32), sds((NX * rows, half_depth), bf16), table),
        tokens,
        near,
        far,
        half,
        other,
        blocks,
        rates,
        scratch=[
            pltpu.VMEM((NX * rows, half_depth), bf16),
            pltpu.VMEM((half_depth, 2 * LANES), bf16),
            pltpu.SemaphoreType.DMA((4, 2)),
        ],
        far=5,
    )
    streams, carries = call(
        project_rest,
        (sds((3, ROWS, 2 * LANES), bf16), sds((count, MODES, LANES), f32)),
        rest,
        product,
        rest_blocks,
        into,
        rates,
        scratch=[
            pltpu.VMEM((half_depth, 2 * LANES), bf16),
            pltpu.VMEM((NX * rows, 2 * LANES), f32),
            pltpu.VMEM((NX // 2, MODES, LANES), f32),
        ],
    )
    onward = [(a * NZ + b, a * NZ + (b + 1) % NZ) for a in range(NX) for b in range(NZ)]
    arrived = lax.ppermute(streams, "ctx", onward)
    carries = lax.all_to_all(carries, "ctx", 0, 0, tiled=True)
    piece = sds((2, 3, HALF, LANES), bf16)
    pieces = call(pack, (piece,) * NX, streams, arrived, scratch=[pltpu.VMEM((2 * NX + 1, 3, HALF, LANES), bf16)])
    moved = [pieces[0]] + [None] * (NX - 1)
    for k in (2, 1, 3):
        turn = [(a * NZ + b, (a + k) % NX * NZ + b) for a in range(NX) for b in range(NZ)]
        moved[k] = lax.ppermute(pieces[k], "ctx", turn)
    return call(
        finish,
        sds((ROWS, 2 * LANES), bf16),
        *moved,
        carries,
        steps,
        jumps,
        forward,
        inverse,
        long_spectrum,
        short_spectrum,
        scratch=[pltpu.VMEM((NX, 2, 3, HALF, LANES), bf16)],
    )


def solution(mesh):
    in_specs = (P("ctx", None), P(None, "ctx", "ch"), P("ch", None), P("ch", None), P("ch", None))
    return jax.shard_map(per_device, mesh=mesh, in_specs=in_specs, out_specs=P("ctx", "ch"), check_vma=False)
```

```python
import math

import jax
import jax.numpy as jnp
import numpy as np
from jax import lax
from jax.experimental import pallas as pl
from jax.experimental.pallas import tpu as pltpu
from jax.sharding import PartitionSpec as P

f32, bf16 = jnp.float32, jnp.bfloat16

NX, NZ, NC = 4, 8, 2
ROWS = 128
LANES = 128
HALF = 64
SPAN = 2 * ROWS
MODES = 16

parity_groups = [[x * NZ + z for x in range(NX) for z in range(p, NZ, 2)] for p in range(2)]
x_groups = [[x * NZ + z for x in range(NX)] for z in range(NZ)]
z_groups = [[x * NZ + z for z in range(NZ)] for x in range(NX)]


def real_transform():
    bins, places = np.arange(ROWS)[:, None], np.arange(SPAN)[None, :]
    angles = 2 * math.pi * (bins * places % SPAN) / SPAN
    real, imag = np.cos(angles), -np.sin(angles)
    imag[0] = np.where(np.arange(SPAN) % 2 == 0, 1.0, -1.0)
    return np.concatenate([real, imag]).astype(np.float32)


def inverse_transform():
    places, bins = np.arange(SPAN)[:, None], np.arange(ROWS)[None, :]
    angles = 2 * math.pi * (bins * places % SPAN) / SPAN
    real, imag = 2 * np.cos(angles), -2 * np.sin(angles)
    real[:, 0] = 1.0
    imag[:, 0] = np.where(np.arange(SPAN) % 2 == 0, 1.0, -1.0)
    return (np.concatenate([real, imag], axis=1) / SPAN).astype(np.float32)


def halves(v):
    high = v.astype(bf16)
    return high, (v - high.astype(f32)).astype(bf16)


def dot_pair(a, b):
    high, low = halves(a)
    if b.dtype == bf16:
        return dot(high, b) + dot(low, b)
    b_high, b_low = halves(b)
    return dot(high, b_high) + (dot(high, b_low) + dot(low, b_high))


def dot(a, b):
    return jnp.dot(a, b, preferred_element_type=f32)


def multiply_spectra(u, h):
    first = lax.broadcasted_iota(jnp.int32, (ROWS, u.shape[1]), 0) == 0
    ur, ui, hr, hi = u[:ROWS], u[ROWS:], h[:ROWS], h[ROWS:]
    both = ui * hi
    real = ur * hr - jnp.where(first, 0.0, both)
    imag = jnp.where(first, both, ur * hi + ui * hr)
    return jnp.concatenate([real, imag], axis=0)


def lower_lanes(shape):
    return lax.broadcasted_iota(jnp.int32, shape, len(shape) - 1) < HALF


def swap_halves(v):
    return pltpu.roll(v, HALF, v.ndim - 1)


VMEM, ANY = pl.BlockSpec(memory_space=pltpu.VMEM), pl.BlockSpec(memory_space=pltpu.HBM)


def call(body, outs, *args, scratch=(), flops=10**8, far=0, out_specs=None):
    return pl.pallas_call(
        body,
        out_shape=outs,
        in_specs=[ANY] * far + [VMEM] * (len(args) - far),
        out_specs=jax.tree.map(lambda _: VMEM, outs) if out_specs is None else out_specs,
        scratch_shapes=scratch,
        compiler_params=pltpu.CompilerParams(vmem_limit_bytes=16 << 20),
        cost_estimate=pl.CostEstimate(flops=flops, bytes_accessed=flops // 200, transcendentals=0),
    )(*args)


def spread_weights(w_ref, out_ref, block_ref, sems):
    low = lower_lanes((ROWS, LANES))
    low_half = lower_lanes((HALF, LANES))
    for x in range(NX):
        at = pl.ds(LANES * (x // 2), LANES)
        a, v, o = (w_ref[k, :, at].astype(f32) for k in range(3))
        if x % 2 == 0:
            both = jnp.where(low, a, swap_halves(v))
            packed = jnp.where(low_half, o[:HALF], swap_halves(o[HALF:]))
        else:
            both = jnp.where(low, swap_halves(a), v)
            packed = jnp.where(low_half, swap_halves(o[:HALF]), o[HALF:])
        both, packed = both.astype(bf16), packed.astype(bf16)
        block_ref[x, :ROWS] = both
        block_ref[x, ROWS:] = packed
        for z in range(NZ // 2):
            at = x * (NZ // 2) + z
            pltpu.make_async_copy(block_ref.at[x], out_ref.at[at], sems.at[at]).start()
    for x in range(NX):
        for z in range(NZ // 2):
            at = x * (NZ // 2) + z
            pltpu.make_async_copy(block_ref.at[x], out_ref.at[at], sems.at[at]).wait()


def own_channels(ref):
    x, _, _ = positions()
    found = ref[:, pl.ds(pl.multiple_of(lax.div(x, 2) * LANES, LANES), LANES)]
    upper = lax.rem(x, 2) == 1
    low = lower_lanes(found.shape)
    turned = swap_halves(found)
    return jnp.where(low, jnp.where(upper, turned, found), jnp.where(upper, found, turned))


def build_tables(rates_ref, residues_ref, taps_ref, fwd_ref, out_ref, long_ref, short_ref):
    x, _, _ = positions()
    rates = own_channels(rates_ref)
    weights = own_channels(residues_ref) * jnp.sqrt(2.0 * rates)
    t = lax.broadcasted_iota(jnp.int32, (ROWS, LANES), 0).astype(f32)
    impulse = jnp.zeros((ROWS, LANES), f32)
    for m in range(MODES):
        rate, weight = rates[m : m + 1, :], weights[m : m + 1, :]
        out_ref[m] = weight * jnp.exp(-rate * (t + 1.0))
        impulse = impulse + weight * jnp.exp(-rate * t)
    own = taps_ref[pl.ds(pl.multiple_of(x * HALF, HALF), HALF), :].astype(f32)
    taps = jnp.concatenate([own, own], axis=0).T
    transform = fwd_ref[:, :ROWS]
    long_ref[...] = dot_pair(transform, impulse)
    short_ref[...] = dot_pair(transform, taps)


def positions():
    ctx, ch = lax.axis_index("ctx"), lax.axis_index("ch")
    return lax.div(ctx, NZ), lax.rem(ctx, NZ), lax.rem(ch, NC)


BLOCKS = NX * NZ // 2


def widen(blocks_ref, wide_ref):
    low_half = lower_lanes((HALF, LANES))
    for block in range(BLOCKS):
        top, bottom = slice(ROWS * block, ROWS * block + HALF), slice(ROWS * block + HALF, ROWS * (block + 1))
        wide_ref[ROWS * block : ROWS * (block + 1), :LANES] = blocks_ref[block, :ROWS]
        packed = blocks_ref[block, ROWS:].astype(f32)
        turned = swap_halves(packed)
        wide_ref[top, LANES:] = jnp.where(low_half, packed, turned).astype(bf16)
        wide_ref[bottom, LANES:] = jnp.where(low_half, turned, packed).astype(bf16)


def project_first(t0, t1, t2, t3, t4, blocks_ref, a_ref, product_ref, rest_ref, into_ref, tokens_ref, wide_ref, sems):
    x, z, core = positions()
    near = lax.rem(x + NX - 1 + 2 * core, NX)
    far = lax.rem(x + NX + 1 - 2 * core, NX)
    across = lax.rem(x + 2, NX)
    half = BLOCKS // NC

    def rows_of(k):
        return pl.ds(pl.multiple_of(k * ROWS, ROWS), ROWS)

    for side, target in ((0, tokens_ref), (1, rest_ref)):
        parity = lax.rem(z + side, 2)
        for i in range(BLOCKS):
            to = pl.ds(LANES * i, LANES)
            at = pl.ds(pl.multiple_of((2 * i + parity) * LANES, LANES), LANES)
            for k, (ref, place) in enumerate(((t0, x), (t1, near), (t2, far))):
                pltpu.make_async_copy(ref.at[:, at], target.at[rows_of(place), to], sems.at[k, side]).start()
            inner = pl.ds(pl.multiple_of((2 * (i % half) + parity) * LANES, LANES), LANES)
            mine = (i // half) == core
            first = pltpu.make_async_copy(t3.at[:, inner], target.at[rows_of(across), to], sems.at[3, side])
            second = pltpu.make_async_copy(t4.at[:, inner], target.at[rows_of(across), to], sems.at[3, side])
            pl.when(mine)(first.start)
            pl.when(jnp.logical_not(mine))(second.start)
    widen(blocks_ref, wide_ref)
    back = ROWS - 1.0 - lax.broadcasted_iota(jnp.int32, (ROWS, LANES), 0).astype(f32)
    rates = own_channels(a_ref)
    for m in range(MODES):
        into_ref[m] = jnp.exp(-rates[m : m + 1, :] * back)

    def wait(target, side):
        for k in range(4):
            rows = target.at[slice(ROWS * k, ROWS * (k + 1))]
            pltpu.make_async_copy(rows, rows, sems.at[k, side]).wait()

    wait(tokens_ref, 0)
    product_ref[...] = jnp.dot(tokens_ref[...], wide_ref[...], preferred_element_type=f32)
    wait(rest_ref, 1)


def project_rest(blocks_ref, rest_ref, product_ref, into_ref, signal_ref, streams_ref, state_ref, wide_ref, total_ref):
    widen(blocks_ref, wide_ref)
    total_ref[...] = product_ref[...] + jnp.dot(rest_ref[...], wide_ref[...], preferred_element_type=f32)
    low = lower_lanes((ROWS, LANES))
    for pair in range(NX // 2):
        lanes = slice(LANES * pair, LANES * (pair + 1))
        chunks = [slice(ROWS * k, ROWS * (k + 1)) for k in (2 * pair, 2 * pair + 1)]
        a, b = (total_ref[k, :LANES].astype(bf16).astype(f32) for k in chunks)
        turned_a, turned_b = swap_halves(a), swap_halves(b)
        gate_in, values = jnp.where(low, a, turned_b), jnp.where(low, turned_a, b)
        gate_out = jnp.where(low, total_ref[chunks[0], LANES:], total_ref[chunks[1], LANES:])
        signal = gate_in * values
        signal_ref[:, lanes] = signal
        for k, value in enumerate((signal, gate_out)):
            streams_ref[k, :, lanes] = value.astype(bf16)
        for m in range(MODES):
            state = jnp.sum(signal * into_ref[m], axis=0, keepdims=True)
            for z in range(NZ):
                state_ref[z, pair * MODES + m : pair * MODES + m + 1, :] = state


def filter_inside(signal, fwd_ref, inv_ref, long_ref):
    spectrum = dot_pair(fwd_ref[:, :ROWS], signal)
    response = jnp.concatenate([long_ref[...]] * 2, axis=1)
    return dot_pair(inv_ref[:ROWS, :], multiply_spectra(spectrum, response))


def filter_chunks(signal_ref, fwd_ref, inv_ref, long_ref, local_ref):
    local_ref[...] = filter_inside(signal_ref[...], fwd_ref, inv_ref, long_ref)


def carry_in(states_ref, a_ref, z):
    low = lower_lanes((MODES, LANES))
    rate = own_channels(a_ref) * float(ROWS)
    decay = jnp.exp(-rate)
    decay_row = jnp.exp(-rate * float(NZ))
    decay_here = jnp.exp(-rate * z.astype(f32))
    before, whole = [], []
    for pair in range(NX // 2):
        upto = jnp.zeros((MODES, LANES), f32)
        total = jnp.zeros((MODES, LANES), f32)
        for k in range(NZ):
            step = states_ref[k, pair * MODES : (pair + 1) * MODES, :]
            upto = jnp.where(k < z, upto * decay + step, upto)
            total = total * decay + step
        before.append(upto)
        whole.append(total)
    swapped = [swap_halves(v) for v in whole]
    first = jnp.where(low, 0.0, swapped[0])
    second = jnp.where(
        low,
        swapped[0] + decay_row * whole[0],
        swapped[1] + decay_row * (whole[0] + decay_row * swapped[0]),
    )
    return [before[0] + decay_here * first, before[1] + decay_here * second]


def gate_rows(streams_ref, local, carries, out_ref):
    parts = []
    for pair in range(NX // 2):
        lanes = slice(LANES * pair, LANES * (pair + 1))
        value = local[:, lanes]
        for m in range(MODES):
            value = value + out_ref[m] * carries[pair][m : m + 1, :]
        parts.append((streams_ref[1, :, lanes].astype(f32) * value).astype(bf16).astype(f32))
    return parts


def finish(streams_ref, local_ref, arrived_ref, states_ref, a_ref, out_ref, fwd_ref, inv_ref, long_ref, short_ref, packed_ref):
    _, z, _ = positions()
    low = lower_lanes((ROWS, LANES))
    before = filter_inside(arrived_ref[0], fwd_ref, inv_ref, long_ref)
    own = gate_rows(streams_ref, local_ref[...], carry_in(states_ref, a_ref, z), out_ref)
    arrived = gate_rows(arrived_ref, before, carry_in(states_ref, a_ref, lax.rem(z + NZ - 1, NZ)), out_ref)
    turned = [swap_halves(v) for v in arrived]
    shifted = [jnp.where(low, 0.0, turned[0]), jnp.where(low, turned[0], turned[1])]
    previous = jnp.concatenate([jnp.where(z == 0, s, a) for s, a in zip(shifted, arrived)], axis=1)
    window = jnp.concatenate([previous, jnp.concatenate(own, axis=1)], axis=0).astype(bf16)
    response = jnp.concatenate([short_ref[...]] * 2, axis=1)
    mixed = dot_pair(inv_ref[ROWS:, :], multiply_spectra(dot_pair(fwd_ref[...], window), response))
    low_half = lower_lanes((HALF, LANES))
    for pair in range(2):
        top = mixed[:HALF, LANES * pair : LANES * (pair + 1)]
        bottom = mixed[HALF:, LANES * pair : LANES * (pair + 1)]
        packed_ref[2 * pair] = jnp.where(low_half, top, swap_halves(bottom)).astype(bf16)
        packed_ref[2 * pair + 1] = jnp.where(low_half, swap_halves(top), bottom).astype(bf16)


def unpack_rows(packed_ref, out_ref):
    low = lower_lanes((HALF, LANES))
    for pair in range(2):
        a, b = (packed_ref[2 * pair + h].astype(f32) for h in range(2))
        lanes = slice(LANES * pair, LANES * (pair + 1))
        out_ref[:HALF, lanes] = jnp.where(low, a, swap_halves(b)).astype(bf16)
        out_ref[HALF:, lanes] = jnp.where(low, swap_halves(a), b).astype(bf16)


def per_device(tokens, projections, decay_rates, residues, short_filter):
    sds = jax.ShapeDtypeStruct
    core = lax.axis_index("ch") % NC
    rows, features = tokens.shape
    width = features // NC
    wide = lax.axis_size("ch")

    def place(a, b, k):
        return (a % NX * NZ + b) * wide + k

    outward = [
        (place(a, b, k), place(a + 1 - 2 * (k % NC), b, k)) for a in range(NX) for b in range(NZ) for k in range(wide)
    ]
    swap = [(k, k ^ 1) for k in range(wide)]
    near = lax.ppermute(tokens, ("ctx", "ch"), outward)
    blocks = call(
        spread_weights,
        sds((BLOCKS, ROWS + HALF, LANES), bf16),
        projections,
        scratch=[pltpu.VMEM((NX, ROWS + HALF, LANES), bf16), pltpu.SemaphoreType.DMA((BLOCKS,))],
        out_specs=ANY,
    )
    blocks = lax.all_to_all(blocks, "ctx", 0, 0, tiled=True, axis_index_groups=parity_groups)
    across = [
        (place(a, b, k), place(a, (b + 1 - 2 * (k % NC)) % NZ, k)) for a in range(NX) for b in range(NZ) for k in range(wide)
    ]
    rest_blocks = lax.ppermute(blocks, ("ctx", "ch"), across)
    far = lax.ppermute(near, "ch", swap)
    half = lax.ppermute(lax.dynamic_slice_in_dim(near, core * width, width, 1), ("ctx", "ch"), outward)
    other = lax.ppermute(half, "ch", swap)

    rates = decay_rates.T
    forward, inverse = jnp.asarray(real_transform()), jnp.asarray(inverse_transform())
    table = sds((MODES, ROWS, LANES), f32)
    spectrum = sds((SPAN, LANES), f32)
    out, long_spectrum, short_spectrum = call(
        build_tables, (table, spectrum, spectrum), rates, residues.T, short_filter, forward
    )
    half_depth = BLOCKS * ROWS
    product, rest, into = call(
        project_first,
        (sds((NX * rows, 2 * LANES), f32), sds((NX * rows, half_depth), bf16), table),
        tokens,
        near,
        far,
        half,
        other,
        blocks,
        rates,
        scratch=[
            pltpu.VMEM((NX * rows, half_depth), bf16),
            pltpu.VMEM((half_depth, 2 * LANES), bf16),
            pltpu.SemaphoreType.DMA((4, 2)),
        ],
        far=5,
    )
    signal, streams, states = call(
        project_rest,
        (sds((ROWS, 2 * LANES), f32), sds((2, ROWS, 2 * LANES), bf16), sds((NZ, 2 * MODES, LANES), f32)),
        rest_blocks,
        rest,
        product,
        into,
        scratch=[
            pltpu.VMEM((half_depth, 2 * LANES), bf16),
            pltpu.VMEM((NX * rows, 2 * LANES), f32),
        ],
    )
    states = lax.all_to_all(states, "ctx", 0, 0, tiled=True, axis_index_groups=z_groups)
    onward = [(a * NZ + b, a * NZ + (b + 1) % NZ) for a in range(NX) for b in range(NZ)]
    arrived = lax.ppermute(streams, "ctx", onward)
    local = call(filter_chunks, sds((ROWS, 2 * LANES), f32), signal, forward, inverse, long_spectrum)
    packed = call(
        finish,
        sds((NX, HALF, LANES), bf16),
        streams,
        local,
        arrived,
        states,
        rates,
        out,
        forward,
        inverse,
        long_spectrum,
        short_spectrum,
    )
    packed = lax.all_to_all(packed, "ctx", 0, 0, tiled=True, axis_index_groups=x_groups)
    return call(unpack_rows, sds((ROWS, 2 * LANES), bf16), packed)


def solution(mesh):
    in_specs = (P("ctx", None), P(None, "ctx", "ch"), P("ch", None), P("ch", None), P("ch", None))
    return jax.shard_map(per_device, mesh=mesh, in_specs=in_specs, out_specs=P("ctx", "ch"), check_vma=False)
```

```python
import math

import jax
import jax.numpy as jnp
import numpy as np
from jax import lax
from jax.experimental import pallas as pl
from jax.experimental.pallas import tpu as pltpu
from jax.sharding import PartitionSpec as P

f32, bf16 = jnp.float32, jnp.bfloat16

NX, NZ, NC = 4, 8, 2
ROWS = 128
LANES = 128
HALF = 64
SPAN = 2 * ROWS
MODES = 16

parity_groups = [[x * NZ + z for x in range(NX) for z in range(p, NZ, 2)] for p in range(2)]
x_groups = [[x * NZ + z for x in range(NX)] for z in range(NZ)]
z_groups = [[x * NZ + z for z in range(NZ)] for x in range(NX)]


def real_transform():
    bins, places = np.arange(ROWS)[:, None], np.arange(SPAN)[None, :]
    angles = 2 * math.pi * (bins * places % SPAN) / SPAN
    real, imag = np.cos(angles), -np.sin(angles)
    imag[0] = np.where(np.arange(SPAN) % 2 == 0, 1.0, -1.0)
    return np.concatenate([real, imag]).astype(np.float32)


def inverse_transform():
    places, bins = np.arange(SPAN)[:, None], np.arange(ROWS)[None, :]
    angles = 2 * math.pi * (bins * places % SPAN) / SPAN
    real, imag = 2 * np.cos(angles), -2 * np.sin(angles)
    real[:, 0] = 1.0
    imag[:, 0] = np.where(np.arange(SPAN) % 2 == 0, 1.0, -1.0)
    return (np.concatenate([real, imag], axis=1) / SPAN).astype(np.float32)


def halves(v):
    high = v.astype(bf16)
    return high, (v - high.astype(f32)).astype(bf16)


def dot_pair(a, b):
    high, low = halves(a)
    if b.dtype == bf16:
        return dot(high, b) + dot(low, b)
    b_high, b_low = halves(b)
    return dot(high, b_high) + (dot(high, b_low) + dot(low, b_high))


def dot(a, b):
    return jnp.dot(a, b, preferred_element_type=f32)


def multiply_spectra(u, h):
    first = lax.broadcasted_iota(jnp.int32, (ROWS, u.shape[1]), 0) == 0
    ur, ui, hr, hi = u[:ROWS], u[ROWS:], h[:ROWS], h[ROWS:]
    both = ui * hi
    real = ur * hr - jnp.where(first, 0.0, both)
    imag = jnp.where(first, both, ur * hi + ui * hr)
    return jnp.concatenate([real, imag], axis=0)


def lower_lanes(shape):
    return lax.broadcasted_iota(jnp.int32, shape, len(shape) - 1) < HALF


def swap_halves(v):
    return pltpu.roll(v, HALF, v.ndim - 1)


VMEM, ANY = pl.BlockSpec(memory_space=pltpu.VMEM), pl.BlockSpec(memory_space=pltpu.HBM)


def call(body, outs, *args, scratch=(), flops=10**8, far=0, out_specs=None):
    return pl.pallas_call(
        body,
        out_shape=outs,
        in_specs=[ANY] * far + [VMEM] * (len(args) - far),
        out_specs=jax.tree.map(lambda _: VMEM, outs) if out_specs is None else out_specs,
        scratch_shapes=scratch,
        compiler_params=pltpu.CompilerParams(vmem_limit_bytes=16 << 20),
        cost_estimate=pl.CostEstimate(flops=flops, bytes_accessed=flops // 200, transcendentals=0),
    )(*args)


def spread_weights(w_ref, out_ref):
    low = lower_lanes((ROWS, LANES))
    low_half = lower_lanes((HALF, LANES))
    for x in range(NX):
        at = pl.ds(LANES * (x // 2), LANES)
        a, v, o = (w_ref[k, :, at].astype(f32) for k in range(3))
        if x % 2 == 0:
            both = jnp.where(low, a, swap_halves(v))
            packed = jnp.where(low_half, o[:HALF], swap_halves(o[HALF:]))
        else:
            both = jnp.where(low, swap_halves(a), v)
            packed = jnp.where(low_half, swap_halves(o[:HALF]), o[HALF:])
        both, packed = both.astype(bf16), packed.astype(bf16)
        for z in range(NZ // 2):
            at = x * (NZ // 2) + z
            out_ref[at, :ROWS] = both
            out_ref[at, ROWS:] = packed


def own_channels(ref):
    x, _, _ = positions()
    found = ref[:, pl.ds(pl.multiple_of(lax.div(x, 2) * LANES, LANES), LANES)]
    upper = lax.rem(x, 2) == 1
    low = lower_lanes(found.shape)
    turned = swap_halves(found)
    return jnp.where(low, jnp.where(upper, turned, found), jnp.where(upper, found, turned))


def build_tables(rates_ref, residues_ref, taps_ref, fwd_ref, out_ref, long_ref, short_ref):
    x, _, _ = positions()
    rates = own_channels(rates_ref)
    weights = own_channels(residues_ref) * jnp.sqrt(2.0 * rates)
    t = lax.broadcasted_iota(jnp.int32, (ROWS, LANES), 0).astype(f32)
    impulse = jnp.zeros((ROWS, LANES), f32)
    for m in range(MODES):
        rate, weight = rates[m : m + 1, :], weights[m : m + 1, :]
        out_ref[m] = weight * jnp.exp(-rate * (t + 1.0))
        impulse = impulse + weight * jnp.exp(-rate * t)
    own = taps_ref[pl.ds(pl.multiple_of(x * HALF, HALF), HALF), :].astype(f32)
    taps = jnp.concatenate([own, own], axis=0).T
    transform = fwd_ref[:, :ROWS]
    long_ref[...] = dot_pair(transform, impulse)
    short_ref[...] = dot_pair(transform, taps)


def positions():
    ctx, ch = lax.axis_index("ctx"), lax.axis_index("ch")
    return lax.div(ctx, NZ), lax.rem(ctx, NZ), lax.rem(ch, NC)


BLOCKS = NX * NZ // 2


def widen(blocks_ref, wide_ref):
    low_half = lower_lanes((HALF, LANES))
    for block in range(BLOCKS):
        top, bottom = slice(ROWS * block, ROWS * block + HALF), slice(ROWS * block + HALF, ROWS * (block + 1))
        wide_ref[ROWS * block : ROWS * (block + 1), :LANES] = blocks_ref[block, :ROWS]
        packed = blocks_ref[block, ROWS:].astype(f32)
        turned = swap_halves(packed)
        wide_ref[top, LANES:] = jnp.where(low_half, packed, turned).astype(bf16)
        wide_ref[bottom, LANES:] = jnp.where(low_half, turned, packed).astype(bf16)


def project_first(t0, t1, t2, t3, t4, blocks_ref, a_ref, product_ref, rest_ref, into_ref, tokens_ref, wide_ref, sems):
    x, z, core = positions()
    near = lax.rem(x + NX - 1 + 2 * core, NX)
    far = lax.rem(x + NX + 1 - 2 * core, NX)
    across = lax.rem(x + 2, NX)
    half = BLOCKS // NC

    def rows_of(k):
        return pl.ds(pl.multiple_of(k * ROWS, ROWS), ROWS)

    for side, target in ((0, tokens_ref), (1, rest_ref)):
        parity = lax.rem(z + side, 2)
        for i in range(BLOCKS):
            to = pl.ds(LANES * i, LANES)
            at = pl.ds(pl.multiple_of((2 * i + parity) * LANES, LANES), LANES)
            for k, (ref, place) in enumerate(((t0, x), (t1, near), (t2, far))):
                pltpu.make_async_copy(ref.at[:, at], target.at[rows_of(place), to], sems.at[k, side]).start()
            inner = pl.ds(pl.multiple_of((2 * (i % half) + parity) * LANES, LANES), LANES)
            mine = (i // half) == core
            first = pltpu.make_async_copy(t3.at[:, inner], target.at[rows_of(across), to], sems.at[3, side])
            second = pltpu.make_async_copy(t4.at[:, inner], target.at[rows_of(across), to], sems.at[3, side])
            pl.when(mine)(first.start)
            pl.when(jnp.logical_not(mine))(second.start)
    widen(blocks_ref, wide_ref)
    back = ROWS - 1.0 - lax.broadcasted_iota(jnp.int32, (ROWS, LANES), 0).astype(f32)
    rates = own_channels(a_ref)
    for m in range(MODES):
        into_ref[m] = jnp.exp(-rates[m : m + 1, :] * back)

    def wait(target, side):
        for k in range(4):
            rows = target.at[slice(ROWS * k, ROWS * (k + 1))]
            pltpu.make_async_copy(rows, rows, sems.at[k, side]).wait()

    wait(tokens_ref, 0)
    product_ref[...] = jnp.dot(tokens_ref[...], wide_ref[...], preferred_element_type=f32)
    wait(rest_ref, 1)


def project_rest(blocks_ref, rest_ref, product_ref, into_ref, signal_ref, streams_ref, state_ref, wide_ref, total_ref):
    widen(blocks_ref, wide_ref)
    total_ref[...] = product_ref[...] + jnp.dot(rest_ref[...], wide_ref[...], preferred_element_type=f32)
    low = lower_lanes((ROWS, LANES))
    for pair in range(NX // 2):
        lanes = slice(LANES * pair, LANES * (pair + 1))
        chunks = [slice(ROWS * k, ROWS * (k + 1)) for k in (2 * pair, 2 * pair + 1)]
        a, b = (total_ref[k, :LANES].astype(bf16).astype(f32) for k in chunks)
        turned_a, turned_b = swap_halves(a), swap_halves(b)
        gate_in, values = jnp.where(low, a, turned_b), jnp.where(low, turned_a, b)
        gate_out = jnp.where(low, total_ref[chunks[0], LANES:], total_ref[chunks[1], LANES:])
        signal = gate_in * values
        signal_ref[:, lanes] = signal
        for k, value in enumerate((signal, gate_out)):
            streams_ref[k, :, lanes] = value.astype(bf16)
        for m in range(MODES):
            state = jnp.sum(signal * into_ref[m], axis=0, keepdims=True)
            for z in range(NZ):
                state_ref[z, pair * MODES + m : pair * MODES + m + 1, :] = state


def filter_inside(signal, fwd_ref, inv_ref, long_ref):
    spectrum = dot_pair(fwd_ref[:, :ROWS], signal)
    response = jnp.concatenate([long_ref[...]] * 2, axis=1)
    return dot_pair(inv_ref[:ROWS, :], multiply_spectra(spectrum, response))


def filter_chunks(signal_ref, fwd_ref, inv_ref, long_ref, local_ref):
    local_ref[...] = filter_inside(signal_ref[...], fwd_ref, inv_ref, long_ref)


def carry_in(states_ref, a_ref, z):
    low = lower_lanes((MODES, LANES))
    rate = own_channels(a_ref) * float(ROWS)
    decay = jnp.exp(-rate)
    decay_row = jnp.exp(-rate * float(NZ))
    decay_here = jnp.exp(-rate * z.astype(f32))
    before, whole = [], []
    for pair in range(NX // 2):
        upto = jnp.zeros((MODES, LANES), f32)
        total = jnp.zeros((MODES, LANES), f32)
        for k in range(NZ):
            step = states_ref[k, pair * MODES : (pair + 1) * MODES, :]
            upto = jnp.where(k < z, upto * decay + step, upto)
            total = total * decay + step
        before.append(upto)
        whole.append(total)
    swapped = [swap_halves(v) for v in whole]
    first = jnp.where(low, 0.0, swapped[0])
    second = jnp.where(
        low,
        swapped[0] + decay_row * whole[0],
        swapped[1] + decay_row * (whole[0] + decay_row * swapped[0]),
    )
    return [before[0] + decay_here * first, before[1] + decay_here * second]


def gate_rows(streams_ref, local, carries, out_ref):
    parts = []
    for pair in range(NX // 2):
        lanes = slice(LANES * pair, LANES * (pair + 1))
        value = local[:, lanes]
        for m in range(MODES):
            value = value + out_ref[m] * carries[pair][m : m + 1, :]
        parts.append((streams_ref[1, :, lanes].astype(f32) * value).astype(bf16).astype(f32))
    return parts


def finish(streams_ref, local_ref, arrived_ref, states_ref, a_ref, out_ref, fwd_ref, inv_ref, long_ref, short_ref, packed_ref):
    _, z, _ = positions()
    low = lower_lanes((ROWS, LANES))
    before = filter_inside(arrived_ref[0], fwd_ref, inv_ref, long_ref)
    own = gate_rows(streams_ref, local_ref[...], carry_in(states_ref, a_ref, z), out_ref)
    arrived = gate_rows(arrived_ref, before, carry_in(states_ref, a_ref, lax.rem(z + NZ - 1, NZ)), out_ref)
    turned = [swap_halves(v) for v in arrived]
    shifted = [jnp.where(low, 0.0, turned[0]), jnp.where(low, turned[0], turned[1])]
    previous = jnp.concatenate([jnp.where(z == 0, s, a) for s, a in zip(shifted, arrived)], axis=1)
    window = jnp.concatenate([previous, jnp.concatenate(own, axis=1)], axis=0).astype(bf16)
    response = jnp.concatenate([short_ref[...]] * 2, axis=1)
    mixed = dot_pair(inv_ref[ROWS:, :], multiply_spectra(dot_pair(fwd_ref[...], window), response))
    low_half = lower_lanes((HALF, LANES))
    for pair in range(2):
        top = mixed[:HALF, LANES * pair : LANES * (pair + 1)]
        bottom = mixed[HALF:, LANES * pair : LANES * (pair + 1)]
        packed_ref[2 * pair] = jnp.where(low_half, top, swap_halves(bottom)).astype(bf16)
        packed_ref[2 * pair + 1] = jnp.where(low_half, swap_halves(top), bottom).astype(bf16)


def unpack_rows(packed_ref, out_ref):
    low = lower_lanes((HALF, LANES))
    for pair in range(2):
        a, b = (packed_ref[2 * pair + h].astype(f32) for h in range(2))
        lanes = slice(LANES * pair, LANES * (pair + 1))
        out_ref[:HALF, lanes] = jnp.where(low, a, swap_halves(b)).astype(bf16)
        out_ref[HALF:, lanes] = jnp.where(low, swap_halves(a), b).astype(bf16)


def per_device(tokens, projections, decay_rates, residues, short_filter):
    sds = jax.ShapeDtypeStruct
    core = lax.axis_index("ch") % NC
    rows, features = tokens.shape
    width = features // NC
    wide = lax.axis_size("ch")

    def place(a, b, k):
        return (a % NX * NZ + b) * wide + k

    outward = [
        (place(a, b, k), place(a + 1 - 2 * (k % NC), b, k)) for a in range(NX) for b in range(NZ) for k in range(wide)
    ]
    swap = [(k, k ^ 1) for k in range(wide)]
    blocks = call(spread_weights, sds((BLOCKS, ROWS + HALF, LANES), bf16), projections)
    near = lax.ppermute(tokens, ("ctx", "ch"), outward)
    blocks = lax.all_to_all(blocks, "ctx", 0, 0, tiled=True, axis_index_groups=parity_groups)
    across = [
        (place(a, b, k), place(a, (b + 1 - 2 * (k % NC)) % NZ, k)) for a in range(NX) for b in range(NZ) for k in range(wide)
    ]
    rest_blocks = lax.ppermute(blocks, ("ctx", "ch"), across)
    far = lax.ppermute(near, "ch", swap)
    half = lax.ppermute(lax.dynamic_slice_in_dim(near, core * width, width, 1), ("ctx", "ch"), outward)
    other = lax.ppermute(half, "ch", swap)

    rates = decay_rates.T
    forward, inverse = jnp.asarray(real_transform()), jnp.asarray(inverse_transform())
    table = sds((MODES, ROWS, LANES), f32)
    spectrum = sds((SPAN, LANES), f32)
    out, long_spectrum, short_spectrum = call(
        build_tables, (table, spectrum, spectrum), rates, residues.T, short_filter, forward
    )
    half_depth = BLOCKS * ROWS
    product, rest, into = call(
        project_first,
        (sds((NX * rows, 2 * LANES), f32), sds((NX * rows, half_depth), bf16), table),
        tokens,
        near,
        far,
        half,
        other,
        blocks,
        rates,
        scratch=[
            pltpu.VMEM((NX * rows, half_depth), bf16),
            pltpu.VMEM((half_depth, 2 * LANES), bf16),
            pltpu.SemaphoreType.DMA((4, 2)),
        ],
        far=5,
    )
    signal, streams, states = call(
        project_rest,
        (sds((ROWS, 2 * LANES), f32), sds((2, ROWS, 2 * LANES), bf16), sds((NZ, 2 * MODES, LANES), f32)),
        rest_blocks,
        rest,
        product,
        into,
        scratch=[
            pltpu.VMEM((half_depth, 2 * LANES), bf16),
            pltpu.VMEM((NX * rows, 2 * LANES), f32),
        ],
    )
    states = lax.all_to_all(states, "ctx", 0, 0, tiled=True, axis_index_groups=z_groups)
    onward = [(a * NZ + b, a * NZ + (b + 1) % NZ) for a in range(NX) for b in range(NZ)]
    arrived = lax.ppermute(streams, "ctx", onward)
    local = call(filter_chunks, sds((ROWS, 2 * LANES), f32), signal, forward, inverse, long_spectrum)
    packed = call(
        finish,
        sds((NX, HALF, LANES), bf16),
        streams,
        local,
        arrived,
        states,
        rates,
        out,
        forward,
        inverse,
        long_spectrum,
        short_spectrum,
    )
    packed = lax.all_to_all(packed, "ctx", 0, 0, tiled=True, axis_index_groups=x_groups)
    return call(unpack_rows, sds((ROWS, 2 * LANES), bf16), packed)


def solution(mesh):
    in_specs = (P("ctx", None), P(None, "ctx", "ch"), P("ch", None), P("ch", None), P("ch", None))
    return jax.shard_map(per_device, mesh=mesh, in_specs=in_specs, out_specs=P("ctx", "ch"), check_vma=False)
```

```python
import math

import jax
import jax.numpy as jnp
import numpy as np
from jax import lax
from jax.experimental import pallas as pl
from jax.experimental.pallas import tpu as pltpu
from jax.sharding import PartitionSpec as P

f32, bf16 = jnp.float32, jnp.bfloat16

NX, NZ, NC = 4, 8, 2
ROWS = 128
LANES = 128
HALF = 64
SPAN = 2 * ROWS
MODES = 16

parity_groups = [[x * NZ + z for x in range(NX) for z in range(p, NZ, 2)] for p in range(2)]
x_groups = [[x * NZ + z for x in range(NX)] for z in range(NZ)]
z_groups = [[x * NZ + z for z in range(NZ)] for x in range(NX)]


def real_transform():
    bins, places = np.arange(ROWS)[:, None], np.arange(SPAN)[None, :]
    angles = 2 * math.pi * (bins * places % SPAN) / SPAN
    real, imag = np.cos(angles), -np.sin(angles)
    imag[0] = np.where(np.arange(SPAN) % 2 == 0, 1.0, -1.0)
    return np.concatenate([real, imag]).astype(np.float32)


def inverse_transform():
    places, bins = np.arange(SPAN)[:, None], np.arange(ROWS)[None, :]
    angles = 2 * math.pi * (bins * places % SPAN) / SPAN
    real, imag = 2 * np.cos(angles), -2 * np.sin(angles)
    real[:, 0] = 1.0
    imag[:, 0] = np.where(np.arange(SPAN) % 2 == 0, 1.0, -1.0)
    return (np.concatenate([real, imag], axis=1) / SPAN).astype(np.float32)


def halves(v):
    high = v.astype(bf16)
    return high, (v - high.astype(f32)).astype(bf16)


def dot_pair(a, b):
    high, low = halves(a)
    if b.dtype == bf16:
        return dot(high, b) + dot(low, b)
    b_high, b_low = halves(b)
    return dot(high, b_high) + (dot(high, b_low) + dot(low, b_high))


def dot(a, b):
    return jnp.dot(a, b, preferred_element_type=f32)


def multiply_spectra(u, h):
    first = lax.broadcasted_iota(jnp.int32, (ROWS, u.shape[1]), 0) == 0
    ur, ui, hr, hi = u[:ROWS], u[ROWS:], h[:ROWS], h[ROWS:]
    both = ui * hi
    real = ur * hr - jnp.where(first, 0.0, both)
    imag = jnp.where(first, both, ur * hi + ui * hr)
    return jnp.concatenate([real, imag], axis=0)


def lower_lanes(shape):
    return lax.broadcasted_iota(jnp.int32, shape, len(shape) - 1) < HALF


def swap_halves(v):
    return pltpu.roll(v, HALF, v.ndim - 1)


VMEM, ANY = pl.BlockSpec(memory_space=pltpu.VMEM), pl.BlockSpec(memory_space=pltpu.HBM)


def call(body, outs, *args, scratch=(), flops=10**8, far=0, out_specs=None):
    return pl.pallas_call(
        body,
        out_shape=outs,
        in_specs=[ANY] * far + [VMEM] * (len(args) - far),
        out_specs=jax.tree.map(lambda _: VMEM, outs) if out_specs is None else out_specs,
        scratch_shapes=scratch,
        compiler_params=pltpu.CompilerParams(vmem_limit_bytes=16 << 20),
        cost_estimate=pl.CostEstimate(flops=flops, bytes_accessed=flops // 200, transcendentals=0),
    )(*args)


def spread_weights(w_ref, out_ref, block_ref, sems):
    low = lower_lanes((ROWS, LANES))
    low_half = lower_lanes((HALF, LANES))
    for x in range(NX):
        at = pl.ds(LANES * (x // 2), LANES)
        a, v, o = (w_ref[k, :, at].astype(f32) for k in range(3))
        if x % 2 == 0:
            both = jnp.where(low, a, swap_halves(v))
            packed = jnp.where(low_half, o[:HALF], swap_halves(o[HALF:]))
        else:
            both = jnp.where(low, swap_halves(a), v)
            packed = jnp.where(low_half, swap_halves(o[:HALF]), o[HALF:])
        both, packed = both.astype(bf16), packed.astype(bf16)
        block_ref[x, :ROWS] = both
        block_ref[x, ROWS:] = packed
        for z in range(NZ // 2):
            at = x * (NZ // 2) + z
            pltpu.make_async_copy(block_ref.at[x], out_ref.at[at], sems.at[at]).start()
    for x in range(NX):
        for z in range(NZ // 2):
            at = x * (NZ // 2) + z
            pltpu.make_async_copy(block_ref.at[x], out_ref.at[at], sems.at[at]).wait()


def own_channels(ref):
    x, _, _ = positions()
    found = ref[:, pl.ds(pl.multiple_of(lax.div(x, 2) * LANES, LANES), LANES)]
    upper = lax.rem(x, 2) == 1
    low = lower_lanes(found.shape)
    turned = swap_halves(found)
    return jnp.where(low, jnp.where(upper, turned, found), jnp.where(upper, found, turned))


def build_tables(rates_ref, residues_ref, taps_ref, fwd_ref, out_ref, long_ref, short_ref):
    x, _, _ = positions()
    rates = own_channels(rates_ref)
    weights = own_channels(residues_ref) * jnp.sqrt(2.0 * rates)
    t = lax.broadcasted_iota(jnp.int32, (ROWS, LANES), 0).astype(f32)
    impulse = jnp.zeros((ROWS, LANES), f32)
    for m in range(MODES):
        rate, weight = rates[m : m + 1, :], weights[m : m + 1, :]
        out_ref[m] = weight * jnp.exp(-rate * (t + 1.0))
        impulse = impulse + weight * jnp.exp(-rate * t)
    own = taps_ref[pl.ds(pl.multiple_of(x * HALF, HALF), HALF), :].astype(f32)
    taps = jnp.concatenate([own, own], axis=0).T
    transform = fwd_ref[:, :ROWS]
    long_ref[...] = dot_pair(transform, impulse)
    short_ref[...] = dot_pair(transform, taps)


def positions():
    ctx, ch = lax.axis_index("ctx"), lax.axis_index("ch")
    return lax.div(ctx, NZ), lax.rem(ctx, NZ), lax.rem(ch, NC)


BLOCKS = NX * NZ // 2


def widen_gates(blocks_ref, first, wide_ref, lanes):
    low_half = lower_lanes((HALF, LANES))
    for block in range(BLOCKS):
        top, bottom = slice(ROWS * block, ROWS * block + HALF), slice(ROWS * block + HALF, ROWS * (block + 1))
        packed = blocks_ref[block, first:].astype(f32)
        turned = swap_halves(packed)
        wide_ref[top, lanes] = jnp.where(low_half, packed, turned).astype(bf16)
        wide_ref[bottom, lanes] = jnp.where(low_half, turned, packed).astype(bf16)


def project_first(t0, t1, t2, t3, t4, blocks_ref, a_ref, product_ref, rest_ref, into_ref, tokens_ref, wide_ref, sems):
    x, z, core = positions()
    near = lax.rem(x + NX - 1 + 2 * core, NX)
    far = lax.rem(x + NX + 1 - 2 * core, NX)
    across = lax.rem(x + 2, NX)
    half = BLOCKS // NC

    def rows_of(k):
        return pl.ds(pl.multiple_of(k * ROWS, ROWS), ROWS)

    for side, target in ((0, tokens_ref), (1, rest_ref)):
        parity = lax.rem(z + side, 2)
        for i in range(BLOCKS):
            to = pl.ds(LANES * i, LANES)
            at = pl.ds(pl.multiple_of((2 * i + parity) * LANES, LANES), LANES)
            for k, (ref, place) in enumerate(((t0, x), (t1, near), (t2, far))):
                pltpu.make_async_copy(ref.at[:, at], target.at[rows_of(place), to], sems.at[k, side]).start()
            inner = pl.ds(pl.multiple_of((2 * (i % half) + parity) * LANES, LANES), LANES)
            mine = (i // half) == core
            first = pltpu.make_async_copy(t3.at[:, inner], target.at[rows_of(across), to], sems.at[3, side])
            second = pltpu.make_async_copy(t4.at[:, inner], target.at[rows_of(across), to], sems.at[3, side])
            pl.when(mine)(first.start)
            pl.when(jnp.logical_not(mine))(second.start)
    for block in range(BLOCKS):
        wide_ref[ROWS * block : ROWS * (block + 1), :LANES] = blocks_ref[block, :ROWS]
    widen_gates(blocks_ref, ROWS, wide_ref, slice(LANES, 2 * LANES))
    back = ROWS - 1.0 - lax.broadcasted_iota(jnp.int32, (ROWS, LANES), 0).astype(f32)
    rates = own_channels(a_ref)
    for m in range(MODES):
        into_ref[m] = jnp.exp(-rates[m : m + 1, :] * back)

    def wait(target, side):
        for k in range(4):
            rows = target.at[slice(ROWS * k, ROWS * (k + 1))]
            pltpu.make_async_copy(rows, rows, sems.at[k, side]).wait()

    wait(tokens_ref, 0)
    product_ref[...] = jnp.dot(tokens_ref[...], wide_ref[...], preferred_element_type=f32)
    wait(rest_ref, 1)


def project_signal(blocks_ref, rest_ref, product_ref, into_ref, signal_ref, state_ref, total_ref):
    weights = blocks_ref[...].reshape(BLOCKS * ROWS, LANES)
    total_ref[...] = product_ref[:, :LANES] + jnp.dot(rest_ref[...], weights, preferred_element_type=f32)
    low = lower_lanes((ROWS, LANES))
    for pair in range(NX // 2):
        chunks = [slice(ROWS * k, ROWS * (k + 1)) for k in (2 * pair, 2 * pair + 1)]
        a, b = (total_ref[k, :].astype(bf16).astype(f32) for k in chunks)
        signal = jnp.where(low, a, swap_halves(b)) * jnp.where(low, swap_halves(a), b)
        signal_ref[:, LANES * pair : LANES * (pair + 1)] = signal
        for m in range(MODES):
            state = jnp.sum(signal * into_ref[m], axis=0, keepdims=True)
            for z in range(NZ):
                state_ref[z, pair * MODES + m : pair * MODES + m + 1, :] = state


def project_gates(blocks_ref, rest_ref, product_ref, signal_ref, streams_ref, wide_ref, total_ref):
    widen_gates(blocks_ref, 0, wide_ref, slice(0, LANES))
    total_ref[...] = product_ref[:, LANES:] + jnp.dot(rest_ref[...], wide_ref[...], preferred_element_type=f32)
    streams_ref[0] = signal_ref[...].astype(bf16)
    low = lower_lanes((ROWS, LANES))
    for pair in range(NX // 2):
        chunks = [slice(ROWS * k, ROWS * (k + 1)) for k in (2 * pair, 2 * pair + 1)]
        gate = jnp.where(low, total_ref[chunks[0], :], total_ref[chunks[1], :])
        streams_ref[1, :, LANES * pair : LANES * (pair + 1)] = gate.astype(bf16)


def filter_inside(signal, fwd_ref, inv_ref, long_ref):
    spectrum = dot_pair(fwd_ref[:, :ROWS], signal)
    response = jnp.concatenate([long_ref[...]] * 2, axis=1)
    return dot_pair(inv_ref[:ROWS, :], multiply_spectra(spectrum, response))


def filter_chunks(signal_ref, fwd_ref, inv_ref, long_ref, local_ref):
    local_ref[...] = filter_inside(signal_ref[...], fwd_ref, inv_ref, long_ref)


def carry_in(states_ref, a_ref, z):
    low = lower_lanes((MODES, LANES))
    rate = own_channels(a_ref) * float(ROWS)
    decay = jnp.exp(-rate)
    decay_row = jnp.exp(-rate * float(NZ))
    decay_here = jnp.exp(-rate * z.astype(f32))
    before, whole = [], []
    for pair in range(NX // 2):
        upto = jnp.zeros((MODES, LANES), f32)
        total = jnp.zeros((MODES, LANES), f32)
        for k in range(NZ):
            step = states_ref[k, pair * MODES : (pair + 1) * MODES, :]
            upto = jnp.where(k < z, upto * decay + step, upto)
            total = total * decay + step
        before.append(upto)
        whole.append(total)
    swapped = [swap_halves(v) for v in whole]
    first = jnp.where(low, 0.0, swapped[0])
    second = jnp.where(
        low,
        swapped[0] + decay_row * whole[0],
        swapped[1] + decay_row * (whole[0] + decay_row * swapped[0]),
    )
    return [before[0] + decay_here * first, before[1] + decay_here * second]


def gate_rows(streams_ref, local, carries, out_ref):
    parts = []
    for pair in range(NX // 2):
        lanes = slice(LANES * pair, LANES * (pair + 1))
        value = local[:, lanes]
        for m in range(MODES):
            value = value + out_ref[m] * carries[pair][m : m + 1, :]
        parts.append((streams_ref[1, :, lanes].astype(f32) * value).astype(bf16).astype(f32))
    return parts


def finish(streams_ref, local_ref, arrived_ref, states_ref, a_ref, out_ref, fwd_ref, inv_ref, long_ref, short_ref, packed_ref):
    _, z, _ = positions()
    low = lower_lanes((ROWS, LANES))
    before = filter_inside(arrived_ref[0], fwd_ref, inv_ref, long_ref)
    own = gate_rows(streams_ref, local_ref[...], carry_in(states_ref, a_ref, z), out_ref)
    arrived = gate_rows(arrived_ref, before, carry_in(states_ref, a_ref, lax.rem(z + NZ - 1, NZ)), out_ref)
    turned = [swap_halves(v) for v in arrived]
    shifted = [jnp.where(low, 0.0, turned[0]), jnp.where(low, turned[0], turned[1])]
    previous = jnp.concatenate([jnp.where(z == 0, s, a) for s, a in zip(shifted, arrived)], axis=1)
    window = jnp.concatenate([previous, jnp.concatenate(own, axis=1)], axis=0).astype(bf16)
    response = jnp.concatenate([short_ref[...]] * 2, axis=1)
    mixed = dot_pair(inv_ref[ROWS:, :], multiply_spectra(dot_pair(fwd_ref[...], window), response))
    low_half = lower_lanes((HALF, LANES))
    for pair in range(2):
        top = mixed[:HALF, LANES * pair : LANES * (pair + 1)]
        bottom = mixed[HALF:, LANES * pair : LANES * (pair + 1)]
        packed_ref[2 * pair] = jnp.where(low_half, top, swap_halves(bottom)).astype(bf16)
        packed_ref[2 * pair + 1] = jnp.where(low_half, swap_halves(top), bottom).astype(bf16)


def unpack_rows(packed_ref, out_ref):
    low = lower_lanes((HALF, LANES))
    for pair in range(2):
        a, b = (packed_ref[2 * pair + h].astype(f32) for h in range(2))
        lanes = slice(LANES * pair, LANES * (pair + 1))
        out_ref[:HALF, lanes] = jnp.where(low, a, swap_halves(b)).astype(bf16)
        out_ref[HALF:, lanes] = jnp.where(low, swap_halves(a), b).astype(bf16)


def per_device(tokens, projections, decay_rates, residues, short_filter):
    sds = jax.ShapeDtypeStruct
    core = lax.axis_index("ch") % NC
    rows, features = tokens.shape
    width = features // NC
    wide = lax.axis_size("ch")

    def place(a, b, k):
        return (a % NX * NZ + b) * wide + k

    outward = [
        (place(a, b, k), place(a + 1 - 2 * (k % NC), b, k)) for a in range(NX) for b in range(NZ) for k in range(wide)
    ]
    swap = [(k, k ^ 1) for k in range(wide)]
    near = lax.ppermute(tokens, ("ctx", "ch"), outward)
    blocks = call(
        spread_weights,
        sds((BLOCKS, ROWS + HALF, LANES), bf16),
        projections,
        scratch=[pltpu.VMEM((NX, ROWS + HALF, LANES), bf16), pltpu.SemaphoreType.DMA((BLOCKS,))],
        out_specs=ANY,
    )
    blocks = lax.all_to_all(blocks, "ctx", 0, 0, tiled=True, axis_index_groups=parity_groups)
    across = [
        (place(a, b, k), place(a, (b + 1 - 2 * (k % NC)) % NZ, k)) for a in range(NX) for b in range(NZ) for k in range(wide)
    ]
    rest_pairs = lax.ppermute(blocks[:, :ROWS], ("ctx", "ch"), across)
    rest_gates = lax.ppermute(blocks[:, ROWS:], ("ctx", "ch"), across)
    far = lax.ppermute(near, "ch", swap)
    half = lax.ppermute(lax.dynamic_slice_in_dim(near, core * width, width, 1), ("ctx", "ch"), outward)
    other = lax.ppermute(half, "ch", swap)

    rates = decay_rates.T
    forward, inverse = jnp.asarray(real_transform()), jnp.asarray(inverse_transform())
    table = sds((MODES, ROWS, LANES), f32)
    spectrum = sds((SPAN, LANES), f32)
    out, long_spectrum, short_spectrum = call(
        build_tables, (table, spectrum, spectrum), rates, residues.T, short_filter, forward
    )
    half_depth = BLOCKS * ROWS
    product, rest, into = call(
        project_first,
        (sds((NX * rows, 2 * LANES), f32), sds((NX * rows, half_depth), bf16), table),
        tokens,
        near,
        far,
        half,
        other,
        blocks,
        rates,
        scratch=[
            pltpu.VMEM((NX * rows, half_depth), bf16),
            pltpu.VMEM((half_depth, 2 * LANES), bf16),
            pltpu.SemaphoreType.DMA((4, 2)),
        ],
        far=5,
    )
    total = pltpu.VMEM((NX * rows, LANES), f32)
    signal, states = call(
        project_signal,
        (sds((ROWS, 2 * LANES), f32), sds((NZ, 2 * MODES, LANES), f32)),
        rest_pairs,
        rest,
        product,
        into,
        scratch=[total],
    )
    states = lax.all_to_all(states, "ctx", 0, 0, tiled=True, axis_index_groups=z_groups)
    onward = [(a * NZ + b, a * NZ + (b + 1) % NZ) for a in range(NX) for b in range(NZ)]
    streams = call(
        project_gates,
        sds((2, ROWS, 2 * LANES), bf16),
        rest_gates,
        rest,
        product,
        signal,
        scratch=[pltpu.VMEM((half_depth, LANES), bf16), total],
    )
    arrived = lax.ppermute(streams, "ctx", onward)
    local = call(filter_chunks, sds((ROWS, 2 * LANES), f32), signal, forward, inverse, long_spectrum)
    packed = call(
        finish,
        sds((NX, HALF, LANES), bf16),
        streams,
        local,
        arrived,
        states,
        rates,
        out,
        forward,
        inverse,
        long_spectrum,
        short_spectrum,
    )
    packed = lax.all_to_all(packed, "ctx", 0, 0, tiled=True, axis_index_groups=x_groups)
    return call(unpack_rows, sds((ROWS, 2 * LANES), bf16), packed)


def solution(mesh):
    in_specs = (P("ctx", None), P(None, "ctx", "ch"), P("ch", None), P("ch", None), P("ch", None))
    return jax.shard_map(per_device, mesh=mesh, in_specs=in_specs, out_specs=P("ctx", "ch"), check_vma=False)
```

```python
import math

import jax
import jax.numpy as jnp
import numpy as np
from jax import lax
from jax.experimental import pallas as pl
from jax.experimental.pallas import tpu as pltpu
from jax.sharding import PartitionSpec as P

f32, bf16 = jnp.float32, jnp.bfloat16

NX, NZ, NC = 4, 8, 2
ROWS = 128
LANES = 128
HALF = 64
SPAN = 2 * ROWS
MODES = 16

parity_groups = [[x * NZ + z for x in range(NX) for z in range(p, NZ, 2)] for p in range(2)]
x_groups = [[x * NZ + z for x in range(NX)] for z in range(NZ)]
z_groups = [[x * NZ + z for z in range(NZ)] for x in range(NX)]


def real_transform():
    bins, places = np.arange(ROWS)[:, None], np.arange(SPAN)[None, :]
    angles = 2 * math.pi * (bins * places % SPAN) / SPAN
    real, imag = np.cos(angles), -np.sin(angles)
    imag[0] = np.where(np.arange(SPAN) % 2 == 0, 1.0, -1.0)
    return np.concatenate([real, imag]).astype(np.float32)


def inverse_transform():
    places, bins = np.arange(SPAN)[:, None], np.arange(ROWS)[None, :]
    angles = 2 * math.pi * (bins * places % SPAN) / SPAN
    real, imag = 2 * np.cos(angles), -2 * np.sin(angles)
    real[:, 0] = 1.0
    imag[:, 0] = np.where(np.arange(SPAN) % 2 == 0, 1.0, -1.0)
    return (np.concatenate([real, imag], axis=1) / SPAN).astype(np.float32)


def halves(v):
    high = v.astype(bf16)
    return high, (v - high.astype(f32)).astype(bf16)


def dot_pair(a, b):
    high, low = halves(a)
    if b.dtype == bf16:
        return dot(high, b) + dot(low, b)
    b_high, b_low = halves(b)
    return dot(high, b_high) + (dot(high, b_low) + dot(low, b_high))


def dot(a, b):
    return jnp.dot(a, b, preferred_element_type=f32)


def multiply_spectra(u, h):
    first = lax.broadcasted_iota(jnp.int32, (ROWS, u.shape[1]), 0) == 0
    ur, ui, hr, hi = u[:ROWS], u[ROWS:], h[:ROWS], h[ROWS:]
    both = ui * hi
    real = ur * hr - jnp.where(first, 0.0, both)
    imag = jnp.where(first, both, ur * hi + ui * hr)
    return jnp.concatenate([real, imag], axis=0)


def lower_lanes(shape):
    return lax.broadcasted_iota(jnp.int32, shape, len(shape) - 1) < HALF


def swap_halves(v):
    return pltpu.roll(v, HALF, v.ndim - 1)


VMEM, ANY = pl.BlockSpec(memory_space=pltpu.VMEM), pl.BlockSpec(memory_space=pltpu.HBM)


def call(body, outs, *args, scratch=(), flops=10**8, far=0, out_specs=None, limit=16):
    return pl.pallas_call(
        body,
        out_shape=outs,
        in_specs=[ANY] * far + [VMEM] * (len(args) - far),
        out_specs=jax.tree.map(lambda _: VMEM, outs) if out_specs is None else out_specs,
        scratch_shapes=scratch,
        compiler_params=pltpu.CompilerParams(vmem_limit_bytes=limit << 20),
        cost_estimate=pl.CostEstimate(flops=flops, bytes_accessed=flops // 200, transcendentals=0),
    )(*args)


def y_side():
    return lax.rem(lax.div(lax.axis_index("ch"), NC), 2)


def spread_weights(tokens_ref, w_ref, out_ref, rows_ref, block_ref, sems, row_sem):
    first = pl.multiple_of(y_side() * HALF, HALF)
    rows = pltpu.make_async_copy(tokens_ref.at[pl.ds(first, HALF)], rows_ref, row_sem)
    rows.start()
    low = lower_lanes((ROWS, LANES))
    low_half = lower_lanes((HALF, LANES))
    for x in range(NX):
        at = pl.ds(LANES * (x // 2), LANES)
        a, v, o = (w_ref[k, :, at].astype(f32) for k in range(3))
        if x % 2 == 0:
            both = jnp.where(low, a, swap_halves(v))
            packed = jnp.where(low_half, o[:HALF], swap_halves(o[HALF:]))
        else:
            both = jnp.where(low, swap_halves(a), v)
            packed = jnp.where(low_half, swap_halves(o[:HALF]), o[HALF:])
        both, packed = both.astype(bf16), packed.astype(bf16)
        block_ref[x, :ROWS] = both
        block_ref[x, ROWS:] = packed
        for z in range(NZ // 2):
            at = x * (NZ // 2) + z
            pltpu.make_async_copy(block_ref.at[x], out_ref.at[at], sems.at[at]).start()
    for x in range(NX):
        for z in range(NZ // 2):
            at = x * (NZ // 2) + z
            pltpu.make_async_copy(block_ref.at[x], out_ref.at[at], sems.at[at]).wait()
    rows.wait()


def own_channels(ref):
    x, _, _ = positions()
    found = ref[:, pl.ds(pl.multiple_of(lax.div(x, 2) * LANES, LANES), LANES)]
    upper = lax.rem(x, 2) == 1
    low = lower_lanes(found.shape)
    turned = swap_halves(found)
    return jnp.where(low, jnp.where(upper, turned, found), jnp.where(upper, found, turned))


def build_tables(rates_ref, residues_ref, taps_ref, fwd_ref, out_ref, long_ref, short_ref):
    x, _, _ = positions()
    rates = own_channels(rates_ref)
    weights = own_channels(residues_ref) * jnp.sqrt(2.0 * rates)
    t = lax.broadcasted_iota(jnp.int32, (ROWS, LANES), 0).astype(f32)
    impulse = jnp.zeros((ROWS, LANES), f32)
    for m in range(MODES):
        rate, weight = rates[m : m + 1, :], weights[m : m + 1, :]
        out_ref[m] = weight * jnp.exp(-rate * (t + 1.0))
        impulse = impulse + weight * jnp.exp(-rate * t)
    own = taps_ref[pl.ds(pl.multiple_of(x * HALF, HALF), HALF), :].astype(f32)
    taps = jnp.concatenate([own, own], axis=0).T
    transform = fwd_ref[:, :ROWS]
    long_ref[...] = dot_pair(transform, impulse)
    short_ref[...] = dot_pair(transform, taps)


def positions():
    ctx, ch = lax.axis_index("ctx"), lax.axis_index("ch")
    return lax.div(ctx, NZ), lax.rem(ctx, NZ), lax.rem(ch, NC)


BLOCKS = NX * NZ // 2


def widen(blocks_ref, wide_ref):
    low_half = lower_lanes((HALF, LANES))
    for block in range(BLOCKS):
        top, bottom = slice(ROWS * block, ROWS * block + HALF), slice(ROWS * block + HALF, ROWS * (block + 1))
        wide_ref[ROWS * block : ROWS * (block + 1), :LANES] = blocks_ref[block, :ROWS]
        packed = blocks_ref[block, ROWS:].astype(f32)
        turned = swap_halves(packed)
        wide_ref[top, LANES:] = jnp.where(low_half, packed, turned).astype(bf16)
        wide_ref[bottom, LANES:] = jnp.where(low_half, turned, packed).astype(bf16)


def project_first(t0, n0, n1, f0, f1, c0, c1, blocks_ref, a_ref, product_ref, rest_ref, into_ref, tokens_ref, wide_ref, sems):
    x, z, core = positions()
    side_y = y_side()
    near = lax.rem(x + NX - 1 + 2 * core, NX)
    far = lax.rem(x + NX + 1 - 2 * core, NX)
    across = lax.rem(x + 2, NX)
    odd = lax.rem(side_y + core, 2)
    pieces = [(1, n0, near, side_y), (1, n1, near, 1 - side_y), (2, f0, far, side_y), (2, f1, far, 1 - side_y)]
    pieces += [(3, c0, across, odd), (3, c1, across, 1 - odd)]
    for side, target in ((0, tokens_ref), (1, rest_ref)):
        parity = lax.rem(z + side, 2)
        for i in range(BLOCKS):
            to = pl.ds(LANES * i, LANES)
            at = pl.ds(pl.multiple_of((2 * i + parity) * LANES, LANES), LANES)
            own = pl.ds(pl.multiple_of(x * ROWS, ROWS), ROWS)
            pltpu.make_async_copy(t0.at[:, at], target.at[own, to], sems.at[0, side]).start()
            for k, ref, place, part in pieces:
                rows = pl.ds(pl.multiple_of(place * ROWS + part * HALF, HALF), HALF)
                pltpu.make_async_copy(ref.at[:, at], target.at[rows, to], sems.at[k, side]).start()
    widen(blocks_ref, wide_ref)
    back = ROWS - 1.0 - lax.broadcasted_iota(jnp.int32, (ROWS, LANES), 0).astype(f32)
    rates = own_channels(a_ref)
    for m in range(MODES):
        into_ref[m] = jnp.exp(-rates[m : m + 1, :] * back)

    def wait(target, side):
        for k in range(4):
            rows = target.at[slice(ROWS * k, ROWS * (k + 1))]
            pltpu.make_async_copy(rows, rows, sems.at[k, side]).wait()

    wait(tokens_ref, 0)
    product_ref[...] = jnp.dot(tokens_ref[...], wide_ref[...], preferred_element_type=f32)
    wait(rest_ref, 1)


def project_rest(blocks_ref, rest_ref, product_ref, into_ref, signal_ref, streams_ref, state_ref, wide_ref, total_ref):
    widen(blocks_ref, wide_ref)
    total_ref[...] = product_ref[...] + jnp.dot(rest_ref[...], wide_ref[...], preferred_element_type=f32)
    low = lower_lanes((ROWS, LANES))
    for pair in range(NX // 2):
        lanes = slice(LANES * pair, LANES * (pair + 1))
        chunks = [slice(ROWS * k, ROWS * (k + 1)) for k in (2 * pair, 2 * pair + 1)]
        a, b = (total_ref[k, :LANES].astype(bf16).astype(f32) for k in chunks)
        turned_a, turned_b = swap_halves(a), swap_halves(b)
        gate_in, values = jnp.where(low, a, turned_b), jnp.where(low, turned_a, b)
        gate_out = jnp.where(low, total_ref[chunks[0], LANES:], total_ref[chunks[1], LANES:])
        signal = gate_in * values
        signal_ref[:, lanes] = signal
        for k, value in enumerate((signal, gate_out)):
            streams_ref[k, :, lanes] = value.astype(bf16)
        for m in range(MODES):
            state = jnp.sum(signal * into_ref[m], axis=0, keepdims=True)
            for z in range(NZ):
                state_ref[z, pair * MODES + m : pair * MODES + m + 1, :] = state


def filter_inside(signal, fwd_ref, inv_ref, long_ref):
    spectrum = dot_pair(fwd_ref[:, :ROWS], signal)
    response = jnp.concatenate([long_ref[...]] * 2, axis=1)
    return dot_pair(inv_ref[:ROWS, :], multiply_spectra(spectrum, response))


def filter_chunks(signal_ref, fwd_ref, inv_ref, long_ref, local_ref):
    local_ref[...] = filter_inside(signal_ref[...], fwd_ref, inv_ref, long_ref)


def carry_in(states_ref, a_ref, z):
    low = lower_lanes((MODES, LANES))
    rate = own_channels(a_ref) * float(ROWS)
    decay = jnp.exp(-rate)
    decay_row = jnp.exp(-rate * float(NZ))
    decay_here = jnp.exp(-rate * z.astype(f32))
    before, whole = [], []
    for pair in range(NX // 2):
        upto = jnp.zeros((MODES, LANES), f32)
        total = jnp.zeros((MODES, LANES), f32)
        for k in range(NZ):
            step = states_ref[k, pair * MODES : (pair + 1) * MODES, :]
            upto = jnp.where(k < z, upto * decay + step, upto)
            total = total * decay + step
        before.append(upto)
        whole.append(total)
    swapped = [swap_halves(v) for v in whole]
    first = jnp.where(low, 0.0, swapped[0])
    second = jnp.where(
        low,
        swapped[0] + decay_row * whole[0],
        swapped[1] + decay_row * (whole[0] + decay_row * swapped[0]),
    )
    return [before[0] + decay_here * first, before[1] + decay_here * second]


def gate_rows(streams_ref, local, carries, out_ref):
    parts = []
    for pair in range(NX // 2):
        lanes = slice(LANES * pair, LANES * (pair + 1))
        value = local[:, lanes]
        for m in range(MODES):
            value = value + out_ref[m] * carries[pair][m : m + 1, :]
        parts.append((streams_ref[1, :, lanes].astype(f32) * value).astype(bf16).astype(f32))
    return parts


def finish(streams_ref, local_ref, arrived_ref, states_ref, a_ref, out_ref, fwd_ref, inv_ref, long_ref, short_ref, packed_ref):
    _, z, _ = positions()
    low = lower_lanes((ROWS, LANES))
    before = filter_inside(arrived_ref[0], fwd_ref, inv_ref, long_ref)
    own = gate_rows(streams_ref, local_ref[...], carry_in(states_ref, a_ref, z), out_ref)
    arrived = gate_rows(arrived_ref, before, carry_in(states_ref, a_ref, lax.rem(z + NZ - 1, NZ)), out_ref)
    turned = [swap_halves(v) for v in arrived]
    shifted = [jnp.where(low, 0.0, turned[0]), jnp.where(low, turned[0], turned[1])]
    previous = jnp.concatenate([jnp.where(z == 0, s, a) for s, a in zip(shifted, arrived)], axis=1)
    window = jnp.concatenate([previous, jnp.concatenate(own, axis=1)], axis=0).astype(bf16)
    response = jnp.concatenate([short_ref[...]] * 2, axis=1)
    mixed = dot_pair(inv_ref[ROWS:, :], multiply_spectra(dot_pair(fwd_ref[...], window), response))
    low_half = lower_lanes((HALF, LANES))
    for pair in range(2):
        top = mixed[:HALF, LANES * pair : LANES * (pair + 1)]
        bottom = mixed[HALF:, LANES * pair : LANES * (pair + 1)]
        packed_ref[2 * pair] = jnp.where(low_half, top, swap_halves(bottom)).astype(bf16)
        packed_ref[2 * pair + 1] = jnp.where(low_half, swap_halves(top), bottom).astype(bf16)


def unpack_rows(packed_ref, out_ref):
    low = lower_lanes((HALF, LANES))
    for pair in range(2):
        a, b = (packed_ref[2 * pair + h].astype(f32) for h in range(2))
        lanes = slice(LANES * pair, LANES * (pair + 1))
        out_ref[:HALF, lanes] = jnp.where(low, a, swap_halves(b)).astype(bf16)
        out_ref[HALF:, lanes] = jnp.where(low, swap_halves(a), b).astype(bf16)


def per_device(tokens, projections, decay_rates, residues, short_filter):
    sds = jax.ShapeDtypeStruct
    core = lax.axis_index("ch") % NC
    rows, features = tokens.shape
    wide = lax.axis_size("ch")

    def place(a, b, k):
        return (a % NX * NZ + b) * wide + k

    outward = [
        (place(a, b, k), place(a + 1 - 2 * (k % NC), b, k)) for a in range(NX) for b in range(NZ) for k in range(wide)
    ]
    swap = [(k, k ^ 1) for k in range(wide)]
    blocks, own_rows = call(
        spread_weights,
        (sds((BLOCKS, ROWS + HALF, LANES), bf16), sds((HALF, features), bf16)),
        tokens,
        projections,
        scratch=[
            pltpu.VMEM((NX, ROWS + HALF, LANES), bf16),
            pltpu.SemaphoreType.DMA((BLOCKS,)),
            pltpu.SemaphoreType.DMA,
        ],
        far=1,
        out_specs=(ANY, VMEM),
        limit=59,
    )
    near = lax.ppermute(own_rows, ("ctx", "ch"), outward)
    blocks = lax.all_to_all(blocks, "ctx", 0, 0, tiled=True, axis_index_groups=parity_groups)
    across = [
        (place(a, b, k), place(a, (b + 1 - 2 * (k % NC)) % NZ, k)) for a in range(NX) for b in range(NZ) for k in range(wide)
    ]
    rest_blocks = lax.ppermute(blocks, ("ctx", "ch"), across)
    near_other = lax.ppermute(near, "ch", [(k, k ^ NC) for k in range(wide)])
    far = lax.ppermute(near, "ch", swap)
    across_rows = lax.ppermute(jnp.where(core == 0, near, near_other), ("ctx", "ch"), outward)
    far_other = lax.ppermute(near_other, "ch", swap)
    across_other = lax.ppermute(across_rows, "ch", swap)

    rates = decay_rates.T
    forward, inverse = jnp.asarray(real_transform()), jnp.asarray(inverse_transform())
    table = sds((MODES, ROWS, LANES), f32)
    spectrum = sds((SPAN, LANES), f32)
    out, long_spectrum, short_spectrum = call(
        build_tables, (table, spectrum, spectrum), rates, residues.T, short_filter, forward
    )
    half_depth = BLOCKS * ROWS
    product, rest, into = call(
        project_first,
        (sds((NX * rows, 2 * LANES), f32), sds((NX * rows, half_depth), bf16), table),
        tokens,
        near,
        near_other,
        far,
        far_other,
        across_rows,
        across_other,
        blocks,
        rates,
        scratch=[
            pltpu.VMEM((NX * rows, half_depth), bf16),
            pltpu.VMEM((half_depth, 2 * LANES), bf16),
            pltpu.SemaphoreType.DMA((4, 2)),
        ],
        far=7,
    )
    signal, streams, states = call(
        project_rest,
        (sds((ROWS, 2 * LANES), f32), sds((2, ROWS, 2 * LANES), bf16), sds((NZ, 2 * MODES, LANES), f32)),
        rest_blocks,
        rest,
        product,
        into,
        scratch=[
            pltpu.VMEM((half_depth, 2 * LANES), bf16),
            pltpu.VMEM((NX * rows, 2 * LANES), f32),
        ],
    )
    states = lax.all_to_all(states, "ctx", 0, 0, tiled=True, axis_index_groups=z_groups)
    onward = [(a * NZ + b, a * NZ + (b + 1) % NZ) for a in range(NX) for b in range(NZ)]
    arrived = lax.ppermute(streams, "ctx", onward)
    local = call(filter_chunks, sds((ROWS, 2 * LANES), f32), signal, forward, inverse, long_spectrum)
    packed = call(
        finish,
        sds((NX, HALF, LANES), bf16),
        streams,
        local,
        arrived,
        states,
        rates,
        out,
        forward,
        inverse,
        long_spectrum,
        short_spectrum,
    )
    packed = lax.all_to_all(packed, "ctx", 0, 0, tiled=True, axis_index_groups=x_groups)
    return call(unpack_rows, sds((ROWS, 2 * LANES), bf16), packed)


def solution(mesh):
    in_specs = (P("ctx", None), P(None, "ctx", "ch"), P("ch", None), P("ch", None), P("ch", None))
    return jax.shard_map(per_device, mesh=mesh, in_specs=in_specs, out_specs=P("ctx", "ch"), check_vma=False)
```

```python
import math

import jax
import jax.numpy as jnp
import numpy as np
from jax import lax
from jax.experimental import pallas as pl
from jax.experimental.pallas import tpu as pltpu
from jax.sharding import PartitionSpec as P

f32, bf16 = jnp.float32, jnp.bfloat16

NX, NZ, NC = 4, 8, 2
ROWS = 128
LANES = 128
HALF = 64
SPAN = 2 * ROWS
MODES = 16

parity_groups = [[x * NZ + z for x in range(NX) for z in range(p, NZ, 2)] for p in range(2)]
x_groups = [[x * NZ + z for x in range(NX)] for z in range(NZ)]
z_groups = [[x * NZ + z for z in range(NZ)] for x in range(NX)]


def real_transform():
    bins, places = np.arange(ROWS)[:, None], np.arange(SPAN)[None, :]
    angles = 2 * math.pi * (bins * places % SPAN) / SPAN
    real, imag = np.cos(angles), -np.sin(angles)
    imag[0] = np.where(np.arange(SPAN) % 2 == 0, 1.0, -1.0)
    return np.concatenate([real, imag]).astype(np.float32)


def inverse_transform():
    places, bins = np.arange(SPAN)[:, None], np.arange(ROWS)[None, :]
    angles = 2 * math.pi * (bins * places % SPAN) / SPAN
    real, imag = 2 * np.cos(angles), -2 * np.sin(angles)
    real[:, 0] = 1.0
    imag[:, 0] = np.where(np.arange(SPAN) % 2 == 0, 1.0, -1.0)
    return (np.concatenate([real, imag], axis=1) / SPAN).astype(np.float32)


def halves(v):
    high = v.astype(bf16)
    return high, (v - high.astype(f32)).astype(bf16)


def dot_pair(a, b):
    high, low = halves(a)
    if b.dtype == bf16:
        return dot(high, b) + dot(low, b)
    b_high, b_low = halves(b)
    return dot(high, b_high) + (dot(high, b_low) + dot(low, b_high))


def dot(a, b):
    return jnp.dot(a, b, preferred_element_type=f32)


def multiply_spectra(u, h):
    first = lax.broadcasted_iota(jnp.int32, (ROWS, u.shape[1]), 0) == 0
    ur, ui, hr, hi = u[:ROWS], u[ROWS:], h[:ROWS], h[ROWS:]
    both = ui * hi
    real = ur * hr - jnp.where(first, 0.0, both)
    imag = jnp.where(first, both, ur * hi + ui * hr)
    return jnp.concatenate([real, imag], axis=0)


def lower_lanes(shape):
    return lax.broadcasted_iota(jnp.int32, shape, len(shape) - 1) < HALF


def swap_halves(v):
    return pltpu.roll(v, HALF, v.ndim - 1)


VMEM, ANY = pl.BlockSpec(memory_space=pltpu.VMEM), pl.BlockSpec(memory_space=pltpu.HBM)


def call(body, outs, *args, scratch=(), flops=10**8, far=0, out_specs=None):
    return pl.pallas_call(
        body,
        out_shape=outs,
        in_specs=[ANY] * far + [VMEM] * (len(args) - far),
        out_specs=jax.tree.map(lambda _: VMEM, outs) if out_specs is None else out_specs,
        scratch_shapes=scratch,
        compiler_params=pltpu.CompilerParams(vmem_limit_bytes=16 << 20),
        cost_estimate=pl.CostEstimate(flops=flops, bytes_accessed=flops // 200, transcendentals=0),
    )(*args)


def spread_weights(w_ref, out_ref, block_ref, sems):
    low = lower_lanes((ROWS, LANES))
    low_half = lower_lanes((HALF, LANES))
    for x in range(NX):
        at = pl.ds(LANES * (x // 2), LANES)
        a, v, o = (w_ref[k, :, at].astype(f32) for k in range(3))
        if x % 2 == 0:
            both = jnp.where(low, a, swap_halves(v))
            packed = jnp.where(low_half, o[:HALF], swap_halves(o[HALF:]))
        else:
            both = jnp.where(low, swap_halves(a), v)
            packed = jnp.where(low_half, swap_halves(o[:HALF]), o[HALF:])
        both, packed = both.astype(bf16), packed.astype(bf16)
        block_ref[x, :ROWS] = both
        block_ref[x, ROWS:] = packed
        for z in range(NZ // 2):
            at = x * (NZ // 2) + z
            pltpu.make_async_copy(block_ref.at[x], out_ref.at[at], sems.at[at]).start()
    for x in range(NX):
        for z in range(NZ // 2):
            at = x * (NZ // 2) + z
            pltpu.make_async_copy(block_ref.at[x], out_ref.at[at], sems.at[at]).wait()


def own_channels(ref):
    x, _, _ = positions()
    found = ref[:, pl.ds(pl.multiple_of(lax.div(x, 2) * LANES, LANES), LANES)]
    upper = lax.rem(x, 2) == 1
    low = lower_lanes(found.shape)
    turned = swap_halves(found)
    return jnp.where(low, jnp.where(upper, turned, found), jnp.where(upper, found, turned))


def build_tables(rates_ref, residues_ref, taps_ref, fwd_ref, out_ref, long_ref, short_ref):
    x, _, _ = positions()
    rates = own_channels(rates_ref)
    weights = own_channels(residues_ref) * jnp.sqrt(2.0 * rates)
    t = lax.broadcasted_iota(jnp.int32, (ROWS, LANES), 0).astype(f32)
    impulse = jnp.zeros((ROWS, LANES), f32)
    for m in range(MODES):
        rate, weight = rates[m : m + 1, :], weights[m : m + 1, :]
        out_ref[m] = weight * jnp.exp(-rate * (t + 1.0))
        impulse = impulse + weight * jnp.exp(-rate * t)
    own = taps_ref[pl.ds(pl.multiple_of(x * HALF, HALF), HALF), :].astype(f32)
    taps = jnp.concatenate([own, own], axis=0).T
    transform = fwd_ref[:, :ROWS]
    long_ref[...] = dot_pair(transform, impulse)
    short_ref[...] = dot_pair(transform, taps)


def positions():
    ctx, ch = lax.axis_index("ctx"), lax.axis_index("ch")
    return lax.div(ctx, NZ), lax.rem(ctx, NZ), lax.rem(ch, NC)


BLOCKS = NX * NZ // 2


def widen(blocks_ref, wide_ref):
    low_half = lower_lanes((HALF, LANES))
    for block in range(BLOCKS):
        top, bottom = slice(ROWS * block, ROWS * block + HALF), slice(ROWS * block + HALF, ROWS * (block + 1))
        wide_ref[ROWS * block : ROWS * (block + 1), :LANES] = blocks_ref[block, :ROWS]
        packed = blocks_ref[block, ROWS:].astype(f32)
        turned = swap_halves(packed)
        wide_ref[top, LANES:] = jnp.where(low_half, packed, turned).astype(bf16)
        wide_ref[bottom, LANES:] = jnp.where(low_half, turned, packed).astype(bf16)


def project_first(t0, t1, t2, t3, t4, blocks_ref, a_ref, product_ref, rest_ref, into_ref, tokens_ref, wide_ref, sems):
    x, z, core = positions()
    near = lax.rem(x + NX - 1 + 2 * core, NX)
    far = lax.rem(x + NX + 1 - 2 * core, NX)
    across = lax.rem(x + 2, NX)
    half = BLOCKS // NC

    def rows_of(k):
        return pl.ds(pl.multiple_of(k * ROWS, ROWS), ROWS)

    for side, target in ((0, tokens_ref), (1, rest_ref)):
        parity = lax.rem(z + side, 2)
        for i in range(BLOCKS):
            to = pl.ds(LANES * i, LANES)
            at = pl.ds(pl.multiple_of((2 * i + parity) * LANES, LANES), LANES)
            for k, (ref, place) in enumerate(((t0, x), (t1, near), (t2, far))):
                pltpu.make_async_copy(ref.at[:, at], target.at[rows_of(place), to], sems.at[k, side]).start()
            inner = pl.ds(pl.multiple_of((2 * (i % half) + parity) * LANES, LANES), LANES)
            mine = (i // half) == core
            first = pltpu.make_async_copy(t3.at[:, inner], target.at[rows_of(across), to], sems.at[3, side])
            second = pltpu.make_async_copy(t4.at[:, inner], target.at[rows_of(across), to], sems.at[3, side])
            pl.when(mine)(first.start)
            pl.when(jnp.logical_not(mine))(second.start)
    widen(blocks_ref, wide_ref)
    back = ROWS - 1.0 - lax.broadcasted_iota(jnp.int32, (ROWS, LANES), 0).astype(f32)
    rates = own_channels(a_ref)
    for m in range(MODES):
        into_ref[m] = jnp.exp(-rates[m : m + 1, :] * back)

    def wait(target, side):
        for k in range(4):
            rows = target.at[slice(ROWS * k, ROWS * (k + 1))]
            pltpu.make_async_copy(rows, rows, sems.at[k, side]).wait()

    wait(tokens_ref, 0)
    product_ref[...] = jnp.dot(tokens_ref[...], wide_ref[...], preferred_element_type=f32)
    wait(rest_ref, 1)


def project_rest(blocks_ref, rest_ref, product_ref, into_ref, signal_ref, streams_ref, state_ref, wide_ref, total_ref):
    widen(blocks_ref, wide_ref)
    total_ref[...] = product_ref[...] + jnp.dot(rest_ref[...], wide_ref[...], preferred_element_type=f32)
    low = lower_lanes((ROWS, LANES))
    for pair in range(NX // 2):
        lanes = slice(LANES * pair, LANES * (pair + 1))
        chunks = [slice(ROWS * k, ROWS * (k + 1)) for k in (2 * pair, 2 * pair + 1)]
        a, b = (total_ref[k, :LANES].astype(bf16).astype(f32) for k in chunks)
        turned_a, turned_b = swap_halves(a), swap_halves(b)
        gate_in, values = jnp.where(low, a, turned_b), jnp.where(low, turned_a, b)
        gate_out = jnp.where(low, total_ref[chunks[0], LANES:], total_ref[chunks[1], LANES:])
        signal = gate_in * values
        signal_ref[:, lanes] = signal
        for k, value in enumerate((*halves(signal), gate_out)):
            streams_ref[k, :, lanes] = value.astype(bf16)
        for m in range(MODES):
            state = jnp.sum(signal * into_ref[m], axis=0, keepdims=True)
            for z in range(NZ):
                state_ref[z, pair * MODES + m : pair * MODES + m + 1, :] = state


def filter_inside(signal, fwd_ref, inv_ref, long_ref):
    spectrum = dot_pair(fwd_ref[:, :ROWS], signal)
    response = jnp.concatenate([long_ref[...]] * 2, axis=1)
    return dot_pair(inv_ref[:ROWS, :], multiply_spectra(spectrum, response))


def filter_chunks(signal_ref, fwd_ref, inv_ref, long_ref, local_ref):
    local_ref[...] = filter_inside(signal_ref[...], fwd_ref, inv_ref, long_ref)


def carry_in(states_ref, a_ref, z):
    low = lower_lanes((MODES, LANES))
    rate = own_channels(a_ref) * float(ROWS)
    decay = jnp.exp(-rate)
    decay_row = jnp.exp(-rate * float(NZ))
    decay_here = jnp.exp(-rate * z.astype(f32))
    before, whole = [], []
    for pair in range(NX // 2):
        upto = jnp.zeros((MODES, LANES), f32)
        total = jnp.zeros((MODES, LANES), f32)
        for k in range(NZ):
            step = states_ref[k, pair * MODES : (pair + 1) * MODES, :]
            upto = jnp.where(k < z, upto * decay + step, upto)
            total = total * decay + step
        before.append(upto)
        whole.append(total)
    swapped = [swap_halves(v) for v in whole]
    first = jnp.where(low, 0.0, swapped[0])
    second = jnp.where(
        low,
        swapped[0] + decay_row * whole[0],
        swapped[1] + decay_row * (whole[0] + decay_row * swapped[0]),
    )
    return [before[0] + decay_here * first, before[1] + decay_here * second]


def gate_rows(streams_ref, local, carries, out_ref):
    parts = []
    for pair in range(NX // 2):
        lanes = slice(LANES * pair, LANES * (pair + 1))
        value = local[:, lanes]
        for m in range(MODES):
            value = value + out_ref[m] * carries[pair][m : m + 1, :]
        parts.append((streams_ref[2, :, lanes].astype(f32) * value).astype(bf16).astype(f32))
    return parts


def finish(streams_ref, local_ref, arrived_ref, states_ref, a_ref, out_ref, fwd_ref, inv_ref, long_ref, short_ref, packed_ref):
    _, z, _ = positions()
    low = lower_lanes((ROWS, LANES))
    before = filter_inside(arrived_ref[0].astype(f32) + arrived_ref[1].astype(f32), fwd_ref, inv_ref, long_ref)
    own = gate_rows(streams_ref, local_ref[...], carry_in(states_ref, a_ref, z), out_ref)
    arrived = gate_rows(arrived_ref, before, carry_in(states_ref, a_ref, lax.rem(z + NZ - 1, NZ)), out_ref)
    turned = [swap_halves(v) for v in arrived]
    shifted = [jnp.where(low, 0.0, turned[0]), jnp.where(low, turned[0], turned[1])]
    previous = jnp.concatenate([jnp.where(z == 0, s, a) for s, a in zip(shifted, arrived)], axis=1)
    window = jnp.concatenate([previous, jnp.concatenate(own, axis=1)], axis=0).astype(bf16)
    response = jnp.concatenate([short_ref[...]] * 2, axis=1)
    mixed = dot_pair(inv_ref[ROWS:, :], multiply_spectra(dot_pair(fwd_ref[...], window), response))
    low_half = lower_lanes((HALF, LANES))
    for pair in range(2):
        top = mixed[:HALF, LANES * pair : LANES * (pair + 1)]
        bottom = mixed[HALF:, LANES * pair : LANES * (pair + 1)]
        packed_ref[2 * pair] = jnp.where(low_half, top, swap_halves(bottom)).astype(bf16)
        packed_ref[2 * pair + 1] = jnp.where(low_half, swap_halves(top), bottom).astype(bf16)


def unpack_rows(packed_ref, out_ref):
    low = lower_lanes((HALF, LANES))
    for pair in range(2):
        a, b = (packed_ref[2 * pair + h].astype(f32) for h in range(2))
        lanes = slice(LANES * pair, LANES * (pair + 1))
        out_ref[:HALF, lanes] = jnp.where(low, a, swap_halves(b)).astype(bf16)
        out_ref[HALF:, lanes] = jnp.where(low, swap_halves(a), b).astype(bf16)


def per_device(tokens, projections, decay_rates, residues, short_filter):
    sds = jax.ShapeDtypeStruct
    core = lax.axis_index("ch") % NC
    rows, features = tokens.shape
    width = features // NC
    wide = lax.axis_size("ch")

    def place(a, b, k):
        return (a % NX * NZ + b) * wide + k

    outward = [
        (place(a, b, k), place(a + 1 - 2 * (k % NC), b, k)) for a in range(NX) for b in range(NZ) for k in range(wide)
    ]
    swap = [(k, k ^ 1) for k in range(wide)]
    near = lax.ppermute(tokens, ("ctx", "ch"), outward)
    blocks = call(
        spread_weights,
        sds((BLOCKS, ROWS + HALF, LANES), bf16),
        projections,
        scratch=[pltpu.VMEM((NX, ROWS + HALF, LANES), bf16), pltpu.SemaphoreType.DMA((BLOCKS,))],
        out_specs=ANY,
    )
    blocks = lax.all_to_all(blocks, "ctx", 0, 0, tiled=True, axis_index_groups=parity_groups)
    across = [
        (place(a, b, k), place(a, (b + 1 - 2 * (k % NC)) % NZ, k)) for a in range(NX) for b in range(NZ) for k in range(wide)
    ]
    rest_blocks = lax.ppermute(blocks, ("ctx", "ch"), across)
    far = lax.ppermute(near, "ch", swap)
    half = lax.ppermute(lax.dynamic_slice_in_dim(near, core * width, width, 1), ("ctx", "ch"), outward)
    other = lax.ppermute(half, "ch", swap)

    rates = decay_rates.T
    forward, inverse = jnp.asarray(real_transform()), jnp.asarray(inverse_transform())
    table = sds((MODES, ROWS, LANES), f32)
    spectrum = sds((SPAN, LANES), f32)
    out, long_spectrum, short_spectrum = call(
        build_tables, (table, spectrum, spectrum), rates, residues.T, short_filter, forward
    )
    half_depth = BLOCKS * ROWS
    product, rest, into = call(
        project_first,
        (sds((NX * rows, 2 * LANES), f32), sds((NX * rows, half_depth), bf16), table),
        tokens,
        near,
        far,
        half,
        other,
        blocks,
        rates,
        scratch=[
            pltpu.VMEM((NX * rows, half_depth), bf16),
            pltpu.VMEM((half_depth, 2 * LANES), bf16),
            pltpu.SemaphoreType.DMA((4, 2)),
        ],
        far=5,
    )
    signal, streams, states = call(
        project_rest,
        (sds((ROWS, 2 * LANES), f32), sds((3, ROWS, 2 * LANES), bf16), sds((NZ, 2 * MODES, LANES), f32)),
        rest_blocks,
        rest,
        product,
        into,
        scratch=[
            pltpu.VMEM((half_depth, 2 * LANES), bf16),
            pltpu.VMEM((NX * rows, 2 * LANES), f32),
        ],
    )
    states = lax.all_to_all(states, "ctx", 0, 0, tiled=True, axis_index_groups=z_groups)
    onward = [(a * NZ + b, a * NZ + (b + 1) % NZ) for a in range(NX) for b in range(NZ)]
    arrived = lax.ppermute(streams, "ctx", onward)
    local = call(filter_chunks, sds((ROWS, 2 * LANES), f32), signal, forward, inverse, long_spectrum)
    packed = call(
        finish,
        sds((NX, HALF, LANES), bf16),
        streams,
        local,
        arrived,
        states,
        rates,
        out,
        forward,
        inverse,
        long_spectrum,
        short_spectrum,
    )
    packed = lax.all_to_all(packed, "ctx", 0, 0, tiled=True, axis_index_groups=x_groups)
    return call(unpack_rows, sds((ROWS, 2 * LANES), bf16), packed)


def solution(mesh):
    in_specs = (P("ctx", None), P(None, "ctx", "ch"), P("ch", None), P("ch", None), P("ch", None))
    return jax.shard_map(per_device, mesh=mesh, in_specs=in_specs, out_specs=P("ctx", "ch"), check_vma=False)
```

```python
import math

import jax
import jax.numpy as jnp
import numpy as np
from jax import lax
from jax.experimental import pallas as pl
from jax.experimental.pallas import tpu as pltpu
from jax.sharding import PartitionSpec as P

f32, bf16 = jnp.float32, jnp.bfloat16

NX, NZ, NC = 4, 8, 2
ROWS = 128
LANES = 128
HALF = 64
SPAN = 2 * ROWS
MODES = 16

parity_groups = [[x * NZ + z for x in range(NX) for z in range(p, NZ, 2)] for p in range(2)]
x_groups = [[x * NZ + z for x in range(NX)] for z in range(NZ)]
z_groups = [[x * NZ + z for z in range(NZ)] for x in range(NX)]


def real_transform():
    bins, places = np.arange(ROWS)[:, None], np.arange(SPAN)[None, :]
    angles = 2 * math.pi * (bins * places % SPAN) / SPAN
    real, imag = np.cos(angles), -np.sin(angles)
    imag[0] = np.where(np.arange(SPAN) % 2 == 0, 1.0, -1.0)
    return np.concatenate([real, imag]).astype(np.float32)


def inverse_transform():
    places, bins = np.arange(SPAN)[:, None], np.arange(ROWS)[None, :]
    angles = 2 * math.pi * (bins * places % SPAN) / SPAN
    real, imag = 2 * np.cos(angles), -2 * np.sin(angles)
    real[:, 0] = 1.0
    imag[:, 0] = np.where(np.arange(SPAN) % 2 == 0, 1.0, -1.0)
    return (np.concatenate([real, imag], axis=1) / SPAN).astype(np.float32)


def halves(v):
    high = v.astype(bf16)
    return high, (v - high.astype(f32)).astype(bf16)


def dot_pair(a, b):
    high, low = halves(a)
    if b.dtype == bf16:
        return dot(high, b) + dot(low, b)
    b_high, b_low = halves(b)
    return dot(high, b_high) + (dot(high, b_low) + dot(low, b_high))


def dot(a, b):
    return jnp.dot(a, b, preferred_element_type=f32)


def multiply_spectra(u, h):
    first = lax.broadcasted_iota(jnp.int32, (ROWS, u.shape[1]), 0) == 0
    ur, ui, hr, hi = u[:ROWS], u[ROWS:], h[:ROWS], h[ROWS:]
    both = ui * hi
    real = ur * hr - jnp.where(first, 0.0, both)
    imag = jnp.where(first, both, ur * hi + ui * hr)
    return jnp.concatenate([real, imag], axis=0)


def lower_lanes(shape):
    return lax.broadcasted_iota(jnp.int32, shape, len(shape) - 1) < HALF


def swap_halves(v):
    return pltpu.roll(v, HALF, v.ndim - 1)


VMEM, ANY = pl.BlockSpec(memory_space=pltpu.VMEM), pl.BlockSpec(memory_space=pltpu.HBM)


def call(body, outs, *args, scratch=(), flops=10**8, far=0, out_specs=None):
    return pl.pallas_call(
        body,
        out_shape=outs,
        in_specs=[ANY] * far + [VMEM] * (len(args) - far),
        out_specs=jax.tree.map(lambda _: VMEM, outs) if out_specs is None else out_specs,
        scratch_shapes=scratch,
        compiler_params=pltpu.CompilerParams(vmem_limit_bytes=16 << 20),
        cost_estimate=pl.CostEstimate(flops=flops, bytes_accessed=flops // 200, transcendentals=0),
    )(*args)


def spread_weights(w_ref, out_ref):
    low = lower_lanes((ROWS, LANES))
    low_half = lower_lanes((HALF, LANES))
    for x in range(NX):
        at = pl.ds(LANES * (x // 2), LANES)
        a, v, o = (w_ref[k, :, at].astype(f32) for k in range(3))
        if x % 2 == 0:
            both = jnp.where(low, a, swap_halves(v))
            packed = jnp.where(low_half, o[:HALF], swap_halves(o[HALF:]))
        else:
            both = jnp.where(low, swap_halves(a), v)
            packed = jnp.where(low_half, swap_halves(o[:HALF]), o[HALF:])
        both, packed = both.astype(bf16), packed.astype(bf16)
        for z in range(NZ // 2):
            at = x * (NZ // 2) + z
            out_ref[at, :ROWS] = both
            out_ref[at, ROWS:] = packed


def own_channels(ref):
    x, _, _ = positions()
    found = ref[:, pl.ds(pl.multiple_of(lax.div(x, 2) * LANES, LANES), LANES)]
    upper = lax.rem(x, 2) == 1
    low = lower_lanes(found.shape)
    turned = swap_halves(found)
    return jnp.where(low, jnp.where(upper, turned, found), jnp.where(upper, found, turned))


def build_tables(rates_ref, residues_ref, taps_ref, fwd_ref, out_ref, long_ref, short_ref):
    x, _, _ = positions()
    rates = own_channels(rates_ref)
    weights = own_channels(residues_ref) * jnp.sqrt(2.0 * rates)
    t = lax.broadcasted_iota(jnp.int32, (ROWS, LANES), 0).astype(f32)
    impulse = jnp.zeros((ROWS, LANES), f32)
    for m in range(MODES):
        rate, weight = rates[m : m + 1, :], weights[m : m + 1, :]
        out_ref[m] = weight * jnp.exp(-rate * (t + 1.0))
        impulse = impulse + weight * jnp.exp(-rate * t)
    own = taps_ref[pl.ds(pl.multiple_of(x * HALF, HALF), HALF), :].astype(f32)
    taps = jnp.concatenate([own, own], axis=0).T
    transform = fwd_ref[:, :ROWS]
    long_ref[...] = dot_pair(transform, impulse)
    short_ref[...] = dot_pair(transform, taps)


def positions():
    ctx, ch = lax.axis_index("ctx"), lax.axis_index("ch")
    return lax.div(ctx, NZ), lax.rem(ctx, NZ), lax.rem(ch, NC)


BLOCKS = NX * NZ // 2


def widen(blocks_ref, wide_ref):
    low_half = lower_lanes((HALF, LANES))
    for block in range(BLOCKS):
        top, bottom = slice(ROWS * block, ROWS * block + HALF), slice(ROWS * block + HALF, ROWS * (block + 1))
        wide_ref[ROWS * block : ROWS * (block + 1), :LANES] = blocks_ref[block, :ROWS]
        packed = blocks_ref[block, ROWS:].astype(f32)
        turned = swap_halves(packed)
        wide_ref[top, LANES:] = jnp.where(low_half, packed, turned).astype(bf16)
        wide_ref[bottom, LANES:] = jnp.where(low_half, turned, packed).astype(bf16)


def project_first(t0, t1, t2, t3, t4, blocks_ref, a_ref, product_ref, rest_ref, into_ref, tokens_ref, wide_ref, sems):
    x, z, core = positions()
    near = lax.rem(x + NX - 1 + 2 * core, NX)
    far = lax.rem(x + NX + 1 - 2 * core, NX)
    across = lax.rem(x + 2, NX)
    half = BLOCKS // NC

    def rows_of(k):
        return pl.ds(pl.multiple_of(k * ROWS, ROWS), ROWS)

    for side, target in ((0, tokens_ref), (1, rest_ref)):
        parity = lax.rem(z + side, 2)
        for i in range(BLOCKS):
            to = pl.ds(LANES * i, LANES)
            at = pl.ds(pl.multiple_of((2 * i + parity) * LANES, LANES), LANES)
            for k, (ref, place) in enumerate(((t0, x), (t1, near), (t2, far))):
                pltpu.make_async_copy(ref.at[:, at], target.at[rows_of(place), to], sems.at[k, side]).start()
            inner = pl.ds(pl.multiple_of((2 * (i % half) + parity) * LANES, LANES), LANES)
            mine = (i // half) == core
            first = pltpu.make_async_copy(t3.at[:, inner], target.at[rows_of(across), to], sems.at[3, side])
            second = pltpu.make_async_copy(t4.at[:, inner], target.at[rows_of(across), to], sems.at[3, side])
            pl.when(mine)(first.start)
            pl.when(jnp.logical_not(mine))(second.start)
    widen(blocks_ref, wide_ref)
    back = ROWS - 1.0 - lax.broadcasted_iota(jnp.int32, (ROWS, LANES), 0).astype(f32)
    rates = own_channels(a_ref)
    for m in range(MODES):
        into_ref[m] = jnp.exp(-rates[m : m + 1, :] * back)

    def wait(target, side):
        for k in range(4):
            rows = target.at[slice(ROWS * k, ROWS * (k + 1))]
            pltpu.make_async_copy(rows, rows, sems.at[k, side]).wait()

    wait(tokens_ref, 0)
    product_ref[...] = jnp.dot(tokens_ref[...], wide_ref[...], preferred_element_type=f32)
    wait(rest_ref, 1)


def project_rest(blocks_ref, rest_ref, product_ref, into_ref, signal_ref, streams_ref, state_ref, wide_ref, total_ref):
    widen(blocks_ref, wide_ref)
    total_ref[...] = product_ref[...] + jnp.dot(rest_ref[...], wide_ref[...], preferred_element_type=f32)
    low = lower_lanes((ROWS, LANES))
    for pair in range(NX // 2):
        lanes = slice(LANES * pair, LANES * (pair + 1))
        chunks = [slice(ROWS * k, ROWS * (k + 1)) for k in (2 * pair, 2 * pair + 1)]
        a, b = (total_ref[k, :LANES].astype(bf16).astype(f32) for k in chunks)
        turned_a, turned_b = swap_halves(a), swap_halves(b)
        gate_in, values = jnp.where(low, a, turned_b), jnp.where(low, turned_a, b)
        gate_out = jnp.where(low, total_ref[chunks[0], LANES:], total_ref[chunks[1], LANES:])
        signal = gate_in * values
        signal_ref[:, lanes] = signal
        for k, value in enumerate((signal, gate_out)):
            streams_ref[k, :, lanes] = value.astype(bf16)
        for m in range(MODES):
            state = jnp.sum(signal * into_ref[m], axis=0, keepdims=True)
            for z in range(NZ):
                state_ref[z, pair * MODES + m : pair * MODES + m + 1, :] = state


def filter_inside(signal, fwd_ref, inv_ref, long_ref):
    spectrum = dot_pair(fwd_ref[:, :ROWS], signal)
    response = jnp.concatenate([long_ref[...]] * 2, axis=1)
    return dot_pair(inv_ref[:ROWS, :], multiply_spectra(spectrum, response))


def filter_chunks(signal_ref, fwd_ref, inv_ref, long_ref, local_ref):
    local_ref[...] = filter_inside(signal_ref[...], fwd_ref, inv_ref, long_ref)


def carry_in(states_ref, a_ref, z):
    low = lower_lanes((MODES, LANES))
    rate = own_channels(a_ref) * float(ROWS)
    decay = jnp.exp(-rate)
    decay_row = jnp.exp(-rate * float(NZ))
    decay_here = jnp.exp(-rate * z.astype(f32))
    before, whole = [], []
    for pair in range(NX // 2):
        upto = jnp.zeros((MODES, LANES), f32)
        total = jnp.zeros((MODES, LANES), f32)
        for k in range(NZ):
            step = states_ref[k, pair * MODES : (pair + 1) * MODES, :]
            upto = jnp.where(k < z, upto * decay + step, upto)
            total = total * decay + step
        before.append(upto)
        whole.append(total)
    swapped = [swap_halves(v) for v in whole]
    first = jnp.where(low, 0.0, swapped[0])
    second = jnp.where(
        low,
        swapped[0] + decay_row * whole[0],
        swapped[1] + decay_row * (whole[0] + decay_row * swapped[0]),
    )
    return [before[0] + decay_here * first, before[1] + decay_here * second]


def gate_rows(chunks, out_ref):
    gated = [[] for _ in chunks]
    for pair in range(NX // 2):
        lanes = slice(LANES * pair, LANES * (pair + 1))
        values = [local[:, lanes] for _, local, _ in chunks]
        for m in range(MODES):
            table = out_ref[m]
            values = [v + table * c[2][pair][m : m + 1, :] for v, c in zip(values, chunks)]
        for rows, value, (streams_ref, _, _) in zip(gated, values, chunks):
            rows.append((streams_ref[1, :, lanes].astype(f32) * value).astype(bf16).astype(f32))
    return gated


def finish(streams_ref, local_ref, arrived_ref, states_ref, a_ref, out_ref, fwd_ref, inv_ref, long_ref, short_ref, packed_ref):
    _, z, _ = positions()
    low = lower_lanes((ROWS, LANES))
    before = filter_inside(arrived_ref[0], fwd_ref, inv_ref, long_ref)
    carries = [carry_in(states_ref, a_ref, place) for place in (z, lax.rem(z + NZ - 1, NZ))]
    own, arrived = gate_rows(
        ((streams_ref, local_ref[...], carries[0]), (arrived_ref, before, carries[1])), out_ref
    )
    turned = [swap_halves(v) for v in arrived]
    shifted = [jnp.where(low, 0.0, turned[0]), jnp.where(low, turned[0], turned[1])]
    previous = jnp.concatenate([jnp.where(z == 0, s, a) for s, a in zip(shifted, arrived)], axis=1)
    window = jnp.concatenate([previous, jnp.concatenate(own, axis=1)], axis=0).astype(bf16)
    response = jnp.concatenate([short_ref[...]] * 2, axis=1)
    mixed = dot_pair(inv_ref[ROWS:, :], multiply_spectra(dot_pair(fwd_ref[...], window), response))
    low_half = lower_lanes((HALF, LANES))
    for pair in range(2):
        top = mixed[:HALF, LANES * pair : LANES * (pair + 1)]
        bottom = mixed[HALF:, LANES * pair : LANES * (pair + 1)]
        packed_ref[2 * pair] = jnp.where(low_half, top, swap_halves(bottom)).astype(bf16)
        packed_ref[2 * pair + 1] = jnp.where(low_half, swap_halves(top), bottom).astype(bf16)


def unpack_rows(packed_ref, out_ref):
    low = lower_lanes((HALF, LANES))
    for pair in range(2):
        a, b = (packed_ref[2 * pair + h].astype(f32) for h in range(2))
        lanes = slice(LANES * pair, LANES * (pair + 1))
        out_ref[:HALF, lanes] = jnp.where(low, a, swap_halves(b)).astype(bf16)
        out_ref[HALF:, lanes] = jnp.where(low, swap_halves(a), b).astype(bf16)


def per_device(tokens, projections, decay_rates, residues, short_filter):
    sds = jax.ShapeDtypeStruct
    core = lax.axis_index("ch") % NC
    rows, features = tokens.shape
    width = features // NC
    wide = lax.axis_size("ch")

    def place(a, b, k):
        return (a % NX * NZ + b) * wide + k

    outward = [
        (place(a, b, k), place(a + 1 - 2 * (k % NC), b, k)) for a in range(NX) for b in range(NZ) for k in range(wide)
    ]
    swap = [(k, k ^ 1) for k in range(wide)]
    near = lax.ppermute(tokens, ("ctx", "ch"), outward)
    blocks = call(spread_weights, sds((BLOCKS, ROWS + HALF, LANES), bf16), projections)
    blocks = lax.all_to_all(blocks, "ctx", 0, 0, tiled=True, axis_index_groups=parity_groups)
    across = [
        (place(a, b, k), place(a, (b + 1 - 2 * (k % NC)) % NZ, k)) for a in range(NX) for b in range(NZ) for k in range(wide)
    ]
    rest_blocks = lax.ppermute(blocks, ("ctx", "ch"), across)
    far = lax.ppermute(near, "ch", swap)
    half = lax.ppermute(lax.dynamic_slice_in_dim(near, core * width, width, 1), ("ctx", "ch"), outward)
    other = lax.ppermute(half, "ch", swap)

    rates = decay_rates.T
    forward, inverse = jnp.asarray(real_transform()), jnp.asarray(inverse_transform())
    table = sds((MODES, ROWS, LANES), f32)
    spectrum = sds((SPAN, LANES), f32)
    out, long_spectrum, short_spectrum = call(
        build_tables, (table, spectrum, spectrum), rates, residues.T, short_filter, forward
    )
    half_depth = BLOCKS * ROWS
    product, rest, into = call(
        project_first,
        (sds((NX * rows, 2 * LANES), f32), sds((NX * rows, half_depth), bf16), table),
        tokens,
        near,
        far,
        half,
        other,
        blocks,
        rates,
        scratch=[
            pltpu.VMEM((NX * rows, half_depth), bf16),
            pltpu.VMEM((half_depth, 2 * LANES), bf16),
            pltpu.SemaphoreType.DMA((4, 2)),
        ],
        far=5,
    )
    signal, streams, states = call(
        project_rest,
        (sds((ROWS, 2 * LANES), f32), sds((2, ROWS, 2 * LANES), bf16), sds((NZ, 2 * MODES, LANES), f32)),
        rest_blocks,
        rest,
        product,
        into,
        scratch=[
            pltpu.VMEM((half_depth, 2 * LANES), bf16),
            pltpu.VMEM((NX * rows, 2 * LANES), f32),
        ],
    )
    states = lax.all_to_all(states, "ctx", 0, 0, tiled=True, axis_index_groups=z_groups)
    onward = [(a * NZ + b, a * NZ + (b + 1) % NZ) for a in range(NX) for b in range(NZ)]
    arrived = lax.ppermute(streams, "ctx", onward)
    local = call(filter_chunks, sds((ROWS, 2 * LANES), f32), signal, forward, inverse, long_spectrum)
    packed = call(
        finish,
        sds((NX, HALF, LANES), bf16),
        streams,
        local,
        arrived,
        states,
        rates,
        out,
        forward,
        inverse,
        long_spectrum,
        short_spectrum,
    )
    packed = lax.all_to_all(packed, "ctx", 0, 0, tiled=True, axis_index_groups=x_groups)
    return call(unpack_rows, sds((ROWS, 2 * LANES), bf16), packed)


def solution(mesh):
    in_specs = (P("ctx", None), P(None, "ctx", "ch"), P("ch", None), P("ch", None), P("ch", None))
    return jax.shard_map(per_device, mesh=mesh, in_specs=in_specs, out_specs=P("ctx", "ch"), check_vma=False)
```
